32 devices in a mesh: front: 2 (over y), wide: 16 (over z, x, core).
Axes of the slice: x: 2, y: 2, z: 4, core: 2. Of those that a mesh axis runs over, the one named last changes fastest.
Arguments:
- updates: bfloat16 [2, 8192, 1024], P('front', 'wide'), may hold values from -6 to 6
- parent_panels: bfloat16 [2, 16384, 2048], P('front', 'wide'), may hold values from -6 to 6
- slot_parent: int32 [2, 64, 1], P('front', 'wide'), may hold values from 0 to 1; in each aligned block of 4 rows (0 to 3, 4 to 7, ..., all dimensions but the last counted through in order) at most 2 rows name the same one
- slot_row: int32 [2, 64], P('front', 'wide'), may hold values from 0 to 7
- slot_cols: int32 [2, 64, 8], P('front', 'wide'), may hold values from 0 to 15, as said below
- slot_mask: int32 [2, 64, 8], P('front', 'wide'), may hold values 0 or 1
Outputs:
- parent_grid: bfloat16 [2, 131072, 256], P('front', 'wide')
The draws below stay inside these ranges and needn't reach their ends.
Inputs may be any that keep to these rules, and one draw needn't show every extreme that they name: `slot_parent`: among the 4 update block rows of one device no parent front is named more than 2 times; in every draw some device names some front exactly 2 times. `slot_cols`: the 8 block columns of one update block row are distinct.
All inputs are finite; a program needn't handle non-finite values. No bound on the sum of `slot_mask` on one device may be relied on, other than what follows from the above.
Results may differ from the reference program's by a relative error of at most 0.001.
Values may be sent and summed in bfloat16 or wider, within the bound.
No kernel may reach another device: no remote copies, remote signals or barrier semaphores. Data moves between devices by JAX's collectives and lax.ppermute only.
A program may use at most 64 MiB of HBM per device.

```python
import math
import jax
import jax.numpy as jnp
import numpy as np
from jax import lax

BLOCK = 128
FRONT_ORDER = 16384
WB = 16
CW = 8
GRID_COLS = 8
SLOTS = 4
FRONTS = 2
PANELS = 16
NB = 128
RB = 8
GRID_ROWS = 2
GRID_BLOCK_ROWS = 64
SLOTS_ALL = 64
CAPF = 2
WIN = 2048
CWID = 1024


def draw_slot_cols(key, part):
    subkeys = jax.random.split(jax.random.fold_in(key, 11), FRONTS * SLOTS_ALL)

    def draw_row(row_key):
        return jax.random.permutation(row_key, WB)[:CW]
    chosen = jax.vmap(draw_row)(subkeys)
    return chosen.reshape(FRONTS, SLOTS_ALL, CW).astype(jnp.int32)


def plant(values, rng, smallest, largest):
    spot = [jax.random.randint(jax.random.fold_in(rng, axis), (), 0, length) for axis, length in enumerate(values.shape)]
    longest = values.shape.index(max(values.shape))
    next_to = spot[:longest] + [(spot[longest] + 1) % values.shape[longest]] + spot[longest + 1:]
    return values.at[tuple(spot)].set(smallest).at[tuple(next_to)].set(largest)


def steps_of(rng, dims, pieces, smallest, top_value):
    def one(position, blocks):
        heights = jax.random.uniform(jax.random.fold_in(jax.random.fold_in(rng, 6), position), (blocks,), jnp.float32, smallest / len(pieces), top_value / len(pieces))
        return jnp.repeat(jnp.exp(heights), dims[position] // blocks).reshape((-1,) + (1,) * (len(dims) - position - 1))

    level = one(*pieces[0])
    for cut in pieces[1:]:
        level = level * one(*cut)
    return level


def shared_out(rng, own, number, rows, amount, top, reach, slope):
    ranking = jax.random.permutation(rng, amount)
    heavy_load, usual = portions_of(amount, rows * top, reach, slope, True), portions_of(amount, rows * top, reach, slope, False)
    places = jnp.arange(amount)

    def named(tallies, turn):
        used = int((tallies > 0).sum())
        fixed = max(1, used // 4)
        passed = fixed + (places - fixed + turn * (used - fixed)) % max(1, amount - fixed)
        return jnp.zeros((amount,), jnp.int32).at[ranking[jnp.where(places < fixed, places, passed)]].set(jnp.asarray(tallies, jnp.int32))

    tallies = jnp.where(number % 4 == 0, named(heavy_load, number // 4), named(usual, number - number // 4 - 1))
    mixed = jax.random.permutation(jax.random.fold_in(own, 3), amount)
    source_of, sink = mixed[0:amount // 2 * 2:2], mixed[1:amount // 2 * 2:2]
    margin = jnp.minimum(tallies[source_of] - 1, reach - tallies[sink]) // 2
    margin = jnp.where((source_of == ranking[0]) | (sink == ranking[0]) | (tallies[sink] == 0), 0, jnp.maximum(margin, 0))
    passed = jax.random.randint(jax.random.fold_in(own, 4), (amount // 2,), 0, 1 << 20) % (margin + 1)
    tallies = tallies.at[source_of].add(-passed).at[sink].add(passed)
    items = jnp.searchsorted(jnp.cumsum(tallies), jnp.arange(rows * top), side="right").astype(jnp.int32)
    table = items.reshape(top, rows).T
    table = table[jax.random.permutation(jax.random.fold_in(own, 1), rows)]
    turn = jax.random.randint(jax.random.fold_in(own, 2), (rows, 1), 0, top)
    return jnp.take_along_axis(table, (jnp.arange(top)[None, :] + turn) % top, axis=1)


def portions_of(number_of, total, reach, lean, full):
    portions = [(1 << 20) // math.isqrt(grade ** lean) + 1 for grade in range(1, number_of + 1)]
    largest = reach if full else min(reach, max(-(-total // number_of), total * portions[0] // sum(portions)))
    least = 1 if total - largest >= number_of - 1 else 0
    holding, spare = [largest] + [least] * (number_of - 1), total - largest - least * (number_of - 1)
    while spare > 0:
        candidates = [i for i in range(1, number_of) if holding[i] < largest] or [i for i in range(1, number_of) if holding[i] < reach]
        mass, remaining = sum([portions[i] for i in candidates]), spare
        for i in candidates:
            addition = min(reach - holding[i], max(1, remaining * portions[i] // mass), spare)
            holding[i] = holding[i] + addition
            spare = spare - addition
    return np.array(holding)


def normal_values(stream_key, dims, width, most, pieces=(), kind=jnp.bfloat16):
    array = width * jax.random.normal(stream_key, dims, jnp.float32)
    if pieces:
        array = array * steps_of(stream_key, dims, pieces, -0.22, 0.18)
    return jnp.clip(array, -most, most).astype(kind)


def setup_inputs(seed: int = 0) -> dict:
    arg_keys = jax.random.split(jax.random.key(seed), 7)
    updates = normal_values(arg_keys[0], (FRONTS, SLOTS_ALL * BLOCK, CWID), 1.0, 6.0, ((0, 2), (1, 16)))
    parent_panels = normal_values(arg_keys[1], (FRONTS, FRONT_ORDER, WIN), 1.0, 6.0, ((0, 2), (1, 16)))
    slot_parent_keys = jax.random.split(jax.random.fold_in(arg_keys[2], 1), FRONTS * SLOTS_ALL // SLOTS)
    slot_parent_turns = jax.random.permutation(jax.random.fold_in(arg_keys[2], 3), FRONTS * SLOTS_ALL // SLOTS)
    slot_parent = jax.vmap(lambda own, number: shared_out(jax.random.fold_in(arg_keys[2], 2), own, number, SLOTS, FRONTS, 1, CAPF, 2))(slot_parent_keys, slot_parent_turns).reshape((FRONTS, SLOTS_ALL, 1))
    slot_row = plant(jax.random.randint(arg_keys[3], (FRONTS, SLOTS_ALL), 0, RB), jax.random.fold_in(arg_keys[3], 1), 0, RB - 1).astype(jnp.int32)
    slot_cols = draw_slot_cols(jax.random.fold_in(arg_keys[6], 71), 0)
    slot_mask = plant((jax.random.randint(arg_keys[5], (FRONTS, SLOTS_ALL, CW), 0, 4) < 3).astype(jnp.int32), jax.random.fold_in(arg_keys[5], 1), 0, 1)
    return dict(updates=updates, parent_panels=parent_panels, slot_parent=slot_parent, slot_row=slot_row, slot_cols=slot_cols, slot_mask=slot_mask)


def reference(updates, parent_panels, slot_parent, slot_row, slot_cols, slot_mask):
    window = parent_panels.reshape(FRONTS, PANELS, RB, BLOCK, WIN)
    window = jnp.transpose(window, (0, 2, 1, 3, 4)).reshape(FRONTS, NB, BLOCK, WB, BLOCK).astype(jnp.float32)
    owners = jnp.arange(SLOTS_ALL, dtype=jnp.int32) // SLOTS

    def add_group(running_sum, group_index):
        blocks = lax.dynamic_index_in_dim(updates, group_index, 0, keepdims=False)
        blocks = blocks.reshape(SLOTS_ALL, BLOCK, CW, BLOCK).astype(jnp.float32)
        blocks = jnp.transpose(blocks, (0, 2, 1, 3))
        pattern = lax.dynamic_index_in_dim(slot_mask, group_index, 0, keepdims=False).astype(jnp.float32)
        blocks = blocks * pattern[:, :, None, None]
        parents = lax.dynamic_index_in_dim(slot_parent, group_index, 0, keepdims=False)[:, 0]
        block_row = lax.dynamic_index_in_dim(slot_row, group_index, 0, keepdims=False) * PANELS + owners
        block_col = lax.dynamic_index_in_dim(slot_cols, group_index, 0, keepdims=False)
        running_sum = running_sum.at[parents[:, None], block_row[:, None], :, block_col, :].add(blocks)
        return running_sum, None

    summed, unused = lax.scan(add_group, window, jnp.arange(FRONTS, dtype=jnp.int32))
    assembled = summed.astype(jnp.bfloat16)
    arranged = assembled.reshape(FRONTS, GRID_BLOCK_ROWS, GRID_ROWS, BLOCK, WB // GRID_COLS, GRID_COLS, BLOCK)
    arranged = jnp.transpose(arranged, (0, 5, 2, 1, 3, 4, 6))
    return arranged.reshape(FRONTS, PANELS * GRID_BLOCK_ROWS * BLOCK, (WB // GRID_COLS) * BLOCK)
```

```python
import functools

import jax
import jax.numpy as jnp
from jax import lax
from jax.experimental import pallas as pl
from jax.experimental.pallas import tpu as pltpu
from jax.sharding import PartitionSpec as P

GRID_COLS = 8
NEAR = GRID_COLS // 2
TAG = 8

ANY = pl.BlockSpec(memory_space=pl.ANY)
HBM = pl.BlockSpec(memory_space=pltpu.HBM)
SMEM = pl.BlockSpec(memory_space=pltpu.SMEM)
VMEM = pl.BlockSpec(memory_space=pltpu.VMEM)


class Plan:
    def __init__(self, updates, panels, slot_cols):
        self.groups = lax.axis_size("front")
        self.lanes = lax.axis_size("wide")
        self.grid_rows = self.lanes // GRID_COLS
        self.slots = slot_cols.shape[1]
        self.columns = slot_cols.shape[2]
        self.block = updates.shape[1] // self.slots
        self.rows = panels.shape[1] // self.block
        self.window = panels.shape[2] // self.block
        self.col_groups = self.window // GRID_COLS
        self.width = self.col_groups * self.block
        self.capacity = max(self.slots // 4, self.slots // self.groups)
        self.first = max(0, self.rows - self.capacity * self.groups)
        self.second = self.rows - self.first


def params():
    return pltpu.CompilerParams(vmem_limit_bytes=48 << 20)


def at(start, size):
    return pl.ds(pl.multiple_of(start * size, size), size)


def parent_of(plan, codes, q):
    return codes[q, 0] // (plan.rows * 2 * plan.window)


def row_of(plan, codes, q):
    return (codes[q, 0] // (2 * plan.window)) % plan.rows


def first_set(plan, code_refs):
    me = lax.axis_index("front")
    touched = jnp.int32(0)
    for codes in code_refs:
        for q in range(plan.slots):
            bit = jnp.left_shift(jnp.int32(1), row_of(plan, codes, q))
            touched = touched | jnp.where(parent_of(plan, codes, q) == me, bit, 0)
    chosen, count = jnp.int32(0), jnp.int32(0)
    for t in range(plan.rows):
        free = (jnp.right_shift(touched, t) & 1) == 0
        take = jnp.logical_and(free, count < plan.first)
        chosen = chosen | jnp.where(take, 1 << t, 0)
        count = count + jnp.where(take, 1, 0)
    return chosen


def positions(plan, chosen):
    out, count = [], jnp.int32(0)
    for t in range(plan.rows):
        bit = jnp.right_shift(chosen, t) & 1
        out.append((bit, jnp.where(bit == 1, count, t - count)))
        count = count + bit
    return out


def run_all(copies):
    for copy in copies:
        copy.start()
    for copy in copies:
        copy.wait()


def bucket_kernel(plan, codes, updates, *refs):
    outs, sems = refs[:-1], refs[-1]
    me = lax.axis_index("front")

    def copies(act):
        for k in range(1, plan.groups):
            target = lax.rem(me + k, plan.groups)
            rank = jnp.int32(0)
            for q in range(plan.slots):
                named = parent_of(plan, codes, q) == target

                @pl.when(named)
                def _():
                    act(
                        pltpu.make_async_copy(
                            updates.at[0, pl.ds(q * plan.block, plan.block)],
                            outs[k - 1].at[rank],
                            sems.at[q],
                        )
                    )

                rank = rank + jnp.where(named, 1, 0)

    copies(lambda c: c.start())
    copies(lambda c: c.wait())


def pack_kernel(plan, *refs):
    groups = plan.groups
    code_refs, panel = refs[:groups], refs[groups]
    outs, order, sems = refs[groups + 1 : -2], refs[-2], refs[-1]
    column = lax.axis_index("wide") // plan.grid_rows
    chosen = first_set(plan, code_refs)
    for t, (bit, place) in enumerate(positions(plan, chosen)):

        @pl.when(bit == 1)
        def _():
            order[place] = t

    copies = []
    for i in range(NEAR):
        target = jnp.bitwise_xor(column, NEAR + i)
        for k in range(plan.first):
            t = order[k]
            for cc in range(plan.col_groups):
                copies.append(
                    pltpu.make_async_copy(
                        panel.at[0, at(t, plan.block), at(cc * GRID_COLS + target, plan.block)],
                        outs[i].at[
                            pl.ds(k * plan.block, plan.block), pl.ds(cc * plan.block, plan.block)
                        ],
                        sems.at[i, k, cc],
                    )
                )
    for copy in copies:
        copy.start()
    tag = jnp.full((TAG, plan.width), chosen.astype(jnp.float32), jnp.float32).astype(jnp.bfloat16)
    for i in range(NEAR):
        outs[i][plan.first * plan.block :, :] = tag
    for copy in copies:
        copy.wait()


def assemble_kernel(plan, *refs):
    groups, block = plan.groups, plan.block
    code_refs, refs = refs[:groups], refs[groups:]
    panel, updates, refs = refs[0], refs[1], refs[2:]
    got, refs = refs[: groups - 1], refs[groups - 1 :]
    far, near, refs = refs[:NEAR], refs[NEAR : 2 * NEAR], refs[2 * NEAR :]
    total, raw, moved, place_ref, row_sems, slot_sems = refs
    me = lax.axis_index("front")
    column = lax.axis_index("wide") // plan.grid_rows

    slot_copies = [
        pltpu.make_async_copy(
            updates.at[0, pl.ds(q * block, block)], moved.at[q], slot_sems.at[q]
        )
        for q in range(plan.slots)
    ]
    for k in range(1, groups):
        for c in range(plan.capacity):
            index = plan.slots + (k - 1) * plan.capacity + c
            slot_copies.append(
                pltpu.make_async_copy(got[k - 1].at[c], moved.at[index], slot_sems.at[index])
            )
    row_copies = [
        pltpu.make_async_copy(panel.at[0, pl.ds(t * block, block)], raw.at[t], row_sems.at[t])
        for t in range(plan.rows)
    ]
    for copy in row_copies + slot_copies:
        copy.start()

    chosen = first_set(plan, code_refs)
    for t, (bit, place) in enumerate(positions(plan, chosen)):
        place_ref[t] = jnp.where(bit == 1, -1, place)

    for t in range(plan.rows):
        row_copies[t].wait()
    for copy in slot_copies:
        copy.wait()

    def widen(t, carry):
        total[t] = raw[t].astype(jnp.float32)
        return carry

    lax.fori_loop(0, plan.rows, widen, 0)

    for s, codes in enumerate(code_refs):

        def add_slot(q, rank):
            named = parent_of(plan, codes, q) == me
            index = q if s == 0 else plan.slots + (s - 1) * plan.capacity + rank
            t = row_of(plan, codes, q)

            @pl.when(named)
            def _():
                for j in range(plan.columns):
                    code = codes[q, j]
                    col = code % plan.window

                    @pl.when((code // plan.window) % 2 == 1)
                    def _():
                        where = at(col, block)
                        total[t, :, where] += moved[
                            index, :, pl.ds(j * block, block)
                        ].astype(jnp.float32)

            return rank + jnp.where(named, 1, 0)

        lax.fori_loop(0, plan.slots, add_slot, jnp.int32(0))

    def pack(t, carry):
        place = place_ref[t]
        for o in range(GRID_COLS):
            target = jnp.bitwise_xor(column, o)

            def put(ref, row):
                for cc in range(plan.col_groups):
                    ref[at(row, block), pl.ds(cc * block, block)] = total[
                        t, :, at(cc * GRID_COLS + target, block)
                    ].astype(jnp.bfloat16)

            if o < NEAR:
                put(near[o], t)
            else:

                @pl.when(place >= 0)
                def _():
                    put(far[o - NEAR], place)

        return carry

    lax.fori_loop(0, plan.rows, pack, 0)


def place_first_kernel(plan, *refs):
    pieces, out, sets, refs = refs[:NEAR], refs[NEAR], refs[NEAR + 1], refs[NEAR + 2 :]
    tags, where, tag_sems, sems = refs
    column = lax.axis_index("wide") // plan.grid_rows
    block = plan.block
    run_all(
        [
            pltpu.make_async_copy(
                pieces[i].at[pl.ds(plan.first * block, TAG)], tags.at[i], tag_sems.at[i]
            )
            for i in range(NEAR)
        ]
    )
    copies = []
    for i in range(NEAR):
        source = jnp.bitwise_xor(column, NEAR + i)
        chosen = jnp.max(tags[i].astype(jnp.float32)).astype(jnp.int32)
        sets[i] = chosen
        for t, (bit, place) in enumerate(positions(plan, chosen)):

            @pl.when(bit == 1)
            def _():
                where[i, place] = t

        for k in range(plan.first):
            copies.append(
                pltpu.make_async_copy(
                    pieces[i].at[pl.ds(k * block, block)],
                    out.at[at(where[i, k] * GRID_COLS + source, block)],
                    sems.at[i, k],
                )
            )
            copies[-1].start()
    for copy in copies:
        copy.wait()


def place_near_kernel(plan, aliased, pieces, out, sems):
    column = lax.axis_index("wide") // plan.grid_rows
    block = plan.block
    copies = []
    for o in pieces:
        source = jnp.bitwise_xor(column, o)
        for t in range(plan.rows):
            copies.append(
                pltpu.make_async_copy(
                    pieces[o].at[pl.ds(t * block, block)],
                    out.at[at(t * GRID_COLS + source, block)],
                    sems.at[o, t],
                )
            )
    run_all(copies)


def place_far_kernel(plan, *refs):
    refs = refs[1:] if plan.first else refs
    sets = refs[0] if plan.first else None
    refs = refs[1:] if plan.first else refs
    pieces, out, where, sems = refs[:NEAR], refs[NEAR], refs[NEAR + 1], refs[NEAR + 2]
    column = lax.axis_index("wide") // plan.grid_rows
    block = plan.block
    copies = []
    for i in range(NEAR):
        source = jnp.bitwise_xor(column, NEAR + i)
        if plan.first:
            for t, (bit, place) in enumerate(positions(plan, sets[i])):

                @pl.when(bit == 0)
                def _():
                    where[i, place] = t

        for k in range(plan.second):
            t = where[i, k] if plan.first else k
            copies.append(
                pltpu.make_async_copy(
                    pieces[i].at[pl.ds(k * block, block)],
                    out.at[at(t * GRID_COLS + source, block)],
                    sems.at[i, k],
                )
            )
            copies[-1].start()
    for copy in copies:
        copy.wait()


def across(value, plan, offset):
    pairs = [
        (c * plan.grid_rows + r, (c ^ offset) * plan.grid_rows + r)
        for c in range(GRID_COLS)
        for r in range(plan.grid_rows)
    ]
    return lax.ppermute(value, "wide", pairs)


def along(value, plan, steps):
    return lax.ppermute(
        value, "front", [(f, (f + steps) % plan.groups) for f in range(plan.groups)]
    )


def local(updates, parent_panels, slot_parent, slot_row, slot_cols, slot_mask):
    plan = Plan(updates, parent_panels, slot_cols)
    block, width = plan.block, plan.width
    bf16 = jnp.bfloat16
    head = slot_parent[0, :, 0] * plan.rows + slot_row[0]
    codes = (head[:, None] * 2 + slot_mask[0]) * plan.window + slot_cols[0]
    all_codes = [codes] + [along(codes, plan, k) for k in range(1, plan.groups)]

    buckets = pl.pallas_call(
        functools.partial(bucket_kernel, plan),
        out_shape=[
            jax.ShapeDtypeStruct((plan.capacity, block, updates.shape[2]), bf16)
            for _ in range(1, plan.groups)
        ],
        in_specs=[SMEM, ANY],
        out_specs=[ANY] * (plan.groups - 1),
        scratch_shapes=[pltpu.SemaphoreType.DMA((plan.slots,))],
        name="bucket",
    )(codes, updates)

    far_first = []
    if plan.first:
        packed = pl.pallas_call(
            functools.partial(pack_kernel, plan),
            out_shape=[jax.ShapeDtypeStruct((plan.first * block + TAG, width), bf16)] * NEAR,
            in_specs=[SMEM] * plan.groups + [ANY],
            out_specs=[VMEM] * NEAR,
            scratch_shapes=[
                pltpu.SMEM((plan.rows,), jnp.int32),
                pltpu.SemaphoreType.DMA((NEAR, plan.first, plan.col_groups)),
            ],
            compiler_params=params(),
            name="pack_first",
        )(*all_codes, parent_panels)
        far_first = [across(packed[i], plan, NEAR + i) for i in range(NEAR)]

    got = [along(buckets[k - 1], plan, k) for k in range(1, plan.groups)]

    moved = plan.slots + (plan.groups - 1) * plan.capacity
    assembled = pl.pallas_call(
        functools.partial(assemble_kernel, plan),
        out_shape=[jax.ShapeDtypeStruct((plan.second * block, width), bf16)] * NEAR
        + [jax.ShapeDtypeStruct((plan.rows * block, width), bf16)] * NEAR,
        in_specs=[SMEM] * plan.groups + [ANY] * (1 + plan.groups),
        out_specs=[VMEM] * (2 * NEAR),
        scratch_shapes=[
            pltpu.VMEM((plan.rows, block, parent_panels.shape[2]), jnp.float32),
            pltpu.VMEM((plan.rows, block, parent_panels.shape[2]), bf16),
            pltpu.VMEM((moved, block, updates.shape[2]), bf16),
            pltpu.SMEM((plan.rows,), jnp.int32),
            pltpu.SemaphoreType.DMA((plan.rows,)),
            pltpu.SemaphoreType.DMA((moved,)),
        ],
        compiler_params=params(),
        name="assemble",
    )(*all_codes, parent_panels, updates, *got)
    far, near = assembled[:NEAR], assembled[NEAR:]
    far_second = [across(far[i], plan, NEAR + i) for i in range(NEAR)]
    near_all = [near[0]] + [across(near[o], plan, o) for o in range(1, NEAR)]

    out_shape = jax.ShapeDtypeStruct((plan.rows * GRID_COLS * block, width), bf16)
    out, sets = None, None
    if plan.first:
        out, sets = pl.pallas_call(
            functools.partial(place_first_kernel, plan),
            out_shape=[out_shape, jax.ShapeDtypeStruct((NEAR,), jnp.int32)],
            in_specs=[ANY] * NEAR,
            out_specs=[HBM, SMEM],
            scratch_shapes=[
                pltpu.VMEM((NEAR, TAG, width), bf16),
                pltpu.SMEM((NEAR, plan.rows), jnp.int32),
                pltpu.SemaphoreType.DMA((NEAR,)),
                pltpu.SemaphoreType.DMA((NEAR, plan.first)),
            ],
            compiler_params=params(),
            name="place_first",
        )(*far_first)

    def near_body(*refs):
        refs = list(refs)
        if plan.first:
            refs = refs[1:]
        place_near_kernel(plan, None, dict(enumerate(refs[:NEAR])), refs[NEAR], refs[NEAR + 1])

    held = [out] if plan.first else []
    out = pl.pallas_call(
        near_body,
        out_shape=out_shape,
        in_specs=[HBM] * len(held) + [ANY] * NEAR,
        out_specs=HBM,
        input_output_aliases={0: 0} if held else {},
        scratch_shapes=[pltpu.SemaphoreType.DMA((NEAR, plan.rows))],
        compiler_params=params(),
        name="place_near",
    )(*held, *near_all)

    extra = [sets] if plan.first else []

    def far_body(*refs):
        refs = list(refs)[1:]
        sets_ref = [refs.pop(0)] if plan.first else []
        lead = [None] if plan.first else []
        place_far_kernel(plan, *(lead + sets_ref + refs))

    out = pl.pallas_call(
        far_body,
        out_shape=out_shape,
        in_specs=[HBM] + [SMEM] * len(extra) + [ANY] * NEAR,
        out_specs=HBM,
        input_output_aliases={0: 0},
        scratch_shapes=[
            pltpu.SMEM((NEAR, plan.rows), jnp.int32),
            pltpu.SemaphoreType.DMA((NEAR, plan.second)),
        ],
        compiler_params=params(),
        name="place_far",
    )(out, *extra, *far_second)
    return out[None]


def solution(mesh):
    return jax.shard_map(
        local,
        mesh=mesh,
        in_specs=(
            P("front", "wide", None),
            P("front", "wide", None),
            P("front", "wide", None),
            P("front", "wide"),
            P("front", "wide", None),
            P("front", "wide", None),
        ),
        out_specs=P("front", "wide", None),
        check_vma=False,
    )
```

```python
import functools

import jax
import jax.numpy as jnp
from jax import lax
from jax.experimental import pallas as pl
from jax.experimental.pallas import tpu as pltpu
from jax.sharding import PartitionSpec as P

GRID_COLS = 8
NEAR = GRID_COLS // 2
FAR = (5, 7, 4, 6)
TAG = 8

ANY = pl.BlockSpec(memory_space=pl.ANY)
HBM = pl.BlockSpec(memory_space=pltpu.HBM)
SMEM = pl.BlockSpec(memory_space=pltpu.SMEM)
VMEM = pl.BlockSpec(memory_space=pltpu.VMEM)


class Plan:
    def __init__(self, updates, panels, slot_cols):
        self.groups = lax.axis_size("front")
        self.lanes = lax.axis_size("wide")
        self.grid_rows = self.lanes // GRID_COLS
        self.slots = slot_cols.shape[1]
        self.columns = slot_cols.shape[2]
        self.block = updates.shape[1] // self.slots
        self.rows = panels.shape[1] // self.block
        self.window = panels.shape[2] // self.block
        self.col_groups = self.window // GRID_COLS
        self.width = self.col_groups * self.block
        self.capacity = max(self.slots // 4, self.slots // self.groups)
        self.first = max(0, self.rows - self.capacity * self.groups)
        self.early = {5: self.first, 7: self.first, 4: self.first, 6: 0}
        self.late = [(o, 0, self.rows) for o in range(NEAR)]
        for o in FAR:
            count = self.rows - self.early[o]
            cuts = [0, count // 2, count] if o == 6 else [0, count]
            self.late += [(o, lo, hi) for lo, hi in zip(cuts, cuts[1:])]


COST = pl.CostEstimate(flops=0, transcendentals=0, bytes_accessed=0)


def params():
    return pltpu.CompilerParams(vmem_limit_bytes=48 << 20)


def at(start, size):
    return pl.ds(pl.multiple_of(start * size, size), size)


def parent_of(plan, heads, q):
    return heads[q] // plan.rows


def row_of(plan, heads, q):
    return heads[q] % plan.rows


def touched_rows(plan, head_refs):
    me = lax.axis_index("front")
    touched = jnp.int32(0)
    for heads in head_refs:
        for q in range(plan.slots):
            bit = jnp.left_shift(jnp.int32(1), row_of(plan, heads, q))
            touched = touched | jnp.where(parent_of(plan, heads, q) == me, bit, 0)
    return touched


def first_rows(plan, touched, limit):
    chosen, count = jnp.int32(0), jnp.int32(0)
    for t in range(plan.rows):
        free = (jnp.right_shift(touched, t) & 1) == 0
        take = jnp.logical_and(free, count < limit)
        chosen = chosen | jnp.where(take, 1 << t, 0)
        count = count + jnp.where(take, 1, 0)
    return chosen


def positions(plan, chosen):
    out, count = [], jnp.int32(0)
    for t in range(plan.rows):
        bit = jnp.right_shift(chosen, t) & 1
        out.append((bit, jnp.where(bit == 1, count, t - count)))
        count = count + bit
    return out


def list_rows(plan, chosen, bit_wanted, where):
    for t, (bit, place) in enumerate(positions(plan, chosen)):

        @pl.when(bit == bit_wanted)
        def _():
            where[place] = t


def run_all(copies):
    for copy in copies:
        copy.start()
    for copy in copies:
        copy.wait()


def bucket_kernel(plan, heads, updates, *refs):
    outs, sems = refs[-plan.groups : -1], refs[-1]
    me = lax.axis_index("front")

    def copies(act):
        for k in range(1, plan.groups):
            target = lax.rem(me + k, plan.groups)
            rank = jnp.int32(0)
            for q in range(plan.slots):
                named = parent_of(plan, heads, q) == target

                @pl.when(named)
                def _():
                    act(
                        pltpu.make_async_copy(
                            updates.at[0, pl.ds(q * plan.block, plan.block)],
                            outs[k - 1].at[rank],
                            sems.at[q],
                        )
                    )

                rank = rank + jnp.where(named, 1, 0)

    copies(lambda c: c.start())
    copies(lambda c: c.wait())


def pack_kernel(plan, offsets, *refs):
    groups = plan.groups
    head_refs, panel = refs[:groups], refs[groups]
    outs, refs = refs[groups + 1 : groups + 1 + len(offsets)], refs[groups + 1 + len(offsets) :]
    touched_out, order, sems = refs
    column = lax.axis_index("wide") // plan.grid_rows
    block = plan.block
    touched = touched_rows(plan, head_refs)
    touched_out[0] = touched
    list_rows(plan, first_rows(plan, touched, plan.first), 1, order)
    copies = []
    for i, o in enumerate(offsets):
        target = jnp.bitwise_xor(column, o)
        for k in range(plan.early[o]):
            for cc in range(plan.col_groups):
                copies.append(
                    pltpu.make_async_copy(
                        panel.at[0, at(order[k], block), at(cc * GRID_COLS + target, block)],
                        outs[i].at[pl.ds(k * block, block), pl.ds(cc * block, block)],
                        sems.at[i, k, cc],
                    )
                )
                copies[-1].start()
    for i, o in enumerate(offsets):
        chosen = first_rows(plan, touched, plan.early[o]).astype(jnp.float32)
        tag = jnp.full((TAG, plan.width), chosen, jnp.float32).astype(jnp.bfloat16)
        outs[i][plan.early[o] * block :, :] = tag
    for copy in copies:
        copy.wait()


def assemble_kernel(plan, *refs):
    groups, block = plan.groups, plan.block
    head_refs, refs = refs[:groups], refs[groups:]
    code_refs, refs = refs[:groups], refs[groups:]
    panel, updates, refs = refs[0], refs[1], refs[2:]
    got, refs = refs[: groups - 1], refs[groups - 1 :]
    outs, refs = refs[: len(plan.late)], refs[len(plan.late) :]
    total, raw, moved, place_ref, row_sems, slot_sems = refs
    me = lax.axis_index("front")
    column = lax.axis_index("wide") // plan.grid_rows

    slot_copies = [
        pltpu.make_async_copy(
            updates.at[0, pl.ds(q * block, block)], moved.at[q], slot_sems.at[q]
        )
        for q in range(plan.slots)
    ]
    for k in range(1, groups):
        for c in range(plan.capacity):
            index = plan.slots + (k - 1) * plan.capacity + c
            slot_copies.append(
                pltpu.make_async_copy(got[k - 1].at[c], moved.at[index], slot_sems.at[index])
            )
    row_copies = [
        pltpu.make_async_copy(panel.at[0, pl.ds(t * block, block)], raw.at[t], row_sems.at[t])
        for t in range(plan.rows)
    ]
    for copy in row_copies + slot_copies:
        copy.start()

    touched = touched_rows(plan, head_refs)
    for o in FAR:
        for t, (bit, place) in enumerate(
            positions(plan, first_rows(plan, touched, plan.early[o]))
        ):
            place_ref[o, t] = jnp.where(bit == 1, -1, place)

    for t in range(plan.rows):
        row_copies[t].wait()
    for copy in slot_copies:
        copy.wait()

    def widen(t, carry):
        total[t] = raw[t].astype(jnp.float32)
        return carry

    lax.fori_loop(0, plan.rows, widen, 0)

    for s, (heads, codes) in enumerate(zip(head_refs, code_refs)):

        def add_slot(q, rank):
            named = parent_of(plan, heads, q) == me
            index = q if s == 0 else plan.slots + (s - 1) * plan.capacity + rank
            t = row_of(plan, heads, q)

            @pl.when(named)
            def _():
                for j in range(plan.columns):
                    code = codes[q, j]
                    col = code % plan.window

                    @pl.when(code >= plan.window)
                    def _():
                        where = at(col, block)
                        total[t, :, where] += moved[
                            index, :, pl.ds(j * block, block)
                        ].astype(jnp.float32)

            return rank + jnp.where(named, 1, 0)

        lax.fori_loop(0, plan.slots, add_slot, jnp.int32(0))

    def pack(t, carry):
        for ref, (o, lo, hi) in zip(outs, plan.late):
            target = jnp.bitwise_xor(column, o)

            def put(row):
                for cc in range(plan.col_groups):
                    ref[at(row, block), pl.ds(cc * block, block)] = total[
                        t, :, at(cc * GRID_COLS + target, block)
                    ].astype(jnp.bfloat16)

            if hi - lo == plan.rows:
                put(t)
            else:
                place = place_ref[o, t] if plan.early[o] else t
                pl.when(jnp.logical_and(place >= lo, place < hi))(lambda: put(place - lo))

        return carry

    lax.fori_loop(0, plan.rows, pack, 0)


def place_early_kernel(plan, offsets, *refs):
    count = len(offsets)
    pieces, out, sets, refs = refs[:count], refs[count], refs[count + 1], refs[count + 2 :]
    tags, where, tag_sems, sems = refs
    column = lax.axis_index("wide") // plan.grid_rows
    block = plan.block
    run_all(
        [
            pltpu.make_async_copy(
                pieces[i].at[pl.ds(plan.early[o] * block, TAG)], tags.at[i], tag_sems.at[i]
            )
            for i, o in enumerate(offsets)
        ]
    )
    copies = []
    for i, o in enumerate(offsets):
        source = jnp.bitwise_xor(column, o)
        chosen = jnp.max(tags[i].astype(jnp.float32)).astype(jnp.int32)
        sets[i] = chosen
        list_rows(plan, chosen, 1, where.at[i])
        for k in range(plan.early[o]):
            copies.append(
                pltpu.make_async_copy(
                    pieces[i].at[pl.ds(k * block, block)],
                    out.at[at(where[i, k] * GRID_COLS + source, block)],
                    sems.at[i, k],
                )
            )
            copies[-1].start()
    for copy in copies:
        copy.wait()


def place_late_kernel(plan, messages, early, sets, pieces, out, where, sems):
    column = lax.axis_index("wide") // plan.grid_rows
    block = plan.block
    copies = []
    for i, (o, lo, hi) in enumerate(messages):
        source = jnp.bitwise_xor(column, o)
        split = o in early
        if split:
            list_rows(plan, sets[early.index(o)], 0, where.at[i])
        for k in range(lo, hi):
            t = where[i, k] if split else k
            copies.append(
                pltpu.make_async_copy(
                    pieces[i].at[pl.ds((k - lo) * block, block)],
                    out.at[at(t * GRID_COLS + source, block)],
                    sems.at[i, k],
                )
            )
            copies[-1].start()
    for copy in copies:
        copy.wait()


def after(value, *others):
    return lax.optimization_barrier((value, *others))[0]


def across(value, plan, offset):
    pairs = [
        (c * plan.grid_rows + r, (c ^ offset) * plan.grid_rows + r)
        for c in range(GRID_COLS)
        for r in range(plan.grid_rows)
    ]
    return lax.ppermute(value, "wide", pairs)


def along(value, plan, steps):
    return lax.ppermute(
        value, "front", [(f, (f + steps) % plan.groups) for f in range(plan.groups)]
    )


def local(updates, parent_panels, slot_parent, slot_row, slot_cols, slot_mask):
    plan = Plan(updates, parent_panels, slot_cols)
    block, width = plan.block, plan.width
    bf16 = jnp.bfloat16
    heads = slot_parent[0, :, 0] * plan.rows + slot_row[0]
    all_heads = [heads] + [along(heads, plan, k) for k in range(1, plan.groups)]
    codes = slot_mask[0] * plan.window + slot_cols[0]
    panels = pltpu.with_memory_space_constraint(parent_panels, pltpu.HBM)


    early = [o for o in FAR if plan.early[o]]
    packed, touched = {}, []
    if early:
        *outs, touched_set = pl.pallas_call(
            functools.partial(pack_kernel, plan, early),
            out_shape=[
                jax.ShapeDtypeStruct((plan.early[o] * block + TAG, width), bf16) for o in early
            ]
            + [jax.ShapeDtypeStruct((1,), jnp.int32)],
            in_specs=[SMEM] * plan.groups + [HBM],
            out_specs=[VMEM] * len(early) + [SMEM],
            scratch_shapes=[
                pltpu.SMEM((plan.rows,), jnp.int32),
                pltpu.SemaphoreType.DMA((len(early), plan.first, plan.col_groups)),
            ],
            compiler_params=params(),
            cost_estimate=COST,
            name="pack_early",
        )(*all_heads, panels)
        packed = dict(zip(early, outs))
        touched = [touched_set]
        codes = after(codes, touched_set)

    buckets = pl.pallas_call(
        functools.partial(bucket_kernel, plan),
        out_shape=[
            jax.ShapeDtypeStruct((plan.capacity, block, updates.shape[2]), bf16)
            for _ in range(1, plan.groups)
        ],
        in_specs=[SMEM, HBM] + [SMEM] * len(touched),
        out_specs=[VMEM] * (plan.groups - 1),
        scratch_shapes=[pltpu.SemaphoreType.DMA((plan.slots,))],
        compiler_params=params(),
        cost_estimate=COST,
        name="bucket",
    )(heads, updates, *touched)

    all_codes = [codes] + [along(codes, plan, k) for k in range(1, plan.groups)]
    got = [along(buckets[k - 1], plan, k) for k in range(1, plan.groups)]

    moved = plan.slots + (plan.groups - 1) * plan.capacity
    assembled = pl.pallas_call(
        functools.partial(assemble_kernel, plan),
        out_shape=[
            jax.ShapeDtypeStruct(((hi - lo) * block, width), bf16) for o, lo, hi in plan.late
        ],
        in_specs=[SMEM] * (2 * plan.groups) + [HBM, HBM] + [ANY] * (plan.groups - 1),
        out_specs=[VMEM] * len(plan.late),
        scratch_shapes=[
            pltpu.VMEM((plan.rows, block, parent_panels.shape[2]), jnp.float32),
            pltpu.VMEM((plan.rows, block, parent_panels.shape[2]), bf16),
            pltpu.VMEM((moved, block, updates.shape[2]), bf16),
            pltpu.SMEM((GRID_COLS, plan.rows), jnp.int32),
            pltpu.SemaphoreType.DMA((plan.rows,)),
            pltpu.SemaphoreType.DMA((moved,)),
        ],
        compiler_params=params(),
        cost_estimate=COST,
        name="assemble",
    )(*all_heads, *all_codes, panels, updates, *got)

    ready = dict(zip(plan.late, assembled))

    def late(o, part=0):
        return [m for m in plan.late if m[0] == o][part]

    first = {o: across(packed[o], plan, o) for o in early}
    arrived = {late(0): ready[late(0)]}

    def send(message, *others):
        arrived[message] = across(after(ready[message], *others), plan, message[0])
        return arrived[message]

    gate = [first[o] for o in early]
    a = send(late(5), *gate)
    b = send(late(7), *gate)
    send(late(4), *gate)
    n1 = send(late(1), *gate)
    n2 = send(late(2), *gate)
    send(late(3), n1, n2)
    send(late(6, 0), a)
    send(late(6, 1), b)

    out_shape = jax.ShapeDtypeStruct((plan.rows * GRID_COLS * block, width), bf16)
    held, sets = [], []
    if early:
        out, sets = pl.pallas_call(
            functools.partial(place_early_kernel, plan, early),
            out_shape=[out_shape, jax.ShapeDtypeStruct((len(early),), jnp.int32)],
            in_specs=[ANY] * len(early),
            out_specs=[HBM, SMEM],
            scratch_shapes=[
                pltpu.VMEM((len(early), TAG, width), bf16),
                pltpu.SMEM((len(early), plan.rows), jnp.int32),
                pltpu.SemaphoreType.DMA((len(early),)),
                pltpu.SemaphoreType.DMA((len(early), plan.first)),
            ],
            compiler_params=params(),
            cost_estimate=COST,
            name="place_early",
        )(*[first[o] for o in early])
        held, sets = [out], [sets]

    def place(held, messages, name):
        def body(*refs):
            refs = list(refs)[len(held) :]
            sets_ref = refs.pop(0) if sets else None
            count = len(messages)
            place_late_kernel(plan, messages, early, sets_ref, refs[:count], *refs[count:])

        return [
            pl.pallas_call(
                body,
                out_shape=out_shape,
                in_specs=[HBM] * len(held) + [SMEM] * len(sets) + [ANY] * len(messages),
                out_specs=HBM,
                input_output_aliases={0: 0} if held else {},
                scratch_shapes=[
                    pltpu.SMEM((len(messages), plan.rows), jnp.int32),
                    pltpu.SemaphoreType.DMA((len(messages), plan.rows)),
                ],
                compiler_params=params(),
                cost_estimate=COST,
                name=name,
            )(*held, *sets, *[arrived[m] for m in messages])
        ]

    last = [late(4), late(6, 0), late(6, 1)]
    held = place(held, [m for m in plan.late if m not in last], "place_mid")
    held = place(held, last, "place_last")
    return held[0][None]


def solution(mesh):
    return jax.shard_map(
        local,
        mesh=mesh,
        in_specs=(
            P("front", "wide", None),
            P("front", "wide", None),
            P("front", "wide", None),
            P("front", "wide"),
            P("front", "wide", None),
            P("front", "wide", None),
        ),
        out_specs=P("front", "wide", None),
        check_vma=False,
    )
```

```python
import functools

import jax
import jax.numpy as jnp
from jax import lax
from jax.experimental import pallas as pl
from jax.experimental.pallas import tpu as pltpu
from jax.sharding import PartitionSpec as P

GRID_COLS = 8
NEAR = GRID_COLS // 2
FAR = (5, 4, 7, 6)
TAG = 8

ANY = pl.BlockSpec(memory_space=pl.ANY)
HBM = pl.BlockSpec(memory_space=pltpu.HBM)
SMEM = pl.BlockSpec(memory_space=pltpu.SMEM)
VMEM = pl.BlockSpec(memory_space=pltpu.VMEM)


class Plan:
    def __init__(self, updates, panels, slot_cols):
        self.groups = lax.axis_size("front")
        self.lanes = lax.axis_size("wide")
        self.grid_rows = self.lanes // GRID_COLS
        self.slots = slot_cols.shape[1]
        self.columns = slot_cols.shape[2]
        self.block = updates.shape[1] // self.slots
        self.rows = panels.shape[1] // self.block
        self.window = panels.shape[2] // self.block
        self.col_groups = self.window // GRID_COLS
        self.width = self.col_groups * self.block
        self.capacity = max(self.slots // 4, self.slots // self.groups)
        self.first = max(0, self.rows - self.capacity * self.groups)
        self.early = {5: self.first, 7: self.first, 4: self.first // 2, 6: 0}
        half = self.rows // 2
        self.late = [(o, 0, self.rows) for o in range(NEAR - 1)]
        self.late += [(NEAR - 1, 0, half), (NEAR - 1, half, self.rows)]
        for o in FAR:
            count = self.rows - self.early[o]
            self.late.append((o, 0, count))


COST = pl.CostEstimate(flops=0, transcendentals=0, bytes_accessed=0)


def params():
    return pltpu.CompilerParams(vmem_limit_bytes=48 << 20)


def at(start, size):
    return pl.ds(pl.multiple_of(start * size, size), size)


def parent_of(plan, heads, q):
    return heads[q] // plan.rows


def row_of(plan, heads, q):
    return heads[q] % plan.rows


def touched_rows(plan, head_refs):
    me = lax.axis_index("front")
    touched = jnp.int32(0)
    for heads in head_refs:
        for q in range(plan.slots):
            bit = jnp.left_shift(jnp.int32(1), row_of(plan, heads, q))
            touched = touched | jnp.where(parent_of(plan, heads, q) == me, bit, 0)
    return touched


def first_rows(plan, touched, limit):
    chosen, count = jnp.int32(0), jnp.int32(0)
    for t in range(plan.rows):
        free = (jnp.right_shift(touched, t) & 1) == 0
        take = jnp.logical_and(free, count < limit)
        chosen = chosen | jnp.where(take, 1 << t, 0)
        count = count + jnp.where(take, 1, 0)
    return chosen


def positions(plan, chosen):
    out, count = [], jnp.int32(0)
    for t in range(plan.rows):
        bit = jnp.right_shift(chosen, t) & 1
        out.append((bit, jnp.where(bit == 1, count, t - count)))
        count = count + bit
    return out


def list_rows(plan, chosen, bit_wanted, where):
    for t, (bit, place) in enumerate(positions(plan, chosen)):

        @pl.when(bit == bit_wanted)
        def _():
            where[place] = t


def run_all(copies):
    for copy in copies:
        copy.start()
    for copy in copies:
        copy.wait()


def bucket_kernel(plan, heads, updates, *refs):
    outs, done, sems = refs[:-2], refs[-2], refs[-1]
    done[0] = 0
    me = lax.axis_index("front")

    def copies(act):
        for k in range(1, plan.groups):
            target = lax.rem(me + k, plan.groups)
            rank = jnp.int32(0)
            for q in range(plan.slots):
                named = parent_of(plan, heads, q) == target

                @pl.when(named)
                def _():
                    act(
                        pltpu.make_async_copy(
                            updates.at[0, pl.ds(q * plan.block, plan.block)],
                            outs[k - 1].at[rank],
                            sems.at[q],
                        )
                    )

                rank = rank + jnp.where(named, 1, 0)

    copies(lambda c: c.start())
    copies(lambda c: c.wait())


def pack_kernel(plan, offsets, *refs):
    groups = plan.groups
    head_refs, panel, refs = refs[:groups], refs[groups + 1], refs[groups + 2 :]
    outs, refs = refs[: len(offsets)], refs[len(offsets) :]
    touched_out, order, sems = refs
    column = lax.axis_index("wide") // plan.grid_rows
    block = plan.block
    touched = touched_rows(plan, head_refs)
    touched_out[0] = touched
    list_rows(plan, first_rows(plan, touched, plan.first), 1, order)
    copies = []
    for i, o in enumerate(offsets):
        target = jnp.bitwise_xor(column, o)
        for k in range(plan.early[o]):
            for cc in range(plan.col_groups):
                copies.append(
                    pltpu.make_async_copy(
                        panel.at[0, at(order[k], block), at(cc * GRID_COLS + target, block)],
                        outs[i].at[pl.ds(k * block, block), pl.ds(cc * block, block)],
                        sems.at[i, k, cc],
                    )
                )
                copies[-1].start()
    for i, o in enumerate(offsets):
        chosen = first_rows(plan, touched, plan.early[o]).astype(jnp.float32)
        tag = jnp.full((TAG, plan.width), chosen, jnp.float32).astype(jnp.bfloat16)
        outs[i][plan.early[o] * block :, :] = tag
    for copy in copies:
        copy.wait()


def assemble_kernel(plan, *refs):
    groups, block = plan.groups, plan.block
    head_refs, refs = refs[:groups], refs[groups:]
    code_refs, refs = refs[:groups], refs[groups:]
    panel, updates, refs = refs[0], refs[1], refs[2:]
    got, refs = refs[: groups - 1], refs[groups - 1 :]
    outs, refs = refs[: len(plan.late)], refs[len(plan.late) :]
    total, raw, moved, place_ref, row_sems, slot_sems = refs
    me = lax.axis_index("front")
    column = lax.axis_index("wide") // plan.grid_rows

    slot_copies = [
        pltpu.make_async_copy(
            updates.at[0, pl.ds(q * block, block)], moved.at[q], slot_sems.at[q]
        )
        for q in range(plan.slots)
    ]
    for k in range(1, groups):
        for c in range(plan.capacity):
            index = plan.slots + (k - 1) * plan.capacity + c
            slot_copies.append(
                pltpu.make_async_copy(got[k - 1].at[c], moved.at[index], slot_sems.at[index])
            )
    row_copies = [
        pltpu.make_async_copy(panel.at[0, pl.ds(t * block, block)], raw.at[t], row_sems.at[t])
        for t in range(plan.rows)
    ]
    for copy in row_copies + slot_copies:
        copy.start()

    touched = touched_rows(plan, head_refs)
    for o in FAR:
        for t, (bit, place) in enumerate(
            positions(plan, first_rows(plan, touched, plan.early[o]))
        ):
            place_ref[o, t] = jnp.where(bit == 1, -1, place)

    for t in range(plan.rows):
        row_copies[t].wait()
    for copy in slot_copies:
        copy.wait()

    def widen(t, carry):
        total[t] = raw[t].astype(jnp.float32)
        return carry

    lax.fori_loop(0, plan.rows, widen, 0)

    for s, (heads, codes) in enumerate(zip(head_refs, code_refs)):

        def add_slot(q, rank):
            named = parent_of(plan, heads, q) == me
            index = q if s == 0 else plan.slots + (s - 1) * plan.capacity + rank
            t = row_of(plan, heads, q)

            @pl.when(named)
            def _():
                for j in range(plan.columns):
                    code = codes[q, j]
                    col = code % plan.window

                    @pl.when(code >= plan.window)
                    def _():
                        where = at(col, block)
                        total[t, :, where] += moved[
                            index, :, pl.ds(j * block, block)
                        ].astype(jnp.float32)

            return rank + jnp.where(named, 1, 0)

        lax.fori_loop(0, plan.slots, add_slot, jnp.int32(0))

    def pack(t, carry):
        for ref, (o, lo, hi) in zip(outs, plan.late):
            target = jnp.bitwise_xor(column, o)

            def put(row):
                for cc in range(plan.col_groups):
                    ref[at(row, block), pl.ds(cc * block, block)] = total[
                        t, :, at(cc * GRID_COLS + target, block)
                    ].astype(jnp.bfloat16)

            if hi - lo == plan.rows:
                put(t)
            else:
                place = place_ref[o, t] if plan.early.get(o) else t
                pl.when(jnp.logical_and(place >= lo, place < hi))(lambda: put(place - lo))

        return carry

    lax.fori_loop(0, plan.rows, pack, 0)


def place_early_kernel(plan, offsets, *refs):
    count = len(offsets)
    pieces, out, sets, refs = refs[:count], refs[count], refs[count + 1], refs[count + 2 :]
    tags, where, tag_sems, sems = refs
    column = lax.axis_index("wide") // plan.grid_rows
    block = plan.block
    run_all(
        [
            pltpu.make_async_copy(
                pieces[i].at[pl.ds(plan.early[o] * block, TAG)], tags.at[i], tag_sems.at[i]
            )
            for i, o in enumerate(offsets)
        ]
    )
    copies = []
    for i, o in enumerate(offsets):
        source = jnp.bitwise_xor(column, o)
        chosen = jnp.max(tags[i].astype(jnp.float32)).astype(jnp.int32)
        sets[i] = chosen
        list_rows(plan, chosen, 1, where.at[i])
        for k in range(plan.early[o]):
            copies.append(
                pltpu.make_async_copy(
                    pieces[i].at[pl.ds(k * block, block)],
                    out.at[at(where[i, k] * GRID_COLS + source, block)],
                    sems.at[i, k],
                )
            )
            copies[-1].start()
    for copy in copies:
        copy.wait()


def place_late_kernel(plan, messages, early, sets, pieces, out, where, sems):
    column = lax.axis_index("wide") // plan.grid_rows
    block = plan.block
    copies = []
    for i, (o, lo, hi) in enumerate(messages):
        source = jnp.bitwise_xor(column, o)
        split = o in early
        if split:
            list_rows(plan, sets[early.index(o)], 0, where.at[i])
        for k in range(lo, hi):
            t = where[i, k] if split else k
            copies.append(
                pltpu.make_async_copy(
                    pieces[i].at[pl.ds((k - lo) * block, block)],
                    out.at[at(t * GRID_COLS + source, block)],
                    sems.at[i, k],
                )
            )
            copies[-1].start()
    for copy in copies:
        copy.wait()


def after(value, *others):
    return lax.optimization_barrier((value, *others))[0]


def across(value, plan, offset):
    pairs = [
        (c * plan.grid_rows + r, (c ^ offset) * plan.grid_rows + r)
        for c in range(GRID_COLS)
        for r in range(plan.grid_rows)
    ]
    return lax.ppermute(value, "wide", pairs)


def along(value, plan, steps):
    return lax.ppermute(
        value, "front", [(f, (f + steps) % plan.groups) for f in range(plan.groups)]
    )


def local(updates, parent_panels, slot_parent, slot_row, slot_cols, slot_mask):
    plan = Plan(updates, parent_panels, slot_cols)
    block, width = plan.block, plan.width
    bf16 = jnp.bfloat16
    heads = slot_parent[0, :, 0] * plan.rows + slot_row[0]
    all_heads = [heads] + [along(heads, plan, k) for k in range(1, plan.groups)]
    codes = slot_mask[0] * plan.window + slot_cols[0]
    panels = pltpu.with_memory_space_constraint(parent_panels, pltpu.HBM)


    *buckets, done = pl.pallas_call(
        functools.partial(bucket_kernel, plan),
        out_shape=[
            jax.ShapeDtypeStruct((plan.capacity, block, updates.shape[2]), bf16)
            for _ in range(1, plan.groups)
        ]
        + [jax.ShapeDtypeStruct((1,), jnp.int32)],
        in_specs=[SMEM, HBM],
        out_specs=[VMEM] * (plan.groups - 1) + [SMEM],
        scratch_shapes=[pltpu.SemaphoreType.DMA((plan.slots,))],
        compiler_params=params(),
        cost_estimate=COST,
        name="bucket",
    )(heads, updates)

    early = [o for o in FAR if plan.early[o]]
    packed, touched = {}, []
    if early:
        *outs, touched_set = pl.pallas_call(
            functools.partial(pack_kernel, plan, early),
            out_shape=[
                jax.ShapeDtypeStruct((plan.early[o] * block + TAG, width), bf16) for o in early
            ]
            + [jax.ShapeDtypeStruct((1,), jnp.int32)],
            in_specs=[SMEM] * (plan.groups + 1) + [HBM],
            out_specs=[VMEM] * len(early) + [SMEM],
            scratch_shapes=[
                pltpu.SMEM((plan.rows,), jnp.int32),
                pltpu.SemaphoreType.DMA((len(early), plan.first, plan.col_groups)),
            ],
            compiler_params=params(),
            cost_estimate=COST,
            name="pack_early",
        )(*all_heads, done, panels)
        packed = dict(zip(early, outs))
        touched = [touched_set]
        codes = after(codes, touched_set)
        buckets = [after(x, touched_set) for x in buckets]

    all_codes = [codes] + [along(codes, plan, k) for k in range(1, plan.groups)]
    got = [along(buckets[k - 1], plan, k) for k in range(1, plan.groups)]

    moved = plan.slots + (plan.groups - 1) * plan.capacity
    assembled = pl.pallas_call(
        functools.partial(assemble_kernel, plan),
        out_shape=[
            jax.ShapeDtypeStruct(((hi - lo) * block, width), bf16) for o, lo, hi in plan.late
        ],
        in_specs=[SMEM] * (2 * plan.groups) + [HBM, HBM] + [ANY] * (plan.groups - 1),
        out_specs=[VMEM] * len(plan.late),
        scratch_shapes=[
            pltpu.VMEM((plan.rows, block, parent_panels.shape[2]), jnp.float32),
            pltpu.VMEM((plan.rows, block, parent_panels.shape[2]), bf16),
            pltpu.VMEM((moved, block, updates.shape[2]), bf16),
            pltpu.SMEM((GRID_COLS, plan.rows), jnp.int32),
            pltpu.SemaphoreType.DMA((plan.rows,)),
            pltpu.SemaphoreType.DMA((moved,)),
        ],
        compiler_params=params(),
        cost_estimate=COST,
        name="assemble",
    )(*all_heads, *all_codes, panels, updates, *got)

    ready = dict(zip(plan.late, assembled))

    def late(o, part=0):
        return [m for m in plan.late if m[0] == o][part]

    first = {}
    for o in early:
        lead = [first[4]] if o == 7 else []
        first[o] = across(after(packed[o], *lead), plan, o)
    arrived = {late(0): ready[late(0)]}

    def send(message, *others):
        arrived[message] = across(after(ready[message], *others), plan, message[0])
        return arrived[message]

    b5 = send(late(5), *[first[o] for o in early if o == 5])
    b7 = send(late(7), *[first[o] for o in early if o == 7])
    send(late(6), b5)
    send(late(4), b7)
    n1 = send(late(1), *[first[o] for o in early if o == 5])
    send(late(2), *[first[o] for o in early if o == 7])
    send(late(3, 0), n1)
    send(late(3, 1), b7)

    out_shape = jax.ShapeDtypeStruct((plan.rows * GRID_COLS * block, width), bf16)
    held, sets = [], []
    if early:
        out, sets = pl.pallas_call(
            functools.partial(place_early_kernel, plan, early),
            out_shape=[out_shape, jax.ShapeDtypeStruct((len(early),), jnp.int32)],
            in_specs=[ANY] * len(early),
            out_specs=[HBM, SMEM],
            scratch_shapes=[
                pltpu.VMEM((len(early), TAG, width), bf16),
                pltpu.SMEM((len(early), plan.rows), jnp.int32),
                pltpu.SemaphoreType.DMA((len(early),)),
                pltpu.SemaphoreType.DMA((len(early), plan.first)),
            ],
            compiler_params=params(),
            cost_estimate=COST,
            name="place_early",
        )(*[first[o] for o in early])
        held, sets = [out], [sets]

    def place(held, messages, name):
        def body(*refs):
            refs = list(refs)[len(held) :]
            sets_ref = refs.pop(0) if sets else None
            count = len(messages)
            place_late_kernel(plan, messages, early, sets_ref, refs[:count], *refs[count:])

        return [
            pl.pallas_call(
                body,
                out_shape=out_shape,
                in_specs=[HBM] * len(held) + [SMEM] * len(sets) + [ANY] * len(messages),
                out_specs=HBM,
                input_output_aliases={0: 0} if held else {},
                scratch_shapes=[
                    pltpu.SMEM((len(messages), plan.rows), jnp.int32),
                    pltpu.SemaphoreType.DMA((len(messages), plan.rows)),
                ],
                compiler_params=params(),
                cost_estimate=COST,
                name=name,
            )(*held, *sets, *[arrived[m] for m in messages])
        ]

    last = [late(4), late(6)]
    held = place(held, [m for m in plan.late if m not in last], "place_mid")
    held = place(held, last, "place_last")
    return held[0][None]


def solution(mesh):
    return jax.shard_map(
        local,
        mesh=mesh,
        in_specs=(
            P("front", "wide", None),
            P("front", "wide", None),
            P("front", "wide", None),
            P("front", "wide"),
            P("front", "wide", None),
            P("front", "wide", None),
        ),
        out_specs=P("front", "wide", None),
        check_vma=False,
    )
```

```python
import functools

import jax
import jax.numpy as jnp
from jax import lax
from jax.experimental import pallas as pl
from jax.experimental.pallas import tpu as pltpu
from jax.sharding import PartitionSpec as P

GRID_COLS = 8
NEAR = GRID_COLS // 2
FAR = (5, 4, 7, 6)
TAG = 8

ANY = pl.BlockSpec(memory_space=pl.ANY)
HBM = pl.BlockSpec(memory_space=pltpu.HBM)
SMEM = pl.BlockSpec(memory_space=pltpu.SMEM)
VMEM = pl.BlockSpec(memory_space=pltpu.VMEM)


class Plan:
    def __init__(self, updates, panels, slot_cols):
        self.groups = lax.axis_size("front")
        self.lanes = lax.axis_size("wide")
        self.grid_rows = self.lanes // GRID_COLS
        self.slots = slot_cols.shape[1]
        self.columns = slot_cols.shape[2]
        self.block = updates.shape[1] // self.slots
        self.rows = panels.shape[1] // self.block
        self.window = panels.shape[2] // self.block
        self.col_groups = self.window // GRID_COLS
        self.width = self.col_groups * self.block
        self.capacity = max(self.slots // 4, self.slots // self.groups)
        self.first = max(0, self.rows - self.capacity * self.groups)
        self.early = {5: self.first, 7: self.first, 4: self.first // 2, 6: 0}
        half = max(1, 3 * self.rows // 8)
        self.late = [(o, 0, self.rows) for o in range(NEAR - 1)]
        self.late += [(NEAR - 1, 0, half), (NEAR - 1, half, self.rows)]
        for o in FAR:
            count = self.rows - self.early[o]
            self.late.append((o, 0, count))


MID = pl.CostEstimate(flops=0, transcendentals=0, bytes_accessed=0)
COST = pl.CostEstimate(flops=0, transcendentals=0, bytes_accessed=0)


def params():
    return pltpu.CompilerParams(vmem_limit_bytes=48 << 20)


def at(start, size):
    return pl.ds(pl.multiple_of(start * size, size), size)


def parent_of(plan, heads, q):
    return heads[q] // plan.rows


def row_of(plan, heads, q):
    return heads[q] % plan.rows


def touched_rows(plan, head_refs):
    me = lax.axis_index("front")
    touched = jnp.int32(0)
    for heads in head_refs:
        for q in range(plan.slots):
            bit = jnp.left_shift(jnp.int32(1), row_of(plan, heads, q))
            touched = touched | jnp.where(parent_of(plan, heads, q) == me, bit, 0)
    return touched


def first_rows(plan, touched, limit):
    chosen, count = jnp.int32(0), jnp.int32(0)
    for t in range(plan.rows):
        free = (jnp.right_shift(touched, t) & 1) == 0
        take = jnp.logical_and(free, count < limit)
        chosen = chosen | jnp.where(take, 1 << t, 0)
        count = count + jnp.where(take, 1, 0)
    return chosen


def positions(plan, chosen):
    out, count = [], jnp.int32(0)
    for t in range(plan.rows):
        bit = jnp.right_shift(chosen, t) & 1
        out.append((bit, jnp.where(bit == 1, count, t - count)))
        count = count + bit
    return out


def list_rows(plan, chosen, bit_wanted, where):
    for t, (bit, place) in enumerate(positions(plan, chosen)):

        @pl.when(bit == bit_wanted)
        def _():
            where[place] = t


def run_all(copies):
    for copy in copies:
        copy.start()
    for copy in copies:
        copy.wait()


def stage_kernel(plan, early, heads, updates, panel, *refs):
    outs, refs = refs[: plan.groups - 1], refs[plan.groups - 1 :]
    staged, (slot_sems, sems) = refs[: len(early)], refs[len(early) :]
    me = lax.axis_index("front")
    column = lax.axis_index("wide") // plan.grid_rows
    block = plan.block

    def buckets(act):
        for k in range(1, plan.groups):
            target = lax.rem(me + k, plan.groups)
            rank = jnp.int32(0)
            for q in range(plan.slots):
                named = parent_of(plan, heads, q) == target

                @pl.when(named)
                def _():
                    act(
                        pltpu.make_async_copy(
                            updates.at[0, pl.ds(q * block, block)],
                            outs[k - 1].at[rank],
                            slot_sems.at[q],
                        )
                    )

                rank = rank + jnp.where(named, 1, 0)

    buckets(lambda c: c.start())
    run_all(
        [
            pltpu.make_async_copy(
                panel.at[0, :, at(cc * GRID_COLS + jnp.bitwise_xor(column, o), block)],
                staged[i].at[:, pl.ds(cc * block, block)],
                sems.at[i, cc],
            )
            for i, o in enumerate(early)
            for cc in range(plan.col_groups)
        ]
    )
    buckets(lambda c: c.wait())


def pack_kernel(plan, offsets, *refs):
    groups, count = plan.groups, len(offsets)
    head_refs, staged, refs = refs[:groups], refs[groups : groups + count], refs[groups + count :]
    outs, (touched_out, order) = refs[:count], refs[count:]
    block = plan.block
    touched = touched_rows(plan, head_refs)
    touched_out[0] = touched
    list_rows(plan, first_rows(plan, touched, plan.first), 1, order)
    for i, o in enumerate(offsets):
        for k in range(plan.early[o]):
            outs[i][pl.ds(k * block, block), :] = staged[i][at(order[k], block), :]
        chosen = first_rows(plan, touched, plan.early[o]).astype(jnp.float32)
        tag = jnp.full((TAG, plan.width), chosen, jnp.float32).astype(jnp.bfloat16)
        outs[i][plan.early[o] * block :, :] = tag


def assemble_kernel(plan, *refs):
    groups, block = plan.groups, plan.block
    head_refs, refs = refs[:groups], refs[groups:]
    code_refs, refs = refs[:groups], refs[groups:]
    panel, updates, refs = refs[0], refs[1], refs[2:]
    got, refs = refs[: groups - 1], refs[groups - 1 :]
    outs, refs = refs[: len(plan.late)], refs[len(plan.late) :]
    total, raw, moved, place_ref, row_sems, slot_sems = refs
    me = lax.axis_index("front")
    column = lax.axis_index("wide") // plan.grid_rows

    slot_copies = [
        pltpu.make_async_copy(
            updates.at[0, pl.ds(q * block, block)], moved.at[q], slot_sems.at[q]
        )
        for q in range(plan.slots)
    ]
    for k in range(1, groups):
        for c in range(plan.capacity):
            index = plan.slots + (k - 1) * plan.capacity + c
            slot_copies.append(
                pltpu.make_async_copy(got[k - 1].at[c], moved.at[index], slot_sems.at[index])
            )
    row_copies = [
        pltpu.make_async_copy(panel.at[0, pl.ds(t * block, block)], raw.at[t], row_sems.at[t])
        for t in range(plan.rows)
    ]
    for copy in row_copies + slot_copies:
        copy.start()

    touched = touched_rows(plan, head_refs)
    for o in FAR:
        for t, (bit, place) in enumerate(
            positions(plan, first_rows(plan, touched, plan.early[o]))
        ):
            place_ref[o, t] = jnp.where(bit == 1, -1, place)

    for t in range(plan.rows):
        row_copies[t].wait()
    for copy in slot_copies:
        copy.wait()

    def widen(t, carry):
        total[t] = raw[t].astype(jnp.float32)
        return carry

    lax.fori_loop(0, plan.rows, widen, 0)

    for s, (heads, codes) in enumerate(zip(head_refs, code_refs)):

        def add_slot(q, rank):
            named = parent_of(plan, heads, q) == me
            index = q if s == 0 else plan.slots + (s - 1) * plan.capacity + rank
            t = row_of(plan, heads, q)

            @pl.when(named)
            def _():
                for j in range(plan.columns):
                    code = codes[q, j]
                    col = code % plan.window

                    @pl.when(code >= plan.window)
                    def _():
                        where = at(col, block)
                        total[t, :, where] += moved[
                            index, :, pl.ds(j * block, block)
                        ].astype(jnp.float32)

            return rank + jnp.where(named, 1, 0)

        lax.fori_loop(0, plan.slots, add_slot, jnp.int32(0))

    def pack(t, carry):
        for ref, (o, lo, hi) in zip(outs, plan.late):
            target = jnp.bitwise_xor(column, o)

            def put(row):
                for cc in range(plan.col_groups):
                    ref[at(row, block), pl.ds(cc * block, block)] = total[
                        t, :, at(cc * GRID_COLS + target, block)
                    ].astype(jnp.bfloat16)

            if hi - lo == plan.rows:
                put(t)
            else:
                place = place_ref[o, t] if plan.early.get(o) else t
                pl.when(jnp.logical_and(place >= lo, place < hi))(lambda: put(place - lo))

        return carry

    lax.fori_loop(0, plan.rows, pack, 0)


def place_early_kernel(plan, offsets, *refs):
    count = len(offsets)
    pieces, out, sets, refs = refs[:count], refs[count], refs[count + 1], refs[count + 2 :]
    tags, where, tag_sems, sems = refs
    column = lax.axis_index("wide") // plan.grid_rows
    block = plan.block
    run_all(
        [
            pltpu.make_async_copy(
                pieces[i].at[pl.ds(plan.early[o] * block, TAG)], tags.at[i], tag_sems.at[i]
            )
            for i, o in enumerate(offsets)
        ]
    )
    copies = []
    for i, o in enumerate(offsets):
        source = jnp.bitwise_xor(column, o)
        chosen = jnp.max(tags[i].astype(jnp.float32)).astype(jnp.int32)
        sets[i] = chosen
        list_rows(plan, chosen, 1, where.at[i])
        for k in range(plan.early[o]):
            copies.append(
                pltpu.make_async_copy(
                    pieces[i].at[pl.ds(k * block, block)],
                    out.at[at(where[i, k] * GRID_COLS + source, block)],
                    sems.at[i, k],
                )
            )
            copies[-1].start()
    for copy in copies:
        copy.wait()


def place_late_kernel(plan, messages, early, sets, pieces, out, held, where, set_sem, sems):
    column = lax.axis_index("wide") // plan.grid_rows
    block = plan.block
    copies = []

    def place(i, rows):
        o, lo, hi = messages[i]
        source = jnp.bitwise_xor(column, o)
        for k in range(lo, hi):
            copies.append(
                pltpu.make_async_copy(
                    pieces[i].at[pl.ds((k - lo) * block, block)],
                    out.at[at(rows[k] * GRID_COLS + source, block)],
                    sems.at[i, k],
                )
            )
            copies[-1].start()

    split = [i for i, m in enumerate(messages) if m[0] in early]
    if split:
        fetch = pltpu.make_async_copy(sets, held, set_sem)
        fetch.start()
    for i in range(len(messages)):
        if i not in split:
            place(i, range(plan.rows))
    if split:
        fetch.wait()
    for i in split:
        list_rows(plan, held[early.index(messages[i][0])], 0, where.at[i])
        place(i, where.at[i])
    for copy in copies:
        copy.wait()


def after(value, *others):
    return lax.optimization_barrier((value, *others))[0]


def across(value, plan, offset):
    pairs = [
        (c * plan.grid_rows + r, (c ^ offset) * plan.grid_rows + r)
        for c in range(GRID_COLS)
        for r in range(plan.grid_rows)
    ]
    return lax.ppermute(value, "wide", pairs)


def along(value, plan, steps):
    return lax.ppermute(
        value, "front", [(f, (f + steps) % plan.groups) for f in range(plan.groups)]
    )


def local(updates, parent_panels, slot_parent, slot_row, slot_cols, slot_mask):
    plan = Plan(updates, parent_panels, slot_cols)
    block, width = plan.block, plan.width
    bf16 = jnp.bfloat16
    heads = slot_parent[0, :, 0] * plan.rows + slot_row[0]
    all_heads = [heads] + [along(heads, plan, k) for k in range(1, plan.groups)]
    codes = slot_mask[0] * plan.window + slot_cols[0]
    panels = pltpu.with_memory_space_constraint(parent_panels, pltpu.HBM)
    moving = pltpu.with_memory_space_constraint(updates, pltpu.HBM)


    early = [o for o in FAR if plan.early[o]]
    staged = pl.pallas_call(
        functools.partial(stage_kernel, plan, early),
        out_shape=[
            jax.ShapeDtypeStruct((plan.capacity, block, updates.shape[2]), bf16)
            for _ in range(1, plan.groups)
        ]
        + [jax.ShapeDtypeStruct((plan.rows * block, width), bf16) for _ in early],
        in_specs=[SMEM, HBM, HBM],
        out_specs=[VMEM] * (plan.groups - 1 + len(early)),
        scratch_shapes=[
            pltpu.SemaphoreType.DMA((plan.slots,)),
            pltpu.SemaphoreType.DMA((max(1, len(early)), plan.col_groups)),
        ],
        compiler_params=params(),
        cost_estimate=COST,
        name="stage",
    )(heads, moving, panels)
    buckets, staged = staged[: plan.groups - 1], staged[plan.groups - 1 :]

    packed = {}
    if early:
        *outs, touched = pl.pallas_call(
            functools.partial(pack_kernel, plan, early),
            out_shape=[
                jax.ShapeDtypeStruct((plan.early[o] * block + TAG, width), bf16) for o in early
            ]
            + [jax.ShapeDtypeStruct((1,), jnp.int32)],
            in_specs=[SMEM] * plan.groups + [VMEM] * len(early),
            out_specs=[VMEM] * len(early) + [SMEM],
            scratch_shapes=[pltpu.SMEM((plan.rows,), jnp.int32)],
            compiler_params=params(),
            cost_estimate=pl.CostEstimate(flops=0, transcendentals=0, bytes_accessed=0),
            name="pack_early",
        )(*all_heads, *staged)
        packed = dict(zip(early, outs))

    all_codes = [codes] + [along(codes, plan, k) for k in range(1, plan.groups)]
    buckets = [after(x, *all_heads, *all_codes) for x in buckets]
    got = [along(buckets[k - 1], plan, k) for k in range(1, plan.groups)]

    moved = plan.slots + (plan.groups - 1) * plan.capacity
    assembled = pl.pallas_call(
        functools.partial(assemble_kernel, plan),
        out_shape=[
            jax.ShapeDtypeStruct(((hi - lo) * block, width), bf16) for o, lo, hi in plan.late
        ],
        in_specs=[SMEM] * (2 * plan.groups) + [HBM, HBM] + [ANY] * (plan.groups - 1),
        out_specs=[VMEM] * len(plan.late),
        scratch_shapes=[
            pltpu.VMEM((plan.rows, block, parent_panels.shape[2]), jnp.float32),
            pltpu.VMEM((plan.rows, block, parent_panels.shape[2]), bf16),
            pltpu.VMEM((moved, block, updates.shape[2]), bf16),
            pltpu.SMEM((GRID_COLS, plan.rows), jnp.int32),
            pltpu.SemaphoreType.DMA((plan.rows,)),
            pltpu.SemaphoreType.DMA((moved,)),
        ],
        compiler_params=params(),
        cost_estimate=COST,
        name="assemble",
    )(*all_heads, *all_codes, panels, moving, *got)

    ready = dict(zip(plan.late, assembled))

    def late(o, part=0):
        return [m for m in plan.late if m[0] == o][part]

    first = {}
    for o in early:
        lead = [first[4]] if o == 7 else []
        first[o] = across(after(packed[o], *lead), plan, o)
    arrived = {late(0): ready[late(0)]}

    def send(message, *others):
        arrived[message] = across(after(ready[message], *others), plan, message[0])
        return arrived[message]

    b5 = send(late(5), *[first[o] for o in early if o == 5])
    b7 = send(late(7), *[first[o] for o in early if o == 7])
    send(late(6), b5)
    send(late(4), b7)
    n2 = send(late(2))
    send(late(3, 1), n2)
    n3 = send(late(3, 0), *[first[o] for o in early if o == 5])
    send(late(1), n3)

    out_shape = jax.ShapeDtypeStruct((plan.rows * GRID_COLS * block, width), bf16)
    held, sets = [], []
    if early:
        out, sets = pl.pallas_call(
            functools.partial(place_early_kernel, plan, early),
            out_shape=[out_shape, jax.ShapeDtypeStruct((len(early),), jnp.int32)],
            in_specs=[ANY] * len(early),
            out_specs=[HBM, SMEM],
            scratch_shapes=[
                pltpu.VMEM((len(early), TAG, width), bf16),
                pltpu.SMEM((len(early), plan.rows), jnp.int32),
                pltpu.SemaphoreType.DMA((len(early),)),
                pltpu.SemaphoreType.DMA((len(early), plan.first)),
            ],
            compiler_params=params(),
            cost_estimate=COST,
            name="place_early",
        )(*[first[o] for o in early])
        held, sets = [out], [sets]

    def place(held, messages, name):
        def body(*refs):
            refs = list(refs)[len(held) :]
            sets_ref = refs.pop(0) if sets else None
            count = len(messages)
            place_late_kernel(plan, messages, early, sets_ref, refs[:count], *refs[count:])

        return [
            pl.pallas_call(
                body,
                out_shape=out_shape,
                in_specs=[HBM] * len(held) + [ANY] * (len(sets) + len(messages)),
                out_specs=HBM,
                input_output_aliases={0: 0} if held else {},
                scratch_shapes=[
                    pltpu.SMEM((max(1, len(early)),), jnp.int32),
                    pltpu.SMEM((len(messages), plan.rows), jnp.int32),
                    pltpu.SemaphoreType.DMA,
                    pltpu.SemaphoreType.DMA((len(messages), plan.rows)),
                ],
                compiler_params=params(),
                cost_estimate=MID if name == "place_mid" else COST,
                name=name,
            )(*held, *sets, *[arrived[m] for m in messages])
        ]

    last = [late(4), late(6)]
    held = place(held, [m for m in plan.late if m not in last], "place_mid")
    held = place(held, last, "place_last")
    return held[0][None]


def solution(mesh):
    return jax.shard_map(
        local,
        mesh=mesh,
        in_specs=(
            P("front", "wide", None),
            P("front", "wide", None),
            P("front", "wide", None),
            P("front", "wide"),
            P("front", "wide", None),
            P("front", "wide", None),
        ),
        out_specs=P("front", "wide", None),
        check_vma=False,
    )
```

```python
import functools

import jax
import jax.numpy as jnp
from jax import lax
from jax.experimental import pallas as pl
from jax.experimental.pallas import tpu as pltpu
from jax.sharding import PartitionSpec as P

GRID_COLS = 8
NEAR = GRID_COLS // 2
TAG = 8

ANY = pl.BlockSpec(memory_space=pl.ANY)
HBM = pl.BlockSpec(memory_space=pltpu.HBM)
SMEM = pl.BlockSpec(memory_space=pltpu.SMEM)
VMEM = pl.BlockSpec(memory_space=pltpu.VMEM)


class Plan:
    def __init__(self, updates, panels, slot_cols):
        self.groups = lax.axis_size("front")
        self.lanes = lax.axis_size("wide")
        self.grid_rows = self.lanes // GRID_COLS
        self.slots = slot_cols.shape[1]
        self.columns = slot_cols.shape[2]
        self.block = updates.shape[1] // self.slots
        self.rows = panels.shape[1] // self.block
        self.window = panels.shape[2] // self.block
        self.col_groups = self.window // GRID_COLS
        self.width = self.col_groups * self.block
        self.capacity = max(self.slots // 4, self.slots // self.groups)
        self.first = max(0, self.rows - self.capacity * self.groups)
        self.early = {4: self.first // 2, 5: self.first, 7: self.first, 2: self.first}
        self.late = []
        for o in range(GRID_COLS):
            count = self.rows - self.early.get(o, 0)
            cuts = [0, count // 2, count] if o == 4 else [0, max(1, 5 * count // 8), count] if o == 6 else [0, count]
            self.late += [(o, lo, hi) for lo, hi in zip(cuts, cuts[1:]) if lo < hi]


MID = pl.CostEstimate(flops=0, transcendentals=0, bytes_accessed=0)
COST = pl.CostEstimate(flops=0, transcendentals=0, bytes_accessed=0)


def params():
    return pltpu.CompilerParams(vmem_limit_bytes=48 << 20)


def at(start, size):
    return pl.ds(pl.multiple_of(start * size, size), size)


def parent_of(plan, heads, q):
    return heads[q] // plan.rows


def row_of(plan, heads, q):
    return heads[q] % plan.rows


def touched_rows(plan, head_refs):
    me = lax.axis_index("front")
    touched = jnp.int32(0)
    for heads in head_refs:
        for q in range(plan.slots):
            bit = jnp.left_shift(jnp.int32(1), row_of(plan, heads, q))
            touched = touched | jnp.where(parent_of(plan, heads, q) == me, bit, 0)
    return touched


def first_rows(plan, touched, limit):
    chosen, count = jnp.int32(0), jnp.int32(0)
    for t in range(plan.rows):
        free = (jnp.right_shift(touched, t) & 1) == 0
        take = jnp.logical_and(free, count < limit)
        chosen = chosen | jnp.where(take, 1 << t, 0)
        count = count + jnp.where(take, 1, 0)
    return chosen


def positions(plan, chosen):
    out, count = [], jnp.int32(0)
    for t in range(plan.rows):
        bit = jnp.right_shift(chosen, t) & 1
        out.append((bit, jnp.where(bit == 1, count, t - count)))
        count = count + bit
    return out


def list_rows(plan, chosen, bit_wanted, where):
    for t, (bit, place) in enumerate(positions(plan, chosen)):

        @pl.when(bit == bit_wanted)
        def _():
            where[place] = t


def run_all(copies):
    for copy in copies:
        copy.start()
    for copy in copies:
        copy.wait()


def stage_kernel(plan, early, heads, updates, panel, *refs):
    outs, refs = refs[: plan.groups - 1], refs[plan.groups - 1 :]
    staged, (slot_sems, sems) = refs[: len(early)], refs[len(early) :]
    me = lax.axis_index("front")
    column = lax.axis_index("wide") // plan.grid_rows
    block = plan.block

    def buckets(act):
        for k in range(1, plan.groups):
            target = lax.rem(me + k, plan.groups)
            rank = jnp.int32(0)
            for q in range(plan.slots):
                named = parent_of(plan, heads, q) == target

                @pl.when(named)
                def _():
                    act(
                        pltpu.make_async_copy(
                            updates.at[0, pl.ds(q * block, block)],
                            outs[k - 1].at[rank],
                            slot_sems.at[q],
                        )
                    )

                rank = rank + jnp.where(named, 1, 0)

    buckets(lambda c: c.start())
    run_all(
        [
            pltpu.make_async_copy(
                panel.at[0, :, at(cc * GRID_COLS + jnp.bitwise_xor(column, o), block)],
                staged[i].at[:, pl.ds(cc * block, block)],
                sems.at[i, cc],
            )
            for i, o in enumerate(early)
            for cc in range(plan.col_groups)
        ]
    )
    buckets(lambda c: c.wait())


def pack_kernel(plan, offsets, *refs):
    groups, count = plan.groups, len(offsets)
    head_refs, staged, refs = refs[:groups], refs[groups : groups + count], refs[groups + count :]
    outs, (touched_out, order) = refs[:count], refs[count:]
    block = plan.block
    touched = touched_rows(plan, head_refs)
    touched_out[0] = touched
    list_rows(plan, first_rows(plan, touched, plan.first), 1, order)
    for i, o in enumerate(offsets):
        for k in range(plan.early[o]):
            outs[i][pl.ds(k * block, block), :] = staged[i][at(order[k], block), :]
        chosen = first_rows(plan, touched, plan.early[o]).astype(jnp.float32)
        tag = jnp.full((TAG, plan.width), chosen, jnp.float32).astype(jnp.bfloat16)
        outs[i][plan.early[o] * block :, :] = tag


def assemble_kernel(plan, *refs):
    groups, block = plan.groups, plan.block
    head_refs, refs = refs[:groups], refs[groups:]
    code_refs, refs = refs[:groups], refs[groups:]
    panel, updates, refs = refs[0], refs[1], refs[2:]
    got, refs = refs[: groups - 1], refs[groups - 1 :]
    outs, refs = refs[: len(plan.late)], refs[len(plan.late) :]
    total, raw, moved, place_ref, row_sems, slot_sems = refs
    me = lax.axis_index("front")
    column = lax.axis_index("wide") // plan.grid_rows

    slot_copies = [
        pltpu.make_async_copy(
            updates.at[0, pl.ds(q * block, block)], moved.at[q], slot_sems.at[q]
        )
        for q in range(plan.slots)
    ]
    for k in range(1, groups):
        for c in range(plan.capacity):
            index = plan.slots + (k - 1) * plan.capacity + c
            slot_copies.append(
                pltpu.make_async_copy(got[k - 1].at[c], moved.at[index], slot_sems.at[index])
            )
    row_copies = [
        pltpu.make_async_copy(panel.at[0, pl.ds(t * block, block)], raw.at[t], row_sems.at[t])
        for t in range(plan.rows)
    ]
    for copy in row_copies + slot_copies:
        copy.start()

    touched = touched_rows(plan, head_refs)
    for o in plan.early:
        for t, (bit, place) in enumerate(
            positions(plan, first_rows(plan, touched, plan.early[o]))
        ):
            place_ref[o, t] = jnp.where(bit == 1, -1, place)

    for t in range(plan.rows):
        row_copies[t].wait()
    for copy in slot_copies:
        copy.wait()

    def widen(t, carry):
        total[t] = raw[t].astype(jnp.float32)
        return carry

    lax.fori_loop(0, plan.rows, widen, 0)

    for s, (heads, codes) in enumerate(zip(head_refs, code_refs)):

        def add_slot(q, rank):
            named = parent_of(plan, heads, q) == me
            index = q if s == 0 else plan.slots + (s - 1) * plan.capacity + rank
            t = row_of(plan, heads, q)

            @pl.when(named)
            def _():
                for j in range(plan.columns):
                    code = codes[q, j]
                    col = code % plan.window

                    @pl.when(code >= plan.window)
                    def _():
                        where = at(col, block)
                        total[t, :, where] += moved[
                            index, :, pl.ds(j * block, block)
                        ].astype(jnp.float32)

            return rank + jnp.where(named, 1, 0)

        lax.fori_loop(0, plan.slots, add_slot, jnp.int32(0))

    def pack(t, carry):
        for ref, (o, lo, hi) in zip(outs, plan.late):
            target = jnp.bitwise_xor(column, o)

            def put(row):
                for cc in range(plan.col_groups):
                    ref[at(row, block), pl.ds(cc * block, block)] = total[
                        t, :, at(cc * GRID_COLS + target, block)
                    ].astype(jnp.bfloat16)

            if hi - lo == plan.rows:
                put(t)
            else:
                place = place_ref[o, t] if plan.early.get(o) else t
                pl.when(jnp.logical_and(place >= lo, place < hi))(lambda: put(place - lo))

        return carry

    lax.fori_loop(0, plan.rows, pack, 0)


def place_early_kernel(plan, offsets, *refs):
    count = len(offsets)
    pieces, out, sets, refs = refs[:count], refs[count], refs[count + 1], refs[count + 2 :]
    tags, where, tag_sems, sems = refs
    column = lax.axis_index("wide") // plan.grid_rows
    block = plan.block
    run_all(
        [
            pltpu.make_async_copy(
                pieces[i].at[pl.ds(plan.early[o] * block, TAG)], tags.at[i], tag_sems.at[i]
            )
            for i, o in enumerate(offsets)
        ]
    )
    copies = []
    for i, o in enumerate(offsets):
        source = jnp.bitwise_xor(column, o)
        chosen = jnp.max(tags[i].astype(jnp.float32)).astype(jnp.int32)
        sets[i] = chosen
        list_rows(plan, chosen, 1, where.at[i])
        for k in range(plan.early[o]):
            copies.append(
                pltpu.make_async_copy(
                    pieces[i].at[pl.ds(k * block, block)],
                    out.at[at(where[i, k] * GRID_COLS + source, block)],
                    sems.at[i, k],
                )
            )
            copies[-1].start()
    for copy in copies:
        copy.wait()


def place_late_kernel(plan, messages, early, sets, pieces, out, held, where, set_sem, sems):
    column = lax.axis_index("wide") // plan.grid_rows
    block = plan.block
    copies = []

    def place(i, rows):
        o, lo, hi = messages[i]
        source = jnp.bitwise_xor(column, o)
        for k in range(lo, hi):
            copies.append(
                pltpu.make_async_copy(
                    pieces[i].at[pl.ds((k - lo) * block, block)],
                    out.at[at(rows[k] * GRID_COLS + source, block)],
                    sems.at[i, k],
                )
            )
            copies[-1].start()

    split = [i for i, m in enumerate(messages) if m[0] in early]
    if split:
        fetch = pltpu.make_async_copy(sets, held, set_sem)
        fetch.start()
    for i in range(len(messages)):
        if i not in split:
            place(i, range(plan.rows))
    if split:
        fetch.wait()
    for i in split:
        list_rows(plan, held[early.index(messages[i][0])], 0, where.at[i])
        place(i, where.at[i])
    for copy in copies:
        copy.wait()


def after(value, *others):
    return lax.optimization_barrier((value, *others))[0]


def across(value, plan, offset):
    pairs = [
        (c * plan.grid_rows + r, (c ^ offset) * plan.grid_rows + r)
        for c in range(GRID_COLS)
        for r in range(plan.grid_rows)
    ]
    return lax.ppermute(value, "wide", pairs)


def along(value, plan, steps):
    return lax.ppermute(
        value, "front", [(f, (f + steps) % plan.groups) for f in range(plan.groups)]
    )


def local(updates, parent_panels, slot_parent, slot_row, slot_cols, slot_mask):
    plan = Plan(updates, parent_panels, slot_cols)
    block, width = plan.block, plan.width
    bf16 = jnp.bfloat16
    heads = slot_parent[0, :, 0] * plan.rows + slot_row[0]
    all_heads = [heads] + [along(heads, plan, k) for k in range(1, plan.groups)]
    codes = slot_mask[0] * plan.window + slot_cols[0]
    panels = pltpu.with_memory_space_constraint(parent_panels, pltpu.HBM)
    moving = pltpu.with_memory_space_constraint(updates, pltpu.HBM)


    early = [o for o in plan.early if plan.early[o]]
    staged = pl.pallas_call(
        functools.partial(stage_kernel, plan, early),
        out_shape=[
            jax.ShapeDtypeStruct((plan.capacity, block, updates.shape[2]), bf16)
            for _ in range(1, plan.groups)
        ]
        + [jax.ShapeDtypeStruct((plan.rows * block, width), bf16) for _ in early],
        in_specs=[SMEM, HBM, HBM],
        out_specs=[VMEM] * (plan.groups - 1 + len(early)),
        scratch_shapes=[
            pltpu.SemaphoreType.DMA((plan.slots,)),
            pltpu.SemaphoreType.DMA((max(1, len(early)), plan.col_groups)),
        ],
        compiler_params=params(),
        cost_estimate=COST,
        name="stage",
    )(heads, moving, panels)
    buckets, staged = staged[: plan.groups - 1], staged[plan.groups - 1 :]

    packed = {}
    if early:
        *outs, touched = pl.pallas_call(
            functools.partial(pack_kernel, plan, early),
            out_shape=[
                jax.ShapeDtypeStruct((plan.early[o] * block + TAG, width), bf16) for o in early
            ]
            + [jax.ShapeDtypeStruct((1,), jnp.int32)],
            in_specs=[SMEM] * plan.groups + [VMEM] * len(early),
            out_specs=[VMEM] * len(early) + [SMEM],
            scratch_shapes=[pltpu.SMEM((plan.rows,), jnp.int32)],
            compiler_params=params(),
            cost_estimate=pl.CostEstimate(flops=0, transcendentals=0, bytes_accessed=0),
            name="pack_early",
        )(*all_heads, *staged)
        packed = dict(zip(early, outs))

    all_codes = [codes] + [along(codes, plan, k) for k in range(1, plan.groups)]
    buckets = [after(x, *all_heads) for x in buckets]
    got = [along(buckets[k - 1], plan, k) for k in range(1, plan.groups)]

    moved = plan.slots + (plan.groups - 1) * plan.capacity
    assembled = pl.pallas_call(
        functools.partial(assemble_kernel, plan),
        out_shape=[
            jax.ShapeDtypeStruct(((hi - lo) * block, width), bf16) for o, lo, hi in plan.late
        ],
        in_specs=[SMEM] * (2 * plan.groups) + [HBM, HBM] + [ANY] * (plan.groups - 1),
        out_specs=[VMEM] * len(plan.late),
        scratch_shapes=[
            pltpu.VMEM((plan.rows, block, parent_panels.shape[2]), jnp.float32),
            pltpu.VMEM((plan.rows, block, parent_panels.shape[2]), bf16),
            pltpu.VMEM((moved, block, updates.shape[2]), bf16),
            pltpu.SMEM((GRID_COLS, plan.rows), jnp.int32),
            pltpu.SemaphoreType.DMA((plan.rows,)),
            pltpu.SemaphoreType.DMA((moved,)),
        ],
        compiler_params=params(),
        cost_estimate=COST,
        name="assemble",
    )(*all_heads, *all_codes, panels, moving, *got)

    ready = dict(zip(plan.late, assembled))

    def late(o, part=0):
        return [m for m in plan.late if m[0] == o][part]

    arrived = {late(0): ready[late(0)]}

    def send(message, *others):
        arrived[message] = across(after(ready[message], *others), plan, message[0])
        return arrived[message]

    first = {}

    def send_early(o, *others):
        if o in packed:
            first[o] = across(after(packed[o], *others), plan, o)

    def came(*offsets):
        return [first[o] for o in offsets if o in first]

    send_early(4)
    send_early(5)
    send_early(2)
    send_early(7, *came(4), *all_codes[1:])
    b5 = send(late(5), *came(5))
    b7 = send(late(7), *came(7))
    b6 = send(late(6, 0), b5)
    send(late(6, 1), b7)
    n3 = send(late(3), *came(2))
    n1 = send(late(1), *came(7))
    b4 = send(late(4, 0), *came(5))
    send(late(4, 1), b4)
    send(late(2), b5)

    out_shape = jax.ShapeDtypeStruct((plan.rows * GRID_COLS * block, width), bf16)
    held, sets = [], []
    if early:
        out, sets = pl.pallas_call(
            functools.partial(place_early_kernel, plan, early),
            out_shape=[out_shape, jax.ShapeDtypeStruct((len(early),), jnp.int32)],
            in_specs=[ANY] * len(early),
            out_specs=[HBM, SMEM],
            scratch_shapes=[
                pltpu.VMEM((len(early), TAG, width), bf16),
                pltpu.SMEM((len(early), plan.rows), jnp.int32),
                pltpu.SemaphoreType.DMA((len(early),)),
                pltpu.SemaphoreType.DMA((len(early), plan.first)),
            ],
            compiler_params=params(),
            cost_estimate=COST,
            name="place_early",
        )(*[first[o] for o in early])
        held, sets = [out], [sets]

    def place(held, messages, name):
        def body(*refs):
            refs = list(refs)[len(held) :]
            sets_ref = refs.pop(0) if sets else None
            count = len(messages)
            place_late_kernel(plan, messages, early, sets_ref, refs[:count], *refs[count:])

        return [
            pl.pallas_call(
                body,
                out_shape=out_shape,
                in_specs=[HBM] * len(held) + [ANY] * (len(sets) + len(messages)),
                out_specs=HBM,
                input_output_aliases={0: 0} if held else {},
                scratch_shapes=[
                    pltpu.SMEM((max(1, len(early)),), jnp.int32),
                    pltpu.SMEM((len(messages), plan.rows), jnp.int32),
                    pltpu.SemaphoreType.DMA,
                    pltpu.SemaphoreType.DMA((len(messages), plan.rows)),
                ],
                compiler_params=params(),
                cost_estimate=MID if name == "place_mid" else COST,
                name=name,
            )(*held, *sets, *[arrived[m] for m in messages])
        ]

    last = [late(4, 1), late(6, 0), late(6, 1)]
    held = place(held, [m for m in plan.late if m not in last], "place_mid")
    held = place(held, last, "place_last")
    return held[0][None]


def solution(mesh):
    return jax.shard_map(
        local,
        mesh=mesh,
        in_specs=(
            P("front", "wide", None),
            P("front", "wide", None),
            P("front", "wide", None),
            P("front", "wide"),
            P("front", "wide", None),
            P("front", "wide", None),
        ),
        out_specs=P("front", "wide", None),
        check_vma=False,
    )
```

```python
import functools

import jax
import jax.numpy as jnp
from jax import lax
from jax.experimental import pallas as pl
from jax.experimental.pallas import tpu as pltpu
from jax.sharding import PartitionSpec as P

GRID_COLS = 8
NEAR = GRID_COLS // 2
TAG = 8

ANY = pl.BlockSpec(memory_space=pl.ANY)
HBM = pl.BlockSpec(memory_space=pltpu.HBM)
SMEM = pl.BlockSpec(memory_space=pltpu.SMEM)
VMEM = pl.BlockSpec(memory_space=pltpu.VMEM)


class Plan:
    def __init__(self, updates, panels, slot_cols):
        self.groups = lax.axis_size("front")
        self.lanes = lax.axis_size("wide")
        self.grid_rows = self.lanes // GRID_COLS
        self.slots = slot_cols.shape[1]
        self.columns = slot_cols.shape[2]
        self.block = updates.shape[1] // self.slots
        self.rows = panels.shape[1] // self.block
        self.window = panels.shape[2] // self.block
        self.col_groups = self.window // GRID_COLS
        self.width = self.col_groups * self.block
        self.capacity = max(self.slots // 4, self.slots // self.groups)
        self.first = max(0, self.rows - self.capacity * self.groups)
        self.early = {4: self.first // 2, 5: self.first, 7: self.first}
        self.late = []
        for o in range(GRID_COLS):
            count = self.rows - self.early.get(o, 0)
            cuts = [0, count // 2, count] if o == 3 else [0, count]
            self.late += [(o, lo, hi) for lo, hi in zip(cuts, cuts[1:]) if lo < hi]


MID = pl.CostEstimate(flops=0, transcendentals=0, bytes_accessed=0)
COST = pl.CostEstimate(flops=0, transcendentals=0, bytes_accessed=0)


def params():
    return pltpu.CompilerParams(vmem_limit_bytes=48 << 20)


def at(start, size):
    return pl.ds(pl.multiple_of(start * size, size), size)


def parent_of(plan, heads, q):
    return heads[q] // plan.rows


def row_of(plan, heads, q):
    return heads[q] % plan.rows


def touched_rows(plan, head_refs):
    me = lax.axis_index("front")
    touched = jnp.int32(0)
    for heads in head_refs:
        for q in range(plan.slots):
            bit = jnp.left_shift(jnp.int32(1), row_of(plan, heads, q))
            touched = touched | jnp.where(parent_of(plan, heads, q) == me, bit, 0)
    return touched


def first_rows(plan, touched, limit):
    chosen, count = jnp.int32(0), jnp.int32(0)
    for t in range(plan.rows):
        free = (jnp.right_shift(touched, t) & 1) == 0
        take = jnp.logical_and(free, count < limit)
        chosen = chosen | jnp.where(take, 1 << t, 0)
        count = count + jnp.where(take, 1, 0)
    return chosen


def positions(plan, chosen):
    out, count = [], jnp.int32(0)
    for t in range(plan.rows):
        bit = jnp.right_shift(chosen, t) & 1
        out.append((bit, jnp.where(bit == 1, count, t - count)))
        count = count + bit
    return out


def list_rows(plan, chosen, bit_wanted, where):
    for t, (bit, place) in enumerate(positions(plan, chosen)):

        @pl.when(bit == bit_wanted)
        def _():
            where[place] = t


def run_all(copies):
    for copy in copies:
        copy.start()
    for copy in copies:
        copy.wait()


def stage_kernel(plan, lead, panel, *refs):
    staged, sems = refs[: len(lead)], refs[len(lead)]
    column = lax.axis_index("wide") // plan.grid_rows
    block = plan.block
    run_all(
        [
            pltpu.make_async_copy(
                panel.at[0, :, at(cc * GRID_COLS + jnp.bitwise_xor(column, o), block)],
                staged[i].at[:, pl.ds(cc * block, block)],
                sems.at[i, cc],
            )
            for i, o in enumerate(lead)
            for cc in range(plan.col_groups)
        ]
    )


def put_tag(plan, touched, o, out):
    chosen = first_rows(plan, touched, plan.early[o]).astype(jnp.float32)
    tag = jnp.full((TAG, plan.width), chosen, jnp.float32).astype(jnp.bfloat16)
    out[plan.early[o] * plan.block :, :] = tag


def pack_kernel(plan, lead, *refs):
    groups, count = plan.groups, len(lead)
    head_refs, staged, refs = refs[:groups], refs[groups : groups + count], refs[groups + count :]
    outs, (touched_out, order) = refs[:count], refs[count:]
    block = plan.block
    touched = touched_rows(plan, head_refs)
    touched_out[0] = touched
    list_rows(plan, first_rows(plan, touched, plan.first), 1, order)
    for i, o in enumerate(lead):
        for k in range(plan.early[o]):
            outs[i][pl.ds(k * block, block), :] = staged[i][at(order[k], block), :]
        put_tag(plan, touched, o, outs[i])


def bucket_kernel(plan, tail, heads, *refs):
    touched_ref, refs = (refs[0], refs[1:]) if tail else (None, refs)
    updates, panel, refs = refs[0], refs[1], refs[2:]
    count = (plan.groups - 1) * plan.capacity
    outs, packed, refs = refs[:count], refs[count : count + len(tail)], refs[count + len(tail) :]
    order, slot_sems, sems = refs
    me = lax.axis_index("front")
    column = lax.axis_index("wide") // plan.grid_rows
    block = plan.block

    def buckets(act):
        for k in range(1, plan.groups):
            target = lax.rem(me + k, plan.groups)
            rank = jnp.int32(0)
            for q in range(plan.slots):
                named = parent_of(plan, heads, q) == target
                for c in range(plan.capacity):

                    @pl.when(jnp.logical_and(named, rank == c))
                    def _():
                        act(
                            pltpu.make_async_copy(
                                updates.at[0, pl.ds(q * block, block)],
                                outs[(k - 1) * plan.capacity + c],
                                slot_sems.at[q],
                            )
                        )

                rank = rank + jnp.where(named, 1, 0)

    buckets(lambda c: c.start())
    copies = []
    if tail:
        touched = touched_ref[0]
        list_rows(plan, first_rows(plan, touched, plan.first), 1, order)
        for i, o in enumerate(tail):
            target = jnp.bitwise_xor(column, o)
            for k in range(plan.early[o]):
                for cc in range(plan.col_groups):
                    copies.append(
                        pltpu.make_async_copy(
                            panel.at[0, at(order[k], block), at(cc * GRID_COLS + target, block)],
                            packed[i].at[pl.ds(k * block, block), pl.ds(cc * block, block)],
                            sems.at[i, k, cc],
                        )
                    )
                    copies[-1].start()
            put_tag(plan, touched, o, packed[i])
    for copy in copies:
        copy.wait()
    buckets(lambda c: c.wait())


def assemble_kernel(plan, *refs):
    groups, block = plan.groups, plan.block
    head_refs, refs = refs[:groups], refs[groups:]
    code_refs, refs = refs[:groups], refs[groups:]
    panel, updates, refs = refs[0], refs[1], refs[2:]
    count = (groups - 1) * plan.capacity
    got, refs = refs[:count], refs[count:]
    outs, refs = refs[: len(plan.late)], refs[len(plan.late) :]
    total, raw, moved, place_ref, row_sems, slot_sems = refs
    me = lax.axis_index("front")
    column = lax.axis_index("wide") // plan.grid_rows

    slot_copies = [
        pltpu.make_async_copy(
            updates.at[0, pl.ds(q * block, block)], moved.at[q], slot_sems.at[q]
        )
        for q in range(plan.slots)
    ]
    for k in range(1, groups):
        for c in range(plan.capacity):
            part = (k - 1) * plan.capacity + c
            index = plan.slots + part
            slot_copies.append(
                pltpu.make_async_copy(got[part], moved.at[index], slot_sems.at[index])
            )
    row_copies = [
        pltpu.make_async_copy(panel.at[0, pl.ds(t * block, block)], raw.at[t], row_sems.at[t])
        for t in range(plan.rows)
    ]
    for copy in row_copies + slot_copies:
        copy.start()

    touched = touched_rows(plan, head_refs)
    for o in plan.early:
        for t, (bit, place) in enumerate(
            positions(plan, first_rows(plan, touched, plan.early[o]))
        ):
            place_ref[o, t] = jnp.where(bit == 1, -1, place)

    for t in range(plan.rows):
        row_copies[t].wait()
    for copy in slot_copies:
        copy.wait()

    def widen(t, carry):
        total[t] = raw[t].astype(jnp.float32)
        return carry

    lax.fori_loop(0, plan.rows, widen, 0)

    for s, (heads, codes) in enumerate(zip(head_refs, code_refs)):

        def add_slot(q, rank):
            named = parent_of(plan, heads, q) == me
            index = q if s == 0 else plan.slots + (s - 1) * plan.capacity + rank
            t = row_of(plan, heads, q)

            @pl.when(named)
            def _():
                for j in range(plan.columns):
                    code = codes[q, j]
                    col = code % plan.window

                    @pl.when(code >= plan.window)
                    def _():
                        where = at(col, block)
                        total[t, :, where] += moved[
                            index, :, pl.ds(j * block, block)
                        ].astype(jnp.float32)

            return rank + jnp.where(named, 1, 0)

        lax.fori_loop(0, plan.slots, add_slot, jnp.int32(0))

    def pack(t, carry):
        for ref, (o, lo, hi) in zip(outs, plan.late):
            target = jnp.bitwise_xor(column, o)

            def put(row):
                for cc in range(plan.col_groups):
                    ref[at(row, block), pl.ds(cc * block, block)] = total[
                        t, :, at(cc * GRID_COLS + target, block)
                    ].astype(jnp.bfloat16)

            if hi - lo == plan.rows:
                put(t)
            else:
                place = place_ref[o, t] if plan.early.get(o) else t
                pl.when(jnp.logical_and(place >= lo, place < hi))(lambda: put(place - lo))

        return carry

    lax.fori_loop(0, plan.rows, pack, 0)


def place_early_kernel(plan, offsets, *refs):
    count = len(offsets)
    pieces, out, sets, refs = refs[:count], refs[count], refs[count + 1], refs[count + 2 :]
    tags, where, tag_sems, sems = refs
    column = lax.axis_index("wide") // plan.grid_rows
    block = plan.block
    run_all(
        [
            pltpu.make_async_copy(
                pieces[i].at[pl.ds(plan.early[o] * block, TAG)], tags.at[i], tag_sems.at[i]
            )
            for i, o in enumerate(offsets)
        ]
    )
    copies = []
    for i, o in enumerate(offsets):
        source = jnp.bitwise_xor(column, o)
        chosen = jnp.max(tags[i].astype(jnp.float32)).astype(jnp.int32)
        sets[i] = chosen
        list_rows(plan, chosen, 1, where.at[i])
        for k in range(plan.early[o]):
            copies.append(
                pltpu.make_async_copy(
                    pieces[i].at[pl.ds(k * block, block)],
                    out.at[at(where[i, k] * GRID_COLS + source, block)],
                    sems.at[i, k],
                )
            )
            copies[-1].start()
    for copy in copies:
        copy.wait()


def place_late_kernel(plan, messages, early, sets, pieces, out, held, where, set_sem, sems):
    column = lax.axis_index("wide") // plan.grid_rows
    block = plan.block
    copies = []

    def place(i, rows):
        o, lo, hi = messages[i]
        source = jnp.bitwise_xor(column, o)
        for k in range(lo, hi):
            copies.append(
                pltpu.make_async_copy(
                    pieces[i].at[pl.ds((k - lo) * block, block)],
                    out.at[at(rows[k] * GRID_COLS + source, block)],
                    sems.at[i, k],
                )
            )
            copies[-1].start()

    split = [i for i, m in enumerate(messages) if m[0] in early]
    if split:
        fetch = pltpu.make_async_copy(sets, held, set_sem)
        fetch.start()
    for i in range(len(messages)):
        if i not in split:
            place(i, range(plan.rows))
    if split:
        fetch.wait()
    for i in split:
        list_rows(plan, held[early.index(messages[i][0])], 0, where.at[i])
        place(i, where.at[i])
    for copy in copies:
        copy.wait()


def after(value, *others):
    return lax.optimization_barrier((value, *others))[0]


def across(value, plan, offset):
    pairs = [
        (c * plan.grid_rows + r, (c ^ offset) * plan.grid_rows + r)
        for c in range(GRID_COLS)
        for r in range(plan.grid_rows)
    ]
    return lax.ppermute(value, "wide", pairs)


def along(value, plan, steps):
    return lax.ppermute(
        value, "front", [(f, (f + steps) % plan.groups) for f in range(plan.groups)]
    )


def local(updates, parent_panels, slot_parent, slot_row, slot_cols, slot_mask):
    plan = Plan(updates, parent_panels, slot_cols)
    block, width = plan.block, plan.width
    bf16 = jnp.bfloat16
    heads = slot_parent[0, :, 0] * plan.rows + slot_row[0]
    all_heads = [heads] + [along(heads, plan, k) for k in range(1, plan.groups)]
    codes = slot_mask[0] * plan.window + slot_cols[0]
    panels = pltpu.with_memory_space_constraint(parent_panels, pltpu.HBM)
    moving = pltpu.with_memory_space_constraint(updates, pltpu.HBM)


    early = [o for o in plan.early if plan.early[o]]
    lead, tail = early[:2], early[2:]
    packed, touched = {}, []

    def early_shape(o):
        return jax.ShapeDtypeStruct((plan.early[o] * block + TAG, width), bf16)

    if lead:
        staged = pl.pallas_call(
            functools.partial(stage_kernel, plan, lead),
            out_shape=[jax.ShapeDtypeStruct((plan.rows * block, width), bf16) for _ in lead],
            in_specs=[HBM],
            out_specs=[VMEM] * len(lead),
            scratch_shapes=[pltpu.SemaphoreType.DMA((len(lead), plan.col_groups))],
            compiler_params=params(),
            cost_estimate=COST,
            name="stage",
        )(panels)
        *outs, touched_set = pl.pallas_call(
            functools.partial(pack_kernel, plan, lead),
            out_shape=[early_shape(o) for o in lead] + [jax.ShapeDtypeStruct((1,), jnp.int32)],
            in_specs=[SMEM] * plan.groups + [VMEM] * len(lead),
            out_specs=[VMEM] * len(lead) + [SMEM],
            scratch_shapes=[pltpu.SMEM((plan.rows,), jnp.int32)],
            compiler_params=params(),
            cost_estimate=COST,
            name="pack_early",
        )(*all_heads, *staged)
        packed = dict(zip(lead, outs))
        touched = [touched_set]

    count = (plan.groups - 1) * plan.capacity
    outs = pl.pallas_call(
        functools.partial(bucket_kernel, plan, tail),
        out_shape=[jax.ShapeDtypeStruct((block, updates.shape[2]), bf16)] * count
        + [early_shape(o) for o in tail],
        in_specs=[SMEM] * (1 + len(touched)) + [HBM, HBM],
        out_specs=[VMEM] * (count + len(tail)),
        scratch_shapes=[
            pltpu.SMEM((plan.rows,), jnp.int32),
            pltpu.SemaphoreType.DMA((plan.slots,)),
            pltpu.SemaphoreType.DMA((max(1, len(tail)), max(1, plan.first), plan.col_groups)),
        ],
        compiler_params=params(),
        cost_estimate=COST,
        name="bucket",
    )(heads, *touched, moving, panels)
    packed.update(zip(tail, outs[count:]))

    all_codes = [after(codes, *touched)]
    all_codes += [along(all_codes[0], plan, k) for k in range(1, plan.groups)]
    got = [
        along(outs[(k - 1) * plan.capacity + c], plan, k)
        for k in range(1, plan.groups)
        for c in range(plan.capacity)
    ]

    moved = plan.slots + (plan.groups - 1) * plan.capacity
    assembled = pl.pallas_call(
        functools.partial(assemble_kernel, plan),
        out_shape=[
            jax.ShapeDtypeStruct(((hi - lo) * block, width), bf16) for o, lo, hi in plan.late
        ],
        in_specs=[SMEM] * (2 * plan.groups) + [HBM, HBM] + [ANY] * len(got),
        out_specs=[VMEM] * len(plan.late),
        scratch_shapes=[
            pltpu.VMEM((plan.rows, block, parent_panels.shape[2]), jnp.float32),
            pltpu.VMEM((plan.rows, block, parent_panels.shape[2]), bf16),
            pltpu.VMEM((moved, block, updates.shape[2]), bf16),
            pltpu.SMEM((GRID_COLS, plan.rows), jnp.int32),
            pltpu.SemaphoreType.DMA((plan.rows,)),
            pltpu.SemaphoreType.DMA((moved,)),
        ],
        compiler_params=params(),
        cost_estimate=COST,
        name="assemble",
    )(*all_heads, *all_codes, panels, moving, *got)

    ready = dict(zip(plan.late, assembled))

    def late(o, part=0):
        return [m for m in plan.late if m[0] == o][part]

    arrived = {late(0): ready[late(0)]}

    def send(message, *others):
        arrived[message] = across(after(ready[message], *others), plan, message[0])
        return arrived[message]

    first = {}

    def send_early(o, *others):
        if o in packed:
            first[o] = across(after(packed[o], *others), plan, o)

    def came(*offsets):
        return [first[o] for o in offsets if o in first]

    send_early(4)
    send_early(5)
    send_early(7, *came(4), *all_codes[1:])
    b5 = send(late(5), *came(5))
    b7 = send(late(7), *came(7))
    send(late(6), b5)
    send(late(4), b7)
    n1 = send(late(1), *came(5))
    send(late(2), *came(7))
    send(late(3, 0), n1)
    send(late(3, 1), b7)

    out_shape = jax.ShapeDtypeStruct((plan.rows * GRID_COLS * block, width), bf16)
    held, sets = [], []
    if early:
        out, sets = pl.pallas_call(
            functools.partial(place_early_kernel, plan, early),
            out_shape=[out_shape, jax.ShapeDtypeStruct((len(early),), jnp.int32)],
            in_specs=[ANY] * len(early),
            out_specs=[HBM, SMEM],
            scratch_shapes=[
                pltpu.VMEM((len(early), TAG, width), bf16),
                pltpu.SMEM((len(early), plan.rows), jnp.int32),
                pltpu.SemaphoreType.DMA((len(early),)),
                pltpu.SemaphoreType.DMA((len(early), plan.first)),
            ],
            compiler_params=params(),
            cost_estimate=COST,
            name="place_early",
        )(*[first[o] for o in early])
        held, sets = [out], [sets]

    def place(held, messages, name):
        def body(*refs):
            refs = list(refs)[len(held) :]
            sets_ref = refs.pop(0) if sets else None
            count = len(messages)
            place_late_kernel(plan, messages, early, sets_ref, refs[:count], *refs[count:])

        return [
            pl.pallas_call(
                body,
                out_shape=out_shape,
                in_specs=[HBM] * len(held) + [ANY] * (len(sets) + len(messages)),
                out_specs=HBM,
                input_output_aliases={0: 0} if held else {},
                scratch_shapes=[
                    pltpu.SMEM((max(1, len(early)),), jnp.int32),
                    pltpu.SMEM((len(messages), plan.rows), jnp.int32),
                    pltpu.SemaphoreType.DMA,
                    pltpu.SemaphoreType.DMA((len(messages), plan.rows)),
                ],
                compiler_params=params(),
                cost_estimate=MID if name == "place_mid" else COST,
                name=name,
            )(*held, *sets, *[arrived[m] for m in messages])
        ]

    last = [late(4), late(6)]
    held = place(held, [m for m in plan.late if m not in last], "place_mid")
    held = place(held, last, "place_last")
    return held[0][None]


def solution(mesh):
    return jax.shard_map(
        local,
        mesh=mesh,
        in_specs=(
            P("front", "wide", None),
            P("front", "wide", None),
            P("front", "wide", None),
            P("front", "wide"),
            P("front", "wide", None),
            P("front", "wide", None),
        ),
        out_specs=P("front", "wide", None),
        check_vma=False,
    )
```

```python
import functools

import jax
import jax.numpy as jnp
from jax import lax
from jax.experimental import pallas as pl
from jax.experimental.pallas import tpu as pltpu
from jax.sharding import PartitionSpec as P

GRID_COLS = 8
NEAR = GRID_COLS // 2
TAG = 8

ANY = pl.BlockSpec(memory_space=pl.ANY)
HBM = pl.BlockSpec(memory_space=pltpu.HBM)
SMEM = pl.BlockSpec(memory_space=pltpu.SMEM)
VMEM = pl.BlockSpec(memory_space=pltpu.VMEM)


class Plan:
    def __init__(self, updates, panels, slot_cols):
        self.groups = lax.axis_size("front")
        self.lanes = lax.axis_size("wide")
        self.grid_rows = self.lanes // GRID_COLS
        self.slots = slot_cols.shape[1]
        self.columns = slot_cols.shape[2]
        self.block = updates.shape[1] // self.slots
        self.rows = panels.shape[1] // self.block
        self.window = panels.shape[2] // self.block
        self.col_groups = self.window // GRID_COLS
        self.width = self.col_groups * self.block
        self.capacity = max(self.slots // 4, self.slots // self.groups)
        self.first = max(0, self.rows - self.capacity * self.groups)
        self.early = {4: self.first // 2, 5: self.first, 7: self.first}
        self.late = []
        for o in range(GRID_COLS):
            count = self.rows - self.early.get(o, 0)
            cuts = [0, count // 2, count] if o == 3 else [0, count]
            self.late += [(o, lo, hi) for lo, hi in zip(cuts, cuts[1:]) if lo < hi]


MID = pl.CostEstimate(flops=0, transcendentals=0, bytes_accessed=0)
COST = pl.CostEstimate(flops=0, transcendentals=0, bytes_accessed=0)


def params():
    return pltpu.CompilerParams(vmem_limit_bytes=48 << 20)


def at(start, size):
    return pl.ds(pl.multiple_of(start * size, size), size)


def own_row(plan, heads, q, front):
    row = heads[q] - front * plan.rows
    return jnp.logical_and(row >= 0, row < plan.rows), row


def touched_rows(plan, head_refs):
    me = lax.axis_index("front")
    touched = jnp.int32(0)
    for heads in head_refs:
        for q in range(plan.slots):
            named, row = own_row(plan, heads, q, me)
            bit = jnp.left_shift(jnp.int32(1), jnp.where(named, row, 0))
            touched = touched | jnp.where(named, bit, 0)
    return touched


def first_rows(plan, touched, limits, order=None):
    chosen, count = [jnp.int32(0) for _ in limits], jnp.int32(0)
    for t in range(plan.rows):
        free = 1 - (jnp.right_shift(touched, t) & 1)
        chosen = [c | jnp.where(count < n, free << t, 0) for c, n in zip(chosen, limits)]
        if order is not None:
            order[count] = t
        count = count + free
    return chosen


def positions(plan, chosen):
    out, count = [], jnp.int32(0)
    for t in range(plan.rows):
        bit = jnp.right_shift(chosen, t) & 1
        out.append((bit, jnp.where(bit == 1, count, t - count)))
        count = count + bit
    return out


def list_rows(plan, chosen, bit_wanted, where):
    for t, (bit, place) in enumerate(positions(plan, chosen)):

        @pl.when(bit == bit_wanted)
        def _():
            where[place] = t


def run_all(copies):
    for copy in copies:
        copy.start()
    for copy in copies:
        copy.wait()


def stage_kernel(plan, lead, panel, *refs):
    staged, sems = refs[: len(lead)], refs[len(lead)]
    column = lax.axis_index("wide") // plan.grid_rows
    block = plan.block
    run_all(
        [
            pltpu.make_async_copy(
                panel.at[0, :, at(cc * GRID_COLS + jnp.bitwise_xor(column, o), block)],
                staged[i].at[:, pl.ds(cc * block, block)],
                sems.at[i, cc],
            )
            for i, o in enumerate(lead)
            for cc in range(plan.col_groups)
        ]
    )


def put_tag(plan, chosen, o, out):
    chosen = chosen.astype(jnp.float32)
    tag = jnp.full((TAG, plan.width), chosen, jnp.float32).astype(jnp.bfloat16)
    out[plan.early[o] * plan.block :, :] = tag


def pack_kernel(plan, lead, *refs):
    groups, count = plan.groups, len(lead)
    head_refs, staged, refs = refs[:groups], refs[groups : groups + count], refs[groups + count :]
    outs, (touched_out, order) = refs[:count], refs[count:]
    block = plan.block
    touched = touched_rows(plan, head_refs)
    touched_out[0] = touched
    chosen = first_rows(plan, touched, [plan.early[o] for o in lead], order)
    for i, o in enumerate(lead):
        for k in range(plan.early[o]):
            outs[i][pl.ds(k * block, block), :] = staged[i][at(order[k], block), :]
        put_tag(plan, chosen[i], o, outs[i])


def bucket_kernel(plan, tail, heads, *refs):
    touched_ref, refs = (refs[0], refs[1:]) if tail else (None, refs)
    updates, panel, refs = refs[0], refs[1], refs[2:]
    count = (plan.groups - 1) * plan.capacity
    outs, packed, refs = refs[:count], refs[count : count + len(tail)], refs[count + len(tail) :]
    order, slot_sems, sems = refs
    me = lax.axis_index("front")
    column = lax.axis_index("wide") // plan.grid_rows
    block = plan.block

    def buckets(act):
        for k in range(1, plan.groups):
            target = lax.rem(me + k, plan.groups)
            rank = jnp.int32(0)
            for q in range(plan.slots):
                named, _ = own_row(plan, heads, q, target)
                for c in range(plan.capacity):

                    @pl.when(jnp.logical_and(named, rank == c))
                    def _():
                        act(
                            pltpu.make_async_copy(
                                updates.at[0, pl.ds(q * block, block)],
                                outs[(k - 1) * plan.capacity + c],
                                slot_sems.at[q],
                            )
                        )

                rank = rank + jnp.where(named, 1, 0)

    buckets(lambda c: c.start())
    copies = []
    if tail:
        touched = touched_ref[0]
        chosen = first_rows(plan, touched, [plan.early[o] for o in tail], order)
        for i, o in enumerate(tail):
            target = jnp.bitwise_xor(column, o)
            for k in range(plan.early[o]):
                for cc in range(plan.col_groups):
                    copies.append(
                        pltpu.make_async_copy(
                            panel.at[0, at(order[k], block), at(cc * GRID_COLS + target, block)],
                            packed[i].at[pl.ds(k * block, block), pl.ds(cc * block, block)],
                            sems.at[i, k, cc],
                        )
                    )
                    copies[-1].start()
            put_tag(plan, chosen[i], o, packed[i])
    for copy in copies:
        copy.wait()
    buckets(lambda c: c.wait())


def assemble_kernel(plan, *refs):
    groups, block = plan.groups, plan.block
    head_refs, refs = refs[:groups], refs[groups:]
    code_refs, refs = refs[:groups], refs[groups:]
    panel, updates, refs = refs[0], refs[1], refs[2:]
    count = (groups - 1) * plan.capacity
    got, refs = refs[:count], refs[count:]
    outs, refs = refs[: len(plan.late)], refs[len(plan.late) :]
    total, raw, moved, place_ref, row_sems, slot_sems = refs
    me = lax.axis_index("front")
    column = lax.axis_index("wide") // plan.grid_rows

    slot_copies = [
        pltpu.make_async_copy(
            updates.at[0, pl.ds(q * block, block)], moved.at[q], slot_sems.at[q]
        )
        for q in range(plan.slots)
    ]
    for k in range(1, groups):
        for c in range(plan.capacity):
            part = (k - 1) * plan.capacity + c
            index = plan.slots + part
            slot_copies.append(
                pltpu.make_async_copy(got[part], moved.at[index], slot_sems.at[index])
            )
    row_copies = [
        pltpu.make_async_copy(panel.at[0, pl.ds(t * block, block)], raw.at[t], row_sems.at[t])
        for t in range(plan.rows)
    ]
    for copy in row_copies + slot_copies:
        copy.start()

    touched = touched_rows(plan, head_refs)
    limits = list(plan.early.values())
    for o, chosen in zip(plan.early, first_rows(plan, touched, limits)):
        for t, (bit, place) in enumerate(positions(plan, chosen)):
            place_ref[o, t] = jnp.where(bit == 1, -1, place)

    for t in range(plan.rows):
        row_copies[t].wait()
    for copy in slot_copies:
        copy.wait()

    def widen(t, carry):
        total[t] = raw[t].astype(jnp.float32)
        return carry

    lax.fori_loop(0, plan.rows, widen, 0)

    for s, (heads, codes) in enumerate(zip(head_refs, code_refs)):

        def add_slot(q, rank):
            named, t = own_row(plan, heads, q, me)
            index = q if s == 0 else plan.slots + (s - 1) * plan.capacity + rank

            @pl.when(named)
            def _():
                for j in range(plan.columns):
                    code = codes[q, j]
                    col = code % plan.window

                    @pl.when(code >= plan.window)
                    def _():
                        where = at(col, block)
                        total[t, :, where] += moved[
                            index, :, pl.ds(j * block, block)
                        ].astype(jnp.float32)

            return rank + jnp.where(named, 1, 0)

        lax.fori_loop(0, plan.slots, add_slot, jnp.int32(0))

    def pack(t, carry):
        for ref, (o, lo, hi) in zip(outs, plan.late):
            target = jnp.bitwise_xor(column, o)

            def put(row):
                for cc in range(plan.col_groups):
                    ref[at(row, block), pl.ds(cc * block, block)] = total[
                        t, :, at(cc * GRID_COLS + target, block)
                    ].astype(jnp.bfloat16)

            if hi - lo == plan.rows:
                put(t)
            else:
                place = place_ref[o, t] if plan.early.get(o) else t
                pl.when(jnp.logical_and(place >= lo, place < hi))(lambda: put(place - lo))

        return carry

    lax.fori_loop(0, plan.rows, pack, 0)


def place_early_kernel(plan, offsets, *refs):
    count = len(offsets)
    pieces, out, sets, refs = refs[:count], refs[count], refs[count + 1], refs[count + 2 :]
    tags, where, tag_sems, sems = refs
    column = lax.axis_index("wide") // plan.grid_rows
    block = plan.block
    run_all(
        [
            pltpu.make_async_copy(
                pieces[i].at[pl.ds(plan.early[o] * block, TAG)], tags.at[i], tag_sems.at[i]
            )
            for i, o in enumerate(offsets)
        ]
    )
    copies = []
    for i, o in enumerate(offsets):
        source = jnp.bitwise_xor(column, o)
        chosen = jnp.max(tags[i].astype(jnp.float32)).astype(jnp.int32)
        sets[i] = chosen
        list_rows(plan, chosen, 1, where.at[i])
        for k in range(plan.early[o]):
            copies.append(
                pltpu.make_async_copy(
                    pieces[i].at[pl.ds(k * block, block)],
                    out.at[at(where[i, k] * GRID_COLS + source, block)],
                    sems.at[i, k],
                )
            )
            copies[-1].start()
    for copy in copies:
        copy.wait()


def place_late_kernel(plan, messages, early, sets, pieces, out, held, where, set_sem, sems):
    column = lax.axis_index("wide") // plan.grid_rows
    block = plan.block
    copies = []

    def place(i, rows):
        o, lo, hi = messages[i]
        source = jnp.bitwise_xor(column, o)
        for k in range(lo, hi):
            copies.append(
                pltpu.make_async_copy(
                    pieces[i].at[pl.ds((k - lo) * block, block)],
                    out.at[at(rows[k] * GRID_COLS + source, block)],
                    sems.at[i, k],
                )
            )
            copies[-1].start()

    split = [i for i, m in enumerate(messages) if m[0] in early]
    if split:
        fetch = pltpu.make_async_copy(sets, held, set_sem)
        fetch.start()
    for i in range(len(messages)):
        if i not in split:
            place(i, range(plan.rows))
    if split:
        fetch.wait()
    for i in split:
        list_rows(plan, held[early.index(messages[i][0])], 0, where.at[i])
        place(i, where.at[i])
    for copy in copies:
        copy.wait()


def after(value, *others):
    return lax.optimization_barrier((value, *others))[0]


def across(value, plan, offset):
    pairs = [
        (c * plan.grid_rows + r, (c ^ offset) * plan.grid_rows + r)
        for c in range(GRID_COLS)
        for r in range(plan.grid_rows)
    ]
    return lax.ppermute(value, "wide", pairs)


def along(value, plan, steps):
    return lax.ppermute(
        value, "front", [(f, (f + steps) % plan.groups) for f in range(plan.groups)]
    )


def local(updates, parent_panels, slot_parent, slot_row, slot_cols, slot_mask):
    plan = Plan(updates, parent_panels, slot_cols)
    block, width = plan.block, plan.width
    bf16 = jnp.bfloat16
    heads = slot_parent[0, :, 0] * plan.rows + slot_row[0]
    all_heads = [heads] + [along(heads, plan, k) for k in range(1, plan.groups)]
    codes = slot_mask[0] * plan.window + slot_cols[0]
    panels = pltpu.with_memory_space_constraint(parent_panels, pltpu.HBM)
    moving = pltpu.with_memory_space_constraint(updates, pltpu.HBM)


    early = [o for o in plan.early if plan.early[o]]
    lead, tail = early[:2], early[2:]
    packed, touched = {}, []

    def early_shape(o):
        return jax.ShapeDtypeStruct((plan.early[o] * block + TAG, width), bf16)

    if lead:
        staged = pl.pallas_call(
            functools.partial(stage_kernel, plan, lead),
            out_shape=[jax.ShapeDtypeStruct((plan.rows * block, width), bf16) for _ in lead],
            in_specs=[HBM],
            out_specs=[VMEM] * len(lead),
            scratch_shapes=[pltpu.SemaphoreType.DMA((len(lead), plan.col_groups))],
            compiler_params=params(),
            cost_estimate=COST,
            name="stage",
        )(panels)
        *outs, touched_set = pl.pallas_call(
            functools.partial(pack_kernel, plan, lead),
            out_shape=[early_shape(o) for o in lead] + [jax.ShapeDtypeStruct((1,), jnp.int32)],
            in_specs=[SMEM] * plan.groups + [VMEM] * len(lead),
            out_specs=[VMEM] * len(lead) + [SMEM],
            scratch_shapes=[pltpu.SMEM((plan.rows,), jnp.int32)],
            compiler_params=params(),
            cost_estimate=COST,
            name="pack_early",
        )(*all_heads, *staged)
        packed = dict(zip(lead, outs))
        touched = [touched_set]

    count = (plan.groups - 1) * plan.capacity
    outs = pl.pallas_call(
        functools.partial(bucket_kernel, plan, tail),
        out_shape=[jax.ShapeDtypeStruct((block, updates.shape[2]), bf16)] * count
        + [early_shape(o) for o in tail],
        in_specs=[SMEM] * (1 + len(touched)) + [HBM, HBM],
        out_specs=[VMEM] * (count + len(tail)),
        scratch_shapes=[
            pltpu.SMEM((plan.rows,), jnp.int32),
            pltpu.SemaphoreType.DMA((plan.slots,)),
            pltpu.SemaphoreType.DMA((max(1, len(tail)), max(1, plan.first), plan.col_groups)),
        ],
        compiler_params=params(),
        cost_estimate=COST,
        name="bucket",
    )(heads, *touched, moving, panels)
    packed.update(zip(tail, outs[count:]))

    all_codes = [after(codes, *touched)]
    all_codes += [along(all_codes[0], plan, k) for k in range(1, plan.groups)]
    got = [
        along(outs[(k - 1) * plan.capacity + c], plan, k)
        for k in range(1, plan.groups)
        for c in range(plan.capacity)
    ]

    moved = plan.slots + (plan.groups - 1) * plan.capacity
    assembled = pl.pallas_call(
        functools.partial(assemble_kernel, plan),
        out_shape=[
            jax.ShapeDtypeStruct(((hi - lo) * block, width), bf16) for o, lo, hi in plan.late
        ],
        in_specs=[SMEM] * (2 * plan.groups) + [HBM, HBM] + [ANY] * len(got),
        out_specs=[VMEM] * len(plan.late),
        scratch_shapes=[
            pltpu.VMEM((plan.rows, block, parent_panels.shape[2]), jnp.float32),
            pltpu.VMEM((plan.rows, block, parent_panels.shape[2]), bf16),
            pltpu.VMEM((moved, block, updates.shape[2]), bf16),
            pltpu.SMEM((GRID_COLS, plan.rows), jnp.int32),
            pltpu.SemaphoreType.DMA((plan.rows,)),
            pltpu.SemaphoreType.DMA((moved,)),
        ],
        compiler_params=params(),
        cost_estimate=COST,
        name="assemble",
    )(*all_heads, *all_codes, panels, moving, *got)

    ready = dict(zip(plan.late, assembled))

    def late(o, part=0):
        return [m for m in plan.late if m[0] == o][part]

    arrived = {late(0): ready[late(0)]}

    def send(message, *others):
        arrived[message] = across(after(ready[message], *others), plan, message[0])
        return arrived[message]

    first = {}

    def send_early(o, *others):
        if o in packed:
            first[o] = across(after(packed[o], *others), plan, o)

    def came(*offsets):
        return [first[o] for o in offsets if o in first]

    send_early(4)
    send_early(5)
    send_early(7, *came(4), *all_codes[1:])
    b5 = send(late(5), *came(5))
    b7 = send(late(7), *came(7))
    send(late(6), b5)
    send(late(4), b7)
    n1 = send(late(1), *came(5))
    send(late(2), *came(7))
    send(late(3, 0), n1)
    send(late(3, 1), b7)

    out_shape = jax.ShapeDtypeStruct((plan.rows * GRID_COLS * block, width), bf16)
    held, sets = [], []
    if early:
        out, sets = pl.pallas_call(
            functools.partial(place_early_kernel, plan, early),
            out_shape=[out_shape, jax.ShapeDtypeStruct((len(early),), jnp.int32)],
            in_specs=[ANY] * len(early),
            out_specs=[HBM, SMEM],
            scratch_shapes=[
                pltpu.VMEM((len(early), TAG, width), bf16),
                pltpu.SMEM((len(early), plan.rows), jnp.int32),
                pltpu.SemaphoreType.DMA((len(early),)),
                pltpu.SemaphoreType.DMA((len(early), plan.first)),
            ],
            compiler_params=params(),
            cost_estimate=COST,
            name="place_early",
        )(*[first[o] for o in early])
        held, sets = [out], [sets]

    def place(held, messages, name):
        def body(*refs):
            refs = list(refs)[len(held) :]
            sets_ref = refs.pop(0) if sets else None
            count = len(messages)
            place_late_kernel(plan, messages, early, sets_ref, refs[:count], *refs[count:])

        return [
            pl.pallas_call(
                body,
                out_shape=out_shape,
                in_specs=[HBM] * len(held) + [ANY] * (len(sets) + len(messages)),
                out_specs=HBM,
                input_output_aliases={0: 0} if held else {},
                scratch_shapes=[
                    pltpu.SMEM((max(1, len(early)),), jnp.int32),
                    pltpu.SMEM((len(messages), plan.rows), jnp.int32),
                    pltpu.SemaphoreType.DMA,
                    pltpu.SemaphoreType.DMA((len(messages), plan.rows)),
                ],
                compiler_params=params(),
                cost_estimate=MID if name == "place_mid" else COST,
                name=name,
            )(*held, *sets, *[arrived[m] for m in messages])
        ]

    last = [late(4), late(6)]
    held = place(held, [m for m in plan.late if m not in last], "place_mid")
    held = place(held, last, "place_last")
    return held[0][None]


def solution(mesh):
    return jax.shard_map(
        local,
        mesh=mesh,
        in_specs=(
            P("front", "wide", None),
            P("front", "wide", None),
            P("front", "wide", None),
            P("front", "wide"),
            P("front", "wide", None),
            P("front", "wide", None),
        ),
        out_specs=P("front", "wide", None),
        check_vma=False,
    )
```

```python
import functools

import jax
import jax.numpy as jnp
from jax import lax
from jax.experimental import pallas as pl
from jax.experimental.pallas import tpu as pltpu
from jax.sharding import PartitionSpec as P

GRID_COLS = 8
NEAR = GRID_COLS // 2
TAG = 8

ANY = pl.BlockSpec(memory_space=pl.ANY)
HBM = pl.BlockSpec(memory_space=pltpu.HBM)
SMEM = pl.BlockSpec(memory_space=pltpu.SMEM)
VMEM = pl.BlockSpec(memory_space=pltpu.VMEM)


class Plan:
    def __init__(self, updates, panels, slot_cols):
        self.groups = lax.axis_size("front")
        self.lanes = lax.axis_size("wide")
        self.grid_rows = self.lanes // GRID_COLS
        self.slots = slot_cols.shape[1]
        self.columns = slot_cols.shape[2]
        self.block = updates.shape[1] // self.slots
        self.rows = panels.shape[1] // self.block
        self.window = panels.shape[2] // self.block
        self.col_groups = self.window // GRID_COLS
        self.width = self.col_groups * self.block
        self.capacity = max(self.slots // 4, self.slots // self.groups)
        self.first = max(0, self.rows - self.capacity * self.groups)
        self.early = {4: self.first // 2, 5: self.first, 7: self.first}
        self.late = []
        for o in range(GRID_COLS):
            count = self.rows - self.early.get(o, 0)
            cuts = [0, count // 2, count] if o == 3 else [0, max(1, count - 2), count] if o in (4, 6) else [0, count]
            self.late += [(o, lo, hi) for lo, hi in zip(cuts, cuts[1:]) if lo < hi]


MID = pl.CostEstimate(flops=0, transcendentals=0, bytes_accessed=0)
COST = pl.CostEstimate(flops=0, transcendentals=0, bytes_accessed=0)


def params():
    return pltpu.CompilerParams(vmem_limit_bytes=48 << 20)


def at(start, size):
    return pl.ds(pl.multiple_of(start * size, size), size)


def own_row(plan, heads, q, front):
    row = heads[q] - front * plan.rows
    return jnp.logical_and(row >= 0, row < plan.rows), row


def touched_rows(plan, head_refs):
    me = lax.axis_index("front")
    touched = jnp.int32(0)
    for heads in head_refs:
        for q in range(plan.slots):
            named, row = own_row(plan, heads, q, me)
            bit = jnp.left_shift(jnp.int32(1), jnp.where(named, row, 0))
            touched = touched | jnp.where(named, bit, 0)
    return touched


def first_rows(plan, touched, limits, order=None):
    chosen, count = [jnp.int32(0) for _ in limits], jnp.int32(0)
    for t in range(plan.rows):
        free = 1 - (jnp.right_shift(touched, t) & 1)
        chosen = [c | jnp.where(count < n, free << t, 0) for c, n in zip(chosen, limits)]
        if order is not None:
            order[count] = t
        count = count + free
    return chosen


def positions(plan, chosen):
    out, count = [], jnp.int32(0)
    for t in range(plan.rows):
        bit = jnp.right_shift(chosen, t) & 1
        out.append((bit, jnp.where(bit == 1, count, t - count)))
        count = count + bit
    return out


def list_rows(plan, chosen, bit_wanted, where):
    for t, (bit, place) in enumerate(positions(plan, chosen)):

        @pl.when(bit == bit_wanted)
        def _():
            where[place] = t


def run_all(copies):
    for copy in copies:
        copy.start()
    for copy in copies:
        copy.wait()


def stage_kernel(plan, lead, panel, *refs):
    staged, sems = refs[: len(lead)], refs[len(lead)]
    column = lax.axis_index("wide") // plan.grid_rows
    block = plan.block
    run_all(
        [
            pltpu.make_async_copy(
                panel.at[0, :, at(cc * GRID_COLS + jnp.bitwise_xor(column, o), block)],
                staged[i].at[:, pl.ds(cc * block, block)],
                sems.at[i, cc],
            )
            for i, o in enumerate(lead)
            for cc in range(plan.col_groups)
        ]
    )


def put_tag(plan, chosen, o, out):
    chosen = chosen.astype(jnp.float32)
    tag = jnp.full((TAG, plan.width), chosen, jnp.float32).astype(jnp.bfloat16)
    out[plan.early[o] * plan.block :, :] = tag


def pack_kernel(plan, lead, *refs):
    groups, count = plan.groups, len(lead)
    head_refs, staged, refs = refs[:groups], refs[groups : groups + count], refs[groups + count :]
    outs, (order, tags, sems) = refs[:count], refs[count:]
    block = plan.block
    touched = touched_rows(plan, head_refs)
    chosen = first_rows(plan, touched, [plan.early[o] for o in lead], order)
    copies = []
    for i, o in enumerate(lead):
        for k in range(plan.early[o]):
            copies.append(
                pltpu.make_async_copy(
                    staged[i].at[at(order[k], block)],
                    outs[i].at[pl.ds(k * block, block)],
                    sems.at[i, k],
                )
            )
            copies[-1].start()
    for i, o in enumerate(lead):
        tag = jnp.full((TAG, plan.width), chosen[i].astype(jnp.float32), jnp.float32)
        tags[i] = tag.astype(jnp.bfloat16)
        copies.append(
            pltpu.make_async_copy(
                tags.at[i],
                outs[i].at[pl.ds(plan.early[o] * block, TAG)],
                sems.at[i, plan.first],
            )
        )
        copies[-1].start()
    for copy in copies:
        copy.wait()


def bucket_kernel(plan, tail, *refs):
    head_refs, refs = refs[: plan.groups], refs[plan.groups :]
    heads = head_refs[0]
    updates, panel, refs = refs[0], refs[1], refs[2:]
    count = (plan.groups - 1) * plan.capacity
    outs, packed, refs = refs[:count], refs[count : count + len(tail)], refs[count + len(tail) :]
    order, slot_sems, sems = refs
    me = lax.axis_index("front")
    column = lax.axis_index("wide") // plan.grid_rows
    block = plan.block

    def buckets(act):
        for k in range(1, plan.groups):
            target = lax.rem(me + k, plan.groups)
            rank = jnp.int32(0)
            for q in range(plan.slots):
                named, _ = own_row(plan, heads, q, target)
                for c in range(plan.capacity):

                    @pl.when(jnp.logical_and(named, rank == c))
                    def _():
                        act(
                            pltpu.make_async_copy(
                                updates.at[0, pl.ds(q * block, block)],
                                outs[(k - 1) * plan.capacity + c],
                                slot_sems.at[q],
                            )
                        )

                rank = rank + jnp.where(named, 1, 0)

    buckets(lambda c: c.start())
    copies = []
    if tail:
        touched = touched_rows(plan, head_refs)
        chosen = first_rows(plan, touched, [plan.early[o] for o in tail], order)
        for i, o in enumerate(tail):
            target = jnp.bitwise_xor(column, o)
            for k in range(plan.early[o]):
                for cc in range(plan.col_groups):
                    copies.append(
                        pltpu.make_async_copy(
                            panel.at[0, at(order[k], block), at(cc * GRID_COLS + target, block)],
                            packed[i].at[pl.ds(k * block, block), pl.ds(cc * block, block)],
                            sems.at[i, k, cc],
                        )
                    )
                    copies[-1].start()
            put_tag(plan, chosen[i], o, packed[i])
    for copy in copies:
        copy.wait()
    buckets(lambda c: c.wait())


def assemble_kernel(plan, *refs):
    groups, block = plan.groups, plan.block
    head_refs, refs = refs[:groups], refs[groups:]
    code_refs, refs = refs[:groups], refs[groups:]
    panel, updates, refs = refs[0], refs[1], refs[2:]
    count = (groups - 1) * plan.capacity
    got, refs = refs[:count], refs[count:]
    outs, refs = refs[: len(plan.late)], refs[len(plan.late) :]
    total, raw, moved, place_ref, row_sems, slot_sems = refs
    me = lax.axis_index("front")
    column = lax.axis_index("wide") // plan.grid_rows

    slot_copies = [
        pltpu.make_async_copy(
            updates.at[0, pl.ds(q * block, block)], moved.at[q], slot_sems.at[q]
        )
        for q in range(plan.slots)
    ]
    for k in range(1, groups):
        for c in range(plan.capacity):
            part = (k - 1) * plan.capacity + c
            index = plan.slots + part
            slot_copies.append(
                pltpu.make_async_copy(got[part], moved.at[index], slot_sems.at[index])
            )
    row_copies = [
        pltpu.make_async_copy(panel.at[0, pl.ds(t * block, block)], raw.at[t], row_sems.at[t])
        for t in range(plan.rows)
    ]
    for copy in row_copies + slot_copies:
        copy.start()

    touched = touched_rows(plan, head_refs)
    limits = list(plan.early.values())
    for o, chosen in zip(plan.early, first_rows(plan, touched, limits)):
        for t, (bit, place) in enumerate(positions(plan, chosen)):
            place_ref[o, t] = jnp.where(bit == 1, -1, place)

    for t in range(plan.rows):
        row_copies[t].wait()
    for copy in slot_copies:
        copy.wait()

    def widen(t, carry):
        total[t] = raw[t].astype(jnp.float32)
        return carry

    lax.fori_loop(0, plan.rows, widen, 0)

    for s, (heads, codes) in enumerate(zip(head_refs, code_refs)):

        def add_slot(q, rank):
            named, t = own_row(plan, heads, q, me)
            index = q if s == 0 else plan.slots + (s - 1) * plan.capacity + rank

            @pl.when(named)
            def _():
                for j in range(plan.columns):
                    code = codes[q, j]
                    col = code % plan.window

                    @pl.when(code >= plan.window)
                    def _():
                        where = at(col, block)
                        total[t, :, where] += moved[
                            index, :, pl.ds(j * block, block)
                        ].astype(jnp.float32)

            return rank + jnp.where(named, 1, 0)

        lax.fori_loop(0, plan.slots, add_slot, jnp.int32(0))

    def pack(t, carry):
        for ref, (o, lo, hi) in zip(outs, plan.late):
            target = jnp.bitwise_xor(column, o)

            def put(row):
                for cc in range(plan.col_groups):
                    ref[at(row, block), pl.ds(cc * block, block)] = total[
                        t, :, at(cc * GRID_COLS + target, block)
                    ].astype(jnp.bfloat16)

            if hi - lo == plan.rows:
                put(t)
            else:
                place = place_ref[o, t] if plan.early.get(o) else t
                pl.when(jnp.logical_and(place >= lo, place < hi))(lambda: put(place - lo))

        return carry

    lax.fori_loop(0, plan.rows, pack, 0)


def place_early_kernel(plan, offsets, *refs):
    count = len(offsets)
    pieces, out, sets, refs = refs[:count], refs[count], refs[count + 1], refs[count + 2 :]
    tags, where, tag_sems, sems = refs
    column = lax.axis_index("wide") // plan.grid_rows
    block = plan.block
    run_all(
        [
            pltpu.make_async_copy(
                pieces[i].at[pl.ds(plan.early[o] * block, TAG)], tags.at[i], tag_sems.at[i]
            )
            for i, o in enumerate(offsets)
        ]
    )
    copies = []
    for i, o in enumerate(offsets):
        source = jnp.bitwise_xor(column, o)
        chosen = jnp.max(tags[i].astype(jnp.float32)).astype(jnp.int32)
        sets[i] = chosen
        list_rows(plan, chosen, 1, where.at[i])
        for k in range(plan.early[o]):
            copies.append(
                pltpu.make_async_copy(
                    pieces[i].at[pl.ds(k * block, block)],
                    out.at[at(where[i, k] * GRID_COLS + source, block)],
                    sems.at[i, k],
                )
            )
            copies[-1].start()
    for copy in copies:
        copy.wait()


def place_late_kernel(plan, messages, early, sets, pieces, out, held, where, set_sem, sems):
    column = lax.axis_index("wide") // plan.grid_rows
    block = plan.block
    copies = []

    def place(i, rows):
        o, lo, hi = messages[i]
        source = jnp.bitwise_xor(column, o)
        for k in range(lo, hi):
            copies.append(
                pltpu.make_async_copy(
                    pieces[i].at[pl.ds((k - lo) * block, block)],
                    out.at[at(rows[k] * GRID_COLS + source, block)],
                    sems.at[i, k],
                )
            )
            copies[-1].start()

    split = [i for i, m in enumerate(messages) if m[0] in early]
    if split:
        fetch = pltpu.make_async_copy(sets, held, set_sem)
        fetch.start()
    for i in range(len(messages)):
        if i not in split:
            place(i, range(plan.rows))
    if split:
        fetch.wait()
    for i in split:
        list_rows(plan, held[early.index(messages[i][0])], 0, where.at[i])
        place(i, where.at[i])
    for copy in copies:
        copy.wait()


def after(value, *others):
    return lax.optimization_barrier((value, *others))[0]


def across(value, plan, offset):
    pairs = [
        (c * plan.grid_rows + r, (c ^ offset) * plan.grid_rows + r)
        for c in range(GRID_COLS)
        for r in range(plan.grid_rows)
    ]
    return lax.ppermute(value, "wide", pairs)


def along(value, plan, steps):
    return lax.ppermute(
        value, "front", [(f, (f + steps) % plan.groups) for f in range(plan.groups)]
    )


def local(updates, parent_panels, slot_parent, slot_row, slot_cols, slot_mask):
    plan = Plan(updates, parent_panels, slot_cols)
    block, width = plan.block, plan.width
    bf16 = jnp.bfloat16
    heads = slot_parent[0, :, 0] * plan.rows + slot_row[0]
    all_heads = [heads] + [along(heads, plan, k) for k in range(1, plan.groups)]
    codes = slot_mask[0] * plan.window + slot_cols[0]
    panels = pltpu.with_memory_space_constraint(parent_panels, pltpu.HBM)
    moving = pltpu.with_memory_space_constraint(updates, pltpu.HBM)


    early = [o for o in plan.early if plan.early[o]]
    lead, tail = early[:2], early[2:]
    packed = {}

    def early_shape(o):
        return jax.ShapeDtypeStruct((plan.early[o] * block + TAG, width), bf16)

    if lead:
        staged = pl.pallas_call(
            functools.partial(stage_kernel, plan, lead),
            out_shape=[jax.ShapeDtypeStruct((plan.rows * block, width), bf16) for _ in lead],
            in_specs=[HBM],
            out_specs=[VMEM] * len(lead),
            scratch_shapes=[pltpu.SemaphoreType.DMA((len(lead), plan.col_groups))],
            compiler_params=params(),
            cost_estimate=COST,
            name="stage",
        )(panels)
        outs = pl.pallas_call(
            functools.partial(pack_kernel, plan, lead),
            out_shape=[early_shape(o) for o in lead],
            in_specs=[SMEM] * plan.groups + [ANY] * len(lead),
            out_specs=[ANY] * len(lead),
            scratch_shapes=[
                pltpu.SMEM((plan.rows,), jnp.int32),
                pltpu.VMEM((len(lead), TAG, width), bf16),
                pltpu.SemaphoreType.DMA((len(lead), plan.first + 1)),
            ],
            compiler_params=params(),
            cost_estimate=COST,
            name="pack_early",
        )(*all_heads, *staged)
        packed = dict(zip(lead, outs))

    count = (plan.groups - 1) * plan.capacity
    outs = pl.pallas_call(
        functools.partial(bucket_kernel, plan, tail),
        out_shape=[jax.ShapeDtypeStruct((block, updates.shape[2]), bf16)] * count
        + [early_shape(o) for o in tail],
        in_specs=[SMEM] * plan.groups + [HBM, HBM],
        out_specs=[VMEM] * (count + len(tail)),
        scratch_shapes=[
            pltpu.SMEM((plan.rows,), jnp.int32),
            pltpu.SemaphoreType.DMA((plan.slots,)),
            pltpu.SemaphoreType.DMA((max(1, len(tail)), max(1, plan.first), plan.col_groups)),
        ],
        compiler_params=params(),
        cost_estimate=COST,
        name="bucket",
    )(after(heads, *packed.values()), *all_heads[1:], moving, panels)
    packed.update(zip(tail, outs[count:]))

    all_codes = [after(codes, *packed.values())]
    all_codes += [along(all_codes[0], plan, k) for k in range(1, plan.groups)]
    got = [
        along(outs[(k - 1) * plan.capacity + c], plan, k)
        for k in range(1, plan.groups)
        for c in range(plan.capacity)
    ]

    moved = plan.slots + (plan.groups - 1) * plan.capacity
    assembled = pl.pallas_call(
        functools.partial(assemble_kernel, plan),
        out_shape=[
            jax.ShapeDtypeStruct(((hi - lo) * block, width), bf16) for o, lo, hi in plan.late
        ],
        in_specs=[SMEM] * (2 * plan.groups) + [HBM, HBM] + [ANY] * len(got),
        out_specs=[VMEM] * len(plan.late),
        scratch_shapes=[
            pltpu.VMEM((plan.rows, block, parent_panels.shape[2]), jnp.float32),
            pltpu.VMEM((plan.rows, block, parent_panels.shape[2]), bf16),
            pltpu.VMEM((moved, block, updates.shape[2]), bf16),
            pltpu.SMEM((GRID_COLS, plan.rows), jnp.int32),
            pltpu.SemaphoreType.DMA((plan.rows,)),
            pltpu.SemaphoreType.DMA((moved,)),
        ],
        compiler_params=params(),
        cost_estimate=COST,
        name="assemble",
    )(*all_heads, *all_codes, panels, moving, *got)

    ready = dict(zip(plan.late, assembled))

    def late(o, part=0):
        return [m for m in plan.late if m[0] == o][part]

    arrived = {late(0): ready[late(0)]}

    def send(message, *others):
        arrived[message] = across(after(ready[message], *others), plan, message[0])
        return arrived[message]

    first = {}

    def send_early(o, *others):
        if o in packed:
            first[o] = across(after(packed[o], *others), plan, o)

    def came(*offsets):
        return [first[o] for o in offsets if o in first]

    send_early(4)
    send_early(5)
    send_early(7, *came(4), *all_codes[1:])

    def parts(o):
        return len([m for m in plan.late if m[0] == o])

    b5 = send(late(5), *came(5))
    b7 = send(late(7), *came(7))
    b6 = send(late(6, 0), b5)
    b4 = send(late(4, 0), b7)
    n1 = send(late(1), *came(5))
    send(late(2), *came(7))
    send(late(3, 0), n1)
    send(late(3, 1), b7)
    out_shape = jax.ShapeDtypeStruct((plan.rows * GRID_COLS * block, width), bf16)
    held, sets = [], []
    if early:
        out, sets = pl.pallas_call(
            functools.partial(place_early_kernel, plan, early),
            out_shape=[out_shape, jax.ShapeDtypeStruct((len(early),), jnp.int32)],
            in_specs=[ANY] * len(early),
            out_specs=[HBM, SMEM],
            scratch_shapes=[
                pltpu.VMEM((len(early), TAG, width), bf16),
                pltpu.SMEM((len(early), plan.rows), jnp.int32),
                pltpu.SemaphoreType.DMA((len(early),)),
                pltpu.SemaphoreType.DMA((len(early), plan.first)),
            ],
            compiler_params=params(),
            cost_estimate=COST,
            name="place_early",
        )(*[first[o] for o in early])
        held, sets = [out], [sets]

    if parts(6) > 1:
        send(late(6, 1), b6, *sets)
    if parts(4) > 1:
        send(late(4, 1), b4)


    def place(held, messages, name):
        def body(*refs):
            refs = list(refs)[len(held) :]
            sets_ref = refs.pop(0) if sets else None
            count = len(messages)
            place_late_kernel(plan, messages, early, sets_ref, refs[:count], *refs[count:])

        return [
            pl.pallas_call(
                body,
                out_shape=out_shape,
                in_specs=[HBM] * len(held) + [ANY] * (len(sets) + len(messages)),
                out_specs=HBM,
                input_output_aliases={0: 0} if held else {},
                scratch_shapes=[
                    pltpu.SMEM((max(1, len(early)),), jnp.int32),
                    pltpu.SMEM((len(messages), plan.rows), jnp.int32),
                    pltpu.SemaphoreType.DMA,
                    pltpu.SemaphoreType.DMA((len(messages), plan.rows)),
                ],
                compiler_params=params(),
                cost_estimate=MID if name == "place_mid" else COST,
                name=name,
            )(*held, *sets, *[arrived[m] for m in messages])
        ]

    last = [late(4, parts(4) - 1), late(6, parts(6) - 1)]
    held = place(held, [m for m in plan.late if m not in last], "place_mid")
    held = place(held, last, "place_last")
    return held[0][None]


def solution(mesh):
    return jax.shard_map(
        local,
        mesh=mesh,
        in_specs=(
            P("front", "wide", None),
            P("front", "wide", None),
            P("front", "wide", None),
            P("front", "wide"),
            P("front", "wide", None),
            P("front", "wide", None),
        ),
        out_specs=P("front", "wide", None),
        check_vma=False,
    )
```

```python
import functools

import jax
import jax.numpy as jnp
from jax import lax
from jax.experimental import pallas as pl
from jax.experimental.pallas import tpu as pltpu
from jax.sharding import PartitionSpec as P

GRID_COLS = 8
NEAR = GRID_COLS // 2
TAG = 8

ANY = pl.BlockSpec(memory_space=pl.ANY)
HBM = pl.BlockSpec(memory_space=pltpu.HBM)
SMEM = pl.BlockSpec(memory_space=pltpu.SMEM)
VMEM = pl.BlockSpec(memory_space=pltpu.VMEM)


class Plan:
    def __init__(self, updates, panels, slot_cols):
        self.groups = lax.axis_size("front")
        self.lanes = lax.axis_size("wide")
        self.grid_rows = self.lanes // GRID_COLS
        self.slots = slot_cols.shape[1]
        self.columns = slot_cols.shape[2]
        self.block = updates.shape[1] // self.slots
        self.rows = panels.shape[1] // self.block
        self.window = panels.shape[2] // self.block
        self.col_groups = self.window // GRID_COLS
        self.width = self.col_groups * self.block
        self.capacity = max(self.slots // 4, self.slots // self.groups)
        self.first = max(0, self.rows - self.capacity * self.groups)
        self.early = {4: self.first // 2, 5: self.first, 7: self.first}
        self.late = []
        for o in range(GRID_COLS):
            count = self.rows - self.early.get(o, 0)
            cuts = [0, count // 2, count] if o == 3 else [0, count]
            self.late += [(o, lo, hi) for lo, hi in zip(cuts, cuts[1:]) if lo < hi]


MID = pl.CostEstimate(flops=0, transcendentals=0, bytes_accessed=0)
COST = pl.CostEstimate(flops=0, transcendentals=0, bytes_accessed=0)


def params():
    return pltpu.CompilerParams(vmem_limit_bytes=48 << 20)


def at(start, size):
    return pl.ds(pl.multiple_of(start * size, size), size)


def own_row(plan, heads, q, front):
    row = heads[q] - front * plan.rows
    return jnp.logical_and(row >= 0, row < plan.rows), row


def touched_rows(plan, head_refs):
    me = lax.axis_index("front")
    touched = jnp.int32(0)
    for heads in head_refs:
        for q in range(plan.slots):
            named, row = own_row(plan, heads, q, me)
            bit = jnp.left_shift(jnp.int32(1), jnp.where(named, row, 0))
            touched = touched | jnp.where(named, bit, 0)
    return touched


def first_rows(plan, touched, limits, order=None):
    chosen, count = [jnp.int32(0) for _ in limits], jnp.int32(0)
    for t in range(plan.rows):
        free = 1 - (jnp.right_shift(touched, t) & 1)
        chosen = [c | jnp.where(count < n, free << t, 0) for c, n in zip(chosen, limits)]
        if order is not None:
            order[count] = t
        count = count + free
    return chosen


def positions(plan, chosen):
    out, count = [], jnp.int32(0)
    for t in range(plan.rows):
        bit = jnp.right_shift(chosen, t) & 1
        out.append((bit, jnp.where(bit == 1, count, t - count)))
        count = count + bit
    return out


def list_rows(plan, chosen, bit_wanted, where):
    for t, (bit, place) in enumerate(positions(plan, chosen)):

        @pl.when(bit == bit_wanted)
        def _():
            where[place] = t


def run_all(copies):
    for copy in copies:
        copy.start()
    for copy in copies:
        copy.wait()


def stage_kernel(plan, lead, panel, *refs):
    staged, sems = refs[: len(lead)], refs[len(lead)]
    column = lax.axis_index("wide") // plan.grid_rows
    block = plan.block
    run_all(
        [
            pltpu.make_async_copy(
                panel.at[0, :, at(cc * GRID_COLS + jnp.bitwise_xor(column, o), block)],
                staged[i].at[:, pl.ds(cc * block, block)],
                sems.at[i, cc],
            )
            for i, o in enumerate(lead)
            for cc in range(plan.col_groups)
        ]
    )


def put_tag(plan, chosen, o, out):
    chosen = chosen.astype(jnp.float32)
    tag = jnp.full((TAG, plan.width), chosen, jnp.float32).astype(jnp.bfloat16)
    out[plan.early[o] * plan.block :, :] = tag


def pack_kernel(plan, lead, *refs):
    groups, count = plan.groups, len(lead)
    head_refs, staged, refs = refs[:groups], refs[groups : groups + count], refs[groups + count :]
    outs, (touched_out, order) = refs[:count], refs[count:]
    block = plan.block
    touched = touched_rows(plan, head_refs)
    touched_out[0] = touched
    chosen = first_rows(plan, touched, [plan.early[o] for o in lead], order)
    for i, o in enumerate(lead):
        for k in range(plan.early[o]):
            outs[i][pl.ds(k * block, block), :] = staged[i][at(order[k], block), :]
        put_tag(plan, chosen[i], o, outs[i])


def bucket_kernel(plan, tail, heads, *refs):
    touched_ref, refs = (refs[0], refs[1:]) if tail else (None, refs)
    updates, panel, refs = refs[0], refs[1], refs[2:]
    count = (plan.groups - 1) * plan.capacity
    outs, packed, refs = refs[:count], refs[count : count + len(tail)], refs[count + len(tail) :]
    order, slot_sems, sems = refs
    me = lax.axis_index("front")
    column = lax.axis_index("wide") // plan.grid_rows
    block = plan.block

    def buckets(act):
        for k in range(1, plan.groups):
            target = lax.rem(me + k, plan.groups)
            rank = jnp.int32(0)
            for q in range(plan.slots):
                named, _ = own_row(plan, heads, q, target)
                for c in range(plan.capacity):

                    @pl.when(jnp.logical_and(named, rank == c))
                    def _():
                        act(
                            pltpu.make_async_copy(
                                updates.at[0, pl.ds(q * block, block)],
                                outs[(k - 1) * plan.capacity + c],
                                slot_sems.at[q],
                            )
                        )

                rank = rank + jnp.where(named, 1, 0)

    buckets(lambda c: c.start())
    copies = []
    if tail:
        touched = touched_ref[0]
        chosen = first_rows(plan, touched, [plan.early[o] for o in tail], order)
        for i, o in enumerate(tail):
            target = jnp.bitwise_xor(column, o)
            for k in range(plan.early[o]):
                for cc in range(plan.col_groups):
                    copies.append(
                        pltpu.make_async_copy(
                            panel.at[0, at(order[k], block), at(cc * GRID_COLS + target, block)],
                            packed[i].at[pl.ds(k * block, block), pl.ds(cc * block, block)],
                            sems.at[i, k, cc],
                        )
                    )
                    copies[-1].start()
            put_tag(plan, chosen[i], o, packed[i])
    for copy in copies:
        copy.wait()
    buckets(lambda c: c.wait())


def assemble_kernel(plan, *refs):
    groups, block = plan.groups, plan.block
    head_refs, refs = refs[:groups], refs[groups:]
    code_refs, refs = refs[:groups], refs[groups:]
    panel, updates, refs = refs[0], refs[1], refs[2:]
    count = (groups - 1) * plan.capacity
    got, refs = refs[:count], refs[count:]
    outs, refs = refs[: len(plan.late)], refs[len(plan.late) :]
    total, raw, moved, place_ref, row_sems, slot_sems = refs
    me = lax.axis_index("front")
    column = lax.axis_index("wide") // plan.grid_rows

    slot_copies = [
        pltpu.make_async_copy(
            updates.at[0, pl.ds(q * block, block)], moved.at[q], slot_sems.at[q]
        )
        for q in range(plan.slots)
    ]
    for k in range(1, groups):
        for c in range(plan.capacity):
            part = (k - 1) * plan.capacity + c
            index = plan.slots + part
            slot_copies.append(
                pltpu.make_async_copy(got[part], moved.at[index], slot_sems.at[index])
            )
    row_copies = [
        pltpu.make_async_copy(panel.at[0, pl.ds(t * block, block)], raw.at[t], row_sems.at[t])
        for t in range(plan.rows)
    ]
    for copy in row_copies + slot_copies:
        copy.start()

    touched = touched_rows(plan, head_refs)
    limits = list(plan.early.values())
    for o, chosen in zip(plan.early, first_rows(plan, touched, limits)):
        for t, (bit, place) in enumerate(positions(plan, chosen)):
            place_ref[o, t] = jnp.where(bit == 1, -1, place)

    for t in range(plan.rows):
        row_copies[t].wait()
    for copy in slot_copies:
        copy.wait()

    def widen(t, carry):
        total[t] = raw[t].astype(jnp.float32)
        return carry

    lax.fori_loop(0, plan.rows, widen, 0)

    for s, (heads, codes) in enumerate(zip(head_refs, code_refs)):

        def add_slot(q, rank):
            named, t = own_row(plan, heads, q, me)
            index = q if s == 0 else plan.slots + (s - 1) * plan.capacity + rank

            @pl.when(named)
            def _():
                for j in range(plan.columns):
                    code = codes[q, j]
                    col = code % plan.window

                    @pl.when(code >= plan.window)
                    def _():
                        where = at(col, block)
                        total[t, :, where] += moved[
                            index, :, pl.ds(j * block, block)
                        ].astype(jnp.float32)

            return rank + jnp.where(named, 1, 0)

        lax.fori_loop(0, plan.slots, add_slot, jnp.int32(0))

    def pack(t, carry):
        for ref, (o, lo, hi) in zip(outs, plan.late):
            target = jnp.bitwise_xor(column, o)

            def put(row):
                for cc in range(plan.col_groups):
                    ref[at(row, block), pl.ds(cc * block, block)] = total[
                        t, :, at(cc * GRID_COLS + target, block)
                    ].astype(jnp.bfloat16)

            if hi - lo == plan.rows:
                put(t)
            else:
                place = place_ref[o, t] if plan.early.get(o) else t
                pl.when(jnp.logical_and(place >= lo, place < hi))(lambda: put(place - lo))

        return carry

    lax.fori_loop(0, plan.rows, pack, 0)


def place_early_kernel(plan, offsets, *refs):
    count = len(offsets)
    pieces, out, sets, refs = refs[:count], refs[count], refs[count + 1], refs[count + 2 :]
    tags, where, tag_sems, sems = refs
    column = lax.axis_index("wide") // plan.grid_rows
    block = plan.block
    run_all(
        [
            pltpu.make_async_copy(
                pieces[i].at[pl.ds(plan.early[o] * block, TAG)], tags.at[i], tag_sems.at[i]
            )
            for i, o in enumerate(offsets)
        ]
    )
    copies = []
    for i, o in enumerate(offsets):
        source = jnp.bitwise_xor(column, o)
        chosen = jnp.max(tags[i].astype(jnp.float32)).astype(jnp.int32)
        sets[i] = chosen
        list_rows(plan, chosen, 1, where.at[i])
        for k in range(plan.early[o]):
            copies.append(
                pltpu.make_async_copy(
                    pieces[i].at[pl.ds(k * block, block)],
                    out.at[where[i, k], source],
                    sems.at[i, k],
                )
            )
            copies[-1].start()
    for copy in copies:
        copy.wait()


def place_late_kernel(plan, messages, early, sets, pieces, out, held, where, set_sem, sems):
    column = lax.axis_index("wide") // plan.grid_rows
    block = plan.block
    copies = []

    def place(i, rows):
        o, lo, hi = messages[i]
        source = jnp.bitwise_xor(column, o)
        if rows is None:
            moves = [(pieces[i], out.at[pl.ds(lo, hi - lo), source])]
        else:
            moves = [(pieces[i].at[k - lo], out.at[rows[k], source]) for k in range(lo, hi)]
        for k, (src, dst) in enumerate(moves):
            copies.append(pltpu.make_async_copy(src, dst, sems.at[i, k]))
            copies[-1].start()

    split = [i for i, m in enumerate(messages) if m[0] in early]
    if split:
        fetch = pltpu.make_async_copy(sets, held, set_sem)
        fetch.start()
    for i in range(len(messages)):
        if i not in split:
            place(i, None)
    if split:
        fetch.wait()
    for i in split:
        list_rows(plan, held[early.index(messages[i][0])], 0, where.at[i])
        place(i, where.at[i])
    for copy in copies:
        copy.wait()


def after(value, *others):
    return lax.optimization_barrier((value, *others))[0]


def across(value, plan, offset):
    pairs = [
        (c * plan.grid_rows + r, (c ^ offset) * plan.grid_rows + r)
        for c in range(GRID_COLS)
        for r in range(plan.grid_rows)
    ]
    return lax.ppermute(value, "wide", pairs)


def along(value, plan, steps):
    return lax.ppermute(
        value, "front", [(f, (f + steps) % plan.groups) for f in range(plan.groups)]
    )


def local(updates, parent_panels, slot_parent, slot_row, slot_cols, slot_mask):
    plan = Plan(updates, parent_panels, slot_cols)
    block, width = plan.block, plan.width
    bf16 = jnp.bfloat16
    heads = slot_parent[0, :, 0] * plan.rows + slot_row[0]
    all_heads = [heads] + [along(heads, plan, k) for k in range(1, plan.groups)]
    codes = slot_mask[0] * plan.window + slot_cols[0]
    panels = pltpu.with_memory_space_constraint(parent_panels, pltpu.HBM)
    moving = pltpu.with_memory_space_constraint(updates, pltpu.HBM)


    early = [o for o in plan.early if plan.early[o]]
    lead, tail = early[:2], early[2:]
    packed, touched = {}, []

    def early_shape(o):
        return jax.ShapeDtypeStruct((plan.early[o] * block + TAG, width), bf16)

    if lead:
        staged = pl.pallas_call(
            functools.partial(stage_kernel, plan, lead),
            out_shape=[jax.ShapeDtypeStruct((plan.rows * block, width), bf16) for _ in lead],
            in_specs=[HBM],
            out_specs=[VMEM] * len(lead),
            scratch_shapes=[pltpu.SemaphoreType.DMA((len(lead), plan.col_groups))],
            compiler_params=params(),
            cost_estimate=COST,
            name="stage",
        )(panels)
        *outs, touched_set = pl.pallas_call(
            functools.partial(pack_kernel, plan, lead),
            out_shape=[early_shape(o) for o in lead] + [jax.ShapeDtypeStruct((1,), jnp.int32)],
            in_specs=[SMEM] * plan.groups + [VMEM] * len(lead),
            out_specs=[VMEM] * len(lead) + [SMEM],
            scratch_shapes=[pltpu.SMEM((plan.rows,), jnp.int32)],
            compiler_params=params(),
            cost_estimate=COST,
            name="pack_early",
        )(*all_heads, *staged)
        packed = dict(zip(lead, outs))
        touched = [touched_set]

    count = (plan.groups - 1) * plan.capacity
    outs = pl.pallas_call(
        functools.partial(bucket_kernel, plan, tail),
        out_shape=[jax.ShapeDtypeStruct((block, updates.shape[2]), bf16)] * count
        + [early_shape(o) for o in tail],
        in_specs=[SMEM] * (1 + len(touched)) + [HBM, HBM],
        out_specs=[VMEM] * (count + len(tail)),
        scratch_shapes=[
            pltpu.SMEM((plan.rows,), jnp.int32),
            pltpu.SemaphoreType.DMA((plan.slots,)),
            pltpu.SemaphoreType.DMA((max(1, len(tail)), max(1, plan.first), plan.col_groups)),
        ],
        compiler_params=params(),
        cost_estimate=COST,
        name="bucket",
    )(heads, *touched, moving, panels)
    packed.update(zip(tail, outs[count:]))

    all_codes = [after(codes, *touched)]
    all_codes += [along(all_codes[0], plan, k) for k in range(1, plan.groups)]
    got = [
        along(outs[(k - 1) * plan.capacity + c], plan, k)
        for k in range(1, plan.groups)
        for c in range(plan.capacity)
    ]

    moved = plan.slots + (plan.groups - 1) * plan.capacity
    assembled = pl.pallas_call(
        functools.partial(assemble_kernel, plan),
        out_shape=[
            jax.ShapeDtypeStruct(((hi - lo) * block, width), bf16) for o, lo, hi in plan.late
        ],
        in_specs=[SMEM] * (2 * plan.groups) + [HBM, HBM] + [ANY] * len(got),
        out_specs=[VMEM] * len(plan.late),
        scratch_shapes=[
            pltpu.VMEM((plan.rows, block, parent_panels.shape[2]), jnp.float32),
            pltpu.VMEM((plan.rows, block, parent_panels.shape[2]), bf16),
            pltpu.VMEM((moved, block, updates.shape[2]), bf16),
            pltpu.SMEM((GRID_COLS, plan.rows), jnp.int32),
            pltpu.SemaphoreType.DMA((plan.rows,)),
            pltpu.SemaphoreType.DMA((moved,)),
        ],
        compiler_params=params(),
        cost_estimate=COST,
        name="assemble",
    )(*all_heads, *all_codes, panels, moving, *got)

    ready = dict(zip(plan.late, assembled))

    def late(o, part=0):
        return [m for m in plan.late if m[0] == o][part]

    arrived = {late(0): ready[late(0)]}

    def send(message, *others):
        arrived[message] = across(after(ready[message], *others), plan, message[0])
        return arrived[message]

    first = {}

    def send_early(o, *others):
        if o in packed:
            first[o] = across(after(packed[o], *others), plan, o)

    def came(*offsets):
        return [first[o] for o in offsets if o in first]

    send_early(4)
    send_early(5)
    send_early(7, *came(4), *all_codes[1:])
    b5 = send(late(5), *came(5))
    b7 = send(late(7), *came(7))
    send(late(6), b5)
    send(late(4), b7)
    n1 = send(late(1), *came(5))
    send(late(2), *came(7))
    send(late(3, 0), n1)
    send(late(3, 1), b7)

    out_shape = jax.ShapeDtypeStruct((plan.rows, GRID_COLS, block, width), bf16)
    held, sets = [], []
    if early:
        out, sets = pl.pallas_call(
            functools.partial(place_early_kernel, plan, early),
            out_shape=[out_shape, jax.ShapeDtypeStruct((len(early),), jnp.int32)],
            in_specs=[ANY] * len(early),
            out_specs=[HBM, SMEM],
            scratch_shapes=[
                pltpu.VMEM((len(early), TAG, width), bf16),
                pltpu.SMEM((len(early), plan.rows), jnp.int32),
                pltpu.SemaphoreType.DMA((len(early),)),
                pltpu.SemaphoreType.DMA((len(early), plan.first)),
            ],
            compiler_params=params(),
            cost_estimate=COST,
            name="place_early",
        )(*[first[o] for o in early])
        held, sets = [out], [sets]

    def place(held, messages, name):
        known = sets if any(m[0] in early for m in messages) else []

        def body(*refs):
            refs = list(refs)[len(held) :]
            sets_ref = refs.pop(0) if known else None
            count = len(messages)
            place_late_kernel(plan, messages, early, sets_ref, refs[:count], *refs[count:])

        return [
            pl.pallas_call(
                body,
                out_shape=out_shape,
                in_specs=[HBM] * len(held) + [ANY] * (len(known) + len(messages)),
                out_specs=HBM,
                input_output_aliases={0: 0} if held else {},
                scratch_shapes=[
                    pltpu.SMEM((max(1, len(early)),), jnp.int32),
                    pltpu.SMEM((len(messages), plan.rows), jnp.int32),
                    pltpu.SemaphoreType.DMA,
                    pltpu.SemaphoreType.DMA((len(messages), plan.rows)),
                ],
                compiler_params=params(),
                cost_estimate=MID if name == "place_mid" else COST,
                name=name,
            )(*held, *known, *[arrived[m].reshape(-1, block, width) for m in messages])
        ]

    last = [late(6), late(4)]
    held = place(held, [m for m in plan.late if m not in last], "place_mid")
    for m in last:
        held = place(held, [m], "place_last%d" % m[0])
    return held[0].reshape(1, plan.rows * GRID_COLS * block, width)


def solution(mesh):
    return jax.shard_map(
        local,
        mesh=mesh,
        in_specs=(
            P("front", "wide", None),
            P("front", "wide", None),
            P("front", "wide", None),
            P("front", "wide"),
            P("front", "wide", None),
            P("front", "wide", None),
        ),
        out_specs=P("front", "wide", None),
        check_vma=False,
    )
```

```python
import functools

import jax
import jax.numpy as jnp
from jax import lax
from jax.experimental import pallas as pl
from jax.experimental.pallas import tpu as pltpu
from jax.sharding import PartitionSpec as P

GRID_COLS = 8
NEAR = GRID_COLS // 2
TAG = 8

ANY = pl.BlockSpec(memory_space=pl.ANY)
HBM = pl.BlockSpec(memory_space=pltpu.HBM)
SMEM = pl.BlockSpec(memory_space=pltpu.SMEM)
VMEM = pl.BlockSpec(memory_space=pltpu.VMEM)


class Plan:
    def __init__(self, updates, panels, slot_cols):
        self.groups = lax.axis_size("front")
        self.lanes = lax.axis_size("wide")
        self.grid_rows = self.lanes // GRID_COLS
        self.slots = slot_cols.shape[1]
        self.columns = slot_cols.shape[2]
        self.block = updates.shape[1] // self.slots
        self.rows = panels.shape[1] // self.block
        self.window = panels.shape[2] // self.block
        self.col_groups = self.window // GRID_COLS
        self.width = self.col_groups * self.block
        self.capacity = max(self.slots // 4, self.slots // self.groups)
        self.first = max(0, self.rows - self.capacity * self.groups)
        self.early = {6: self.first // 2, 5: self.first, 7: self.first}
        self.late = []
        for o in range(GRID_COLS):
            count = self.rows - self.early.get(o, 0)
            cuts = [0, count // 2, count] if o == 3 else [0, count]
            self.late += [(o, lo, hi) for lo, hi in zip(cuts, cuts[1:]) if lo < hi]


MID = pl.CostEstimate(flops=0, transcendentals=0, bytes_accessed=0)
COST = pl.CostEstimate(flops=0, transcendentals=0, bytes_accessed=0)


def params():
    return pltpu.CompilerParams(vmem_limit_bytes=48 << 20)


def at(start, size):
    return pl.ds(pl.multiple_of(start * size, size), size)


def own_row(plan, heads, q, front):
    row = heads[q] - front * plan.rows
    return jnp.logical_and(row >= 0, row < plan.rows), row


def touched_rows(plan, head_refs):
    me = lax.axis_index("front")
    touched = jnp.int32(0)
    for heads in head_refs:
        for q in range(plan.slots):
            named, row = own_row(plan, heads, q, me)
            bit = jnp.left_shift(jnp.int32(1), jnp.where(named, row, 0))
            touched = touched | jnp.where(named, bit, 0)
    return touched


def first_rows(plan, touched, limits, order=None):
    chosen, count = [jnp.int32(0) for _ in limits], jnp.int32(0)
    for t in range(plan.rows):
        free = 1 - (jnp.right_shift(touched, t) & 1)
        chosen = [c | jnp.where(count < n, free << t, 0) for c, n in zip(chosen, limits)]
        if order is not None:
            order[count] = t
        count = count + free
    return chosen


def positions(plan, chosen):
    out, count = [], jnp.int32(0)
    for t in range(plan.rows):
        bit = jnp.right_shift(chosen, t) & 1
        out.append((bit, jnp.where(bit == 1, count, t - count)))
        count = count + bit
    return out


def list_rows(plan, chosen, bit_wanted, where):
    for t, (bit, place) in enumerate(positions(plan, chosen)):

        @pl.when(bit == bit_wanted)
        def _():
            where[place] = t


def run_all(copies):
    for copy in copies:
        copy.start()
    for copy in copies:
        copy.wait()


def stage_kernel(plan, lead, panel, *refs):
    staged, sems = refs[: len(lead)], refs[len(lead)]
    column = lax.axis_index("wide") // plan.grid_rows
    block = plan.block
    run_all(
        [
            pltpu.make_async_copy(
                panel.at[0, :, at(cc * GRID_COLS + jnp.bitwise_xor(column, o), block)],
                staged[i].at[:, pl.ds(cc * block, block)],
                sems.at[i, cc],
            )
            for i, o in enumerate(lead)
            for cc in range(plan.col_groups)
        ]
    )


def put_tag(plan, chosen, o, out):
    chosen = chosen.astype(jnp.float32)
    tag = jnp.full((TAG, plan.width), chosen, jnp.float32).astype(jnp.bfloat16)
    out[plan.early[o] * plan.block :, :] = tag


def pack_kernel(plan, lead, *refs):
    groups, count = plan.groups, len(lead)
    head_refs, staged, refs = refs[:groups], refs[groups : groups + count], refs[groups + count :]
    outs, (touched_out, order) = refs[:count], refs[count:]
    block = plan.block
    touched = touched_rows(plan, head_refs)
    touched_out[0] = touched
    chosen = first_rows(plan, touched, [plan.early[o] for o in lead], order)
    for i, o in enumerate(lead):
        for k in range(plan.early[o]):
            outs[i][pl.ds(k * block, block), :] = staged[i][at(order[k], block), :]
        put_tag(plan, chosen[i], o, outs[i])


def bucket_kernel(plan, tail, heads, *refs):
    touched_ref, refs = (refs[0], refs[1:]) if tail else (None, refs)
    updates, panel, refs = refs[0], refs[1], refs[2:]
    count = (plan.groups - 1) * plan.capacity
    outs, packed, refs = refs[:count], refs[count : count + len(tail)], refs[count + len(tail) :]
    order, slot_sems, sems = refs
    me = lax.axis_index("front")
    column = lax.axis_index("wide") // plan.grid_rows
    block = plan.block

    def buckets(act):
        for k in range(1, plan.groups):
            target = lax.rem(me + k, plan.groups)
            rank = jnp.int32(0)
            for q in range(plan.slots):
                named, _ = own_row(plan, heads, q, target)
                for c in range(plan.capacity):

                    @pl.when(jnp.logical_and(named, rank == c))
                    def _():
                        act(
                            pltpu.make_async_copy(
                                updates.at[0, pl.ds(q * block, block)],
                                outs[(k - 1) * plan.capacity + c],
                                slot_sems.at[q],
                            )
                        )

                rank = rank + jnp.where(named, 1, 0)

    buckets(lambda c: c.start())
    copies = []
    if tail:
        touched = touched_ref[0]
        chosen = first_rows(plan, touched, [plan.early[o] for o in tail], order)
        for i, o in enumerate(tail):
            target = jnp.bitwise_xor(column, o)
            for k in range(plan.early[o]):
                for cc in range(plan.col_groups):
                    copies.append(
                        pltpu.make_async_copy(
                            panel.at[0, at(order[k], block), at(cc * GRID_COLS + target, block)],
                            packed[i].at[pl.ds(k * block, block), pl.ds(cc * block, block)],
                            sems.at[i, k, cc],
                        )
                    )
                    copies[-1].start()
            put_tag(plan, chosen[i], o, packed[i])
    for copy in copies:
        copy.wait()
    buckets(lambda c: c.wait())


def assemble_kernel(plan, *refs):
    groups, block = plan.groups, plan.block
    head_refs, refs = refs[:groups], refs[groups:]
    code_refs, refs = refs[:groups], refs[groups:]
    panel, updates, refs = refs[0], refs[1], refs[2:]
    count = (groups - 1) * plan.capacity
    got, refs = refs[:count], refs[count:]
    outs, refs = refs[: len(plan.late)], refs[len(plan.late) :]
    total, raw, moved, place_ref, row_sems, slot_sems = refs
    me = lax.axis_index("front")
    column = lax.axis_index("wide") // plan.grid_rows

    slot_copies = [
        pltpu.make_async_copy(
            updates.at[0, pl.ds(q * block, block)], moved.at[q], slot_sems.at[q]
        )
        for q in range(plan.slots)
    ]
    for k in range(1, groups):
        for c in range(plan.capacity):
            part = (k - 1) * plan.capacity + c
            index = plan.slots + part
            slot_copies.append(
                pltpu.make_async_copy(got[part], moved.at[index], slot_sems.at[index])
            )
    row_copies = [
        pltpu.make_async_copy(panel.at[0, pl.ds(t * block, block)], raw.at[t], row_sems.at[t])
        for t in range(plan.rows)
    ]
    for copy in row_copies + slot_copies:
        copy.start()

    touched = touched_rows(plan, head_refs)
    limits = list(plan.early.values())
    for o, chosen in zip(plan.early, first_rows(plan, touched, limits)):
        for t, (bit, place) in enumerate(positions(plan, chosen)):
            place_ref[o, t] = jnp.where(bit == 1, -1, place)

    for t in range(plan.rows):
        row_copies[t].wait()
    for copy in slot_copies:
        copy.wait()

    def widen(t, carry):
        total[t] = raw[t].astype(jnp.float32)
        return carry

    lax.fori_loop(0, plan.rows, widen, 0)

    for s, (heads, codes) in enumerate(zip(head_refs, code_refs)):

        def add_slot(q, rank):
            named, t = own_row(plan, heads, q, me)
            index = q if s == 0 else plan.slots + (s - 1) * plan.capacity + rank

            @pl.when(named)
            def _():
                for j in range(plan.columns):
                    code = codes[q, j]
                    col = code % plan.window

                    @pl.when(code >= plan.window)
                    def _():
                        where = at(col, block)
                        total[t, :, where] += moved[
                            index, :, pl.ds(j * block, block)
                        ].astype(jnp.float32)

            return rank + jnp.where(named, 1, 0)

        lax.fori_loop(0, plan.slots, add_slot, jnp.int32(0))

    def pack(t, carry):
        for ref, (o, lo, hi) in zip(outs, plan.late):
            target = jnp.bitwise_xor(column, o)

            def put(row):
                for cc in range(plan.col_groups):
                    ref[at(row, block), pl.ds(cc * block, block)] = total[
                        t, :, at(cc * GRID_COLS + target, block)
                    ].astype(jnp.bfloat16)

            if hi - lo == plan.rows:
                put(t)
            else:
                place = place_ref[o, t] if plan.early.get(o) else t
                pl.when(jnp.logical_and(place >= lo, place < hi))(lambda: put(place - lo))

        return carry

    lax.fori_loop(0, plan.rows, pack, 0)


def place_early_kernel(plan, offsets, *refs):
    count = len(offsets)
    pieces, out, sets, refs = refs[:count], refs[count], refs[count + 1], refs[count + 2 :]
    tags, where, tag_sems, sems = refs
    column = lax.axis_index("wide") // plan.grid_rows
    block = plan.block
    run_all(
        [
            pltpu.make_async_copy(
                pieces[i].at[pl.ds(plan.early[o] * block, TAG)], tags.at[i], tag_sems.at[i]
            )
            for i, o in enumerate(offsets)
        ]
    )
    copies = []
    for i, o in enumerate(offsets):
        source = jnp.bitwise_xor(column, o)
        chosen = jnp.max(tags[i].astype(jnp.float32)).astype(jnp.int32)
        sets[i] = chosen
        list_rows(plan, chosen, 1, where.at[i])
        for k in range(plan.early[o]):
            copies.append(
                pltpu.make_async_copy(
                    pieces[i].at[pl.ds(k * block, block)],
                    out.at[where[i, k], source],
                    sems.at[i, k],
                )
            )
            copies[-1].start()
    for copy in copies:
        copy.wait()


def place_late_kernel(plan, messages, early, sets, pieces, out, held, where, set_sem, sems):
    column = lax.axis_index("wide") // plan.grid_rows
    block = plan.block
    copies = []

    def place(i, rows):
        o, lo, hi = messages[i]
        source = jnp.bitwise_xor(column, o)
        if rows is None:
            moves = [(pieces[i], out.at[pl.ds(lo, hi - lo), source])]
        else:
            moves = [(pieces[i].at[k - lo], out.at[rows[k], source]) for k in range(lo, hi)]
        for k, (src, dst) in enumerate(moves):
            copies.append(pltpu.make_async_copy(src, dst, sems.at[i, k]))
            copies[-1].start()

    split = [i for i, m in enumerate(messages) if m[0] in early]
    if split:
        fetch = pltpu.make_async_copy(sets, held, set_sem)
        fetch.start()
    for i in range(len(messages)):
        if i not in split:
            place(i, None)
    if split:
        fetch.wait()
    for i in split:
        list_rows(plan, held[early.index(messages[i][0])], 0, where.at[i])
        place(i, where.at[i])
    for copy in copies:
        copy.wait()


def after(value, *others):
    return lax.optimization_barrier((value, *others))[0]


def across(value, plan, offset):
    pairs = [
        (c * plan.grid_rows + r, (c ^ offset) * plan.grid_rows + r)
        for c in range(GRID_COLS)
        for r in range(plan.grid_rows)
    ]
    return lax.ppermute(value, "wide", pairs)


def along(value, plan, steps):
    return lax.ppermute(
        value, "front", [(f, (f + steps) % plan.groups) for f in range(plan.groups)]
    )


def local(updates, parent_panels, slot_parent, slot_row, slot_cols, slot_mask):
    plan = Plan(updates, parent_panels, slot_cols)
    block, width = plan.block, plan.width
    bf16 = jnp.bfloat16
    heads = slot_parent[0, :, 0] * plan.rows + slot_row[0]
    all_heads = [heads] + [along(heads, plan, k) for k in range(1, plan.groups)]
    codes = slot_mask[0] * plan.window + slot_cols[0]
    panels = pltpu.with_memory_space_constraint(parent_panels, pltpu.HBM)
    moving = pltpu.with_memory_space_constraint(updates, pltpu.HBM)


    early = [o for o in plan.early if plan.early[o]]
    lead, tail = early[:2], early[2:]
    packed, touched = {}, []

    def early_shape(o):
        return jax.ShapeDtypeStruct((plan.early[o] * block + TAG, width), bf16)

    if lead:
        staged = pl.pallas_call(
            functools.partial(stage_kernel, plan, lead),
            out_shape=[jax.ShapeDtypeStruct((plan.rows * block, width), bf16) for _ in lead],
            in_specs=[HBM],
            out_specs=[VMEM] * len(lead),
            scratch_shapes=[pltpu.SemaphoreType.DMA((len(lead), plan.col_groups))],
            compiler_params=params(),
            cost_estimate=COST,
            name="stage",
        )(panels)
        *outs, touched_set = pl.pallas_call(
            functools.partial(pack_kernel, plan, lead),
            out_shape=[early_shape(o) for o in lead] + [jax.ShapeDtypeStruct((1,), jnp.int32)],
            in_specs=[SMEM] * plan.groups + [VMEM] * len(lead),
            out_specs=[VMEM] * len(lead) + [SMEM],
            scratch_shapes=[pltpu.SMEM((plan.rows,), jnp.int32)],
            compiler_params=params(),
            cost_estimate=COST,
            name="pack_early",
        )(*all_heads, *staged)
        packed = dict(zip(lead, outs))
        touched = [touched_set]

    count = (plan.groups - 1) * plan.capacity
    outs = pl.pallas_call(
        functools.partial(bucket_kernel, plan, tail),
        out_shape=[jax.ShapeDtypeStruct((block, updates.shape[2]), bf16)] * count
        + [early_shape(o) for o in tail],
        in_specs=[SMEM] * (1 + len(touched)) + [HBM, HBM],
        out_specs=[VMEM] * (count + len(tail)),
        scratch_shapes=[
            pltpu.SMEM((plan.rows,), jnp.int32),
            pltpu.SemaphoreType.DMA((plan.slots,)),
            pltpu.SemaphoreType.DMA((max(1, len(tail)), max(1, plan.first), plan.col_groups)),
        ],
        compiler_params=params(),
        cost_estimate=COST,
        name="bucket",
    )(heads, *touched, moving, panels)
    packed.update(zip(tail, outs[count:]))

    all_codes = [after(codes, *touched)]
    all_codes += [along(all_codes[0], plan, k) for k in range(1, plan.groups)]
    got = [
        along(outs[(k - 1) * plan.capacity + c], plan, k)
        for k in range(1, plan.groups)
        for c in range(plan.capacity)
    ]

    moved = plan.slots + (plan.groups - 1) * plan.capacity
    assembled = pl.pallas_call(
        functools.partial(assemble_kernel, plan),
        out_shape=[
            jax.ShapeDtypeStruct(((hi - lo) * block, width), bf16) for o, lo, hi in plan.late
        ],
        in_specs=[SMEM] * (2 * plan.groups) + [HBM, HBM] + [ANY] * len(got),
        out_specs=[VMEM] * len(plan.late),
        scratch_shapes=[
            pltpu.VMEM((plan.rows, block, parent_panels.shape[2]), jnp.float32),
            pltpu.VMEM((plan.rows, block, parent_panels.shape[2]), bf16),
            pltpu.VMEM((moved, block, updates.shape[2]), bf16),
            pltpu.SMEM((GRID_COLS, plan.rows), jnp.int32),
            pltpu.SemaphoreType.DMA((plan.rows,)),
            pltpu.SemaphoreType.DMA((moved,)),
        ],
        compiler_params=params(),
        cost_estimate=COST,
        name="assemble",
    )(*all_heads, *all_codes, panels, moving, *got)

    ready = dict(zip(plan.late, assembled))

    def late(o, part=0):
        return [m for m in plan.late if m[0] == o][part]

    arrived = {late(0): ready[late(0)]}

    def send(message, *others):
        arrived[message] = across(after(ready[message], *others), plan, message[0])
        return arrived[message]

    first = {}

    def send_early(o, *others):
        if o in packed:
            first[o] = across(after(packed[o], *others), plan, o)

    def came(*offsets):
        return [first[o] for o in offsets if o in first]

    send_early(6)
    send_early(5)
    send_early(7, *came(6), *all_codes[1:])
    b5 = send(late(5), *came(5))
    b7 = send(late(7), *came(7))
    send(late(4), b5)
    send(late(6), b7)
    n1 = send(late(1), *came(5))
    send(late(2), *came(7))
    send(late(3, 0), n1)
    send(late(3, 1), b7)

    out_shape = jax.ShapeDtypeStruct((plan.rows, GRID_COLS, block, width), bf16)
    held, sets = [], []
    if early:
        out, sets = pl.pallas_call(
            functools.partial(place_early_kernel, plan, early),
            out_shape=[out_shape, jax.ShapeDtypeStruct((len(early),), jnp.int32)],
            in_specs=[ANY] * len(early),
            out_specs=[HBM, SMEM],
            scratch_shapes=[
                pltpu.VMEM((len(early), TAG, width), bf16),
                pltpu.SMEM((len(early), plan.rows), jnp.int32),
                pltpu.SemaphoreType.DMA((len(early),)),
                pltpu.SemaphoreType.DMA((len(early), plan.first)),
            ],
            compiler_params=params(),
            cost_estimate=COST,
            name="place_early",
        )(*[first[o] for o in early])
        held, sets = [out], [sets]

    def place(held, messages, name):
        known = sets if any(m[0] in early for m in messages) else []

        def body(*refs):
            refs = list(refs)[len(held) :]
            sets_ref = refs.pop(0) if known else None
            count = len(messages)
            place_late_kernel(plan, messages, early, sets_ref, refs[:count], *refs[count:])

        return [
            pl.pallas_call(
                body,
                out_shape=out_shape,
                in_specs=[HBM] * len(held) + [ANY] * (len(known) + len(messages)),
                out_specs=HBM,
                input_output_aliases={0: 0} if held else {},
                scratch_shapes=[
                    pltpu.SMEM((max(1, len(early)),), jnp.int32),
                    pltpu.SMEM((len(messages), plan.rows), jnp.int32),
                    pltpu.SemaphoreType.DMA,
                    pltpu.SemaphoreType.DMA((len(messages), plan.rows)),
                ],
                compiler_params=params(),
                cost_estimate=MID if name == "place_mid" else COST,
                name=name,
            )(*held, *known, *[arrived[m].reshape(-1, block, width) for m in messages])
        ]

    last = [late(6), late(4)]
    held = place(held, [m for m in plan.late if m not in last], "place_mid")
    for m in last:
        held = place(held, [m], "place_last%d" % m[0])
    return held[0].reshape(1, plan.rows * GRID_COLS * block, width)


def solution(mesh):
    return jax.shard_map(
        local,
        mesh=mesh,
        in_specs=(
            P("front", "wide", None),
            P("front", "wide", None),
            P("front", "wide", None),
            P("front", "wide"),
            P("front", "wide", None),
            P("front", "wide", None),
        ),
        out_specs=P("front", "wide", None),
        check_vma=False,
    )
```

```python
import functools

import jax
import jax.numpy as jnp
from jax import lax
from jax.experimental import pallas as pl
from jax.experimental.pallas import tpu as pltpu
from jax.sharding import PartitionSpec as P

GRID_COLS = 8
NEAR = GRID_COLS // 2
TAG = 8

ANY = pl.BlockSpec(memory_space=pl.ANY)
HBM = pl.BlockSpec(memory_space=pltpu.HBM)
SMEM = pl.BlockSpec(memory_space=pltpu.SMEM)
VMEM = pl.BlockSpec(memory_space=pltpu.VMEM)


class Plan:
    def __init__(self, updates, panels, slot_cols):
        self.groups = lax.axis_size("front")
        self.lanes = lax.axis_size("wide")
        self.grid_rows = self.lanes // GRID_COLS
        self.slots = slot_cols.shape[1]
        self.columns = slot_cols.shape[2]
        self.block = updates.shape[1] // self.slots
        self.rows = panels.shape[1] // self.block
        self.window = panels.shape[2] // self.block
        self.col_groups = self.window // GRID_COLS
        self.width = self.col_groups * self.block
        self.capacity = max(self.slots // 4, self.slots // self.groups)
        self.first = max(0, self.rows - self.capacity * self.groups)
        self.early = {4: self.first // 2, 5: self.first, 7: self.first}
        self.late = []
        for o in range(GRID_COLS):
            count = self.rows - self.early.get(o, 0)
            cuts = [0, count // 2, count] if o == 1 else [0, count]
            self.late += [(o, lo, hi) for lo, hi in zip(cuts, cuts[1:]) if lo < hi]


MID = pl.CostEstimate(flops=0, transcendentals=0, bytes_accessed=0)
COST = pl.CostEstimate(flops=0, transcendentals=0, bytes_accessed=0)


def params():
    return pltpu.CompilerParams(vmem_limit_bytes=48 << 20)


def at(start, size):
    return pl.ds(pl.multiple_of(start * size, size), size)


def own_row(plan, heads, q, front):
    row = heads[q] - front * plan.rows
    return jnp.logical_and(row >= 0, row < plan.rows), row


def touched_rows(plan, head_refs):
    me = lax.axis_index("front")
    touched = jnp.int32(0)
    for heads in head_refs:
        for q in range(plan.slots):
            named, row = own_row(plan, heads, q, me)
            bit = jnp.left_shift(jnp.int32(1), jnp.where(named, row, 0))
            touched = touched | jnp.where(named, bit, 0)
    return touched


def first_rows(plan, touched, limits, order=None):
    chosen, count = [jnp.int32(0) for _ in limits], jnp.int32(0)
    for t in range(plan.rows):
        free = 1 - (jnp.right_shift(touched, t) & 1)
        chosen = [c | jnp.where(count < n, free << t, 0) for c, n in zip(chosen, limits)]
        if order is not None:
            order[count] = t
        count = count + free
    return chosen


def positions(plan, chosen):
    out, count = [], jnp.int32(0)
    for t in range(plan.rows):
        bit = jnp.right_shift(chosen, t) & 1
        out.append((bit, jnp.where(bit == 1, count, t - count)))
        count = count + bit
    return out


def list_rows(plan, chosen, bit_wanted, where):
    for t, (bit, place) in enumerate(positions(plan, chosen)):

        @pl.when(bit == bit_wanted)
        def _():
            where[place] = t


def run_all(copies):
    for copy in copies:
        copy.start()
    for copy in copies:
        copy.wait()


def stage_kernel(plan, lead, panel, *refs):
    staged, sems = refs[: len(lead)], refs[len(lead)]
    column = lax.axis_index("wide") // plan.grid_rows
    block = plan.block
    run_all(
        [
            pltpu.make_async_copy(
                panel.at[0, :, at(cc * GRID_COLS + jnp.bitwise_xor(column, o), block)],
                staged[i].at[:, pl.ds(cc * block, block)],
                sems.at[i, cc],
            )
            for i, o in enumerate(lead)
            for cc in range(plan.col_groups)
        ]
    )


def put_tag(plan, chosen, o, out):
    chosen = chosen.astype(jnp.float32)
    tag = jnp.full((TAG, plan.width), chosen, jnp.float32).astype(jnp.bfloat16)
    out[plan.early[o] * plan.block :, :] = tag


def pack_kernel(plan, lead, *refs):
    groups, count = plan.groups, len(lead)
    head_refs, staged, refs = refs[:groups], refs[groups : groups + count], refs[groups + count :]
    outs, (touched_out, order) = refs[:count], refs[count:]
    block = plan.block
    touched = touched_rows(plan, head_refs)
    touched_out[0] = touched
    chosen = first_rows(plan, touched, [plan.early[o] for o in lead], order)
    for i, o in enumerate(lead):
        for k in range(plan.early[o]):
            outs[i][pl.ds(k * block, block), :] = staged[i][at(order[k], block), :]
        put_tag(plan, chosen[i], o, outs[i])


def bucket_kernel(plan, tail, heads, *refs):
    touched_ref, refs = (refs[0], refs[1:]) if tail else (None, refs)
    updates, panel, refs = refs[0], refs[1], refs[2:]
    count = (plan.groups - 1) * plan.capacity
    outs, packed, refs = refs[:count], refs[count : count + len(tail)], refs[count + len(tail) :]
    order, slot_sems, sems = refs
    me = lax.axis_index("front")
    column = lax.axis_index("wide") // plan.grid_rows
    block = plan.block

    def buckets(act):
        for k in range(1, plan.groups):
            target = lax.rem(me + k, plan.groups)
            rank = jnp.int32(0)
            for q in range(plan.slots):
                named, _ = own_row(plan, heads, q, target)
                for c in range(plan.capacity):

                    @pl.when(jnp.logical_and(named, rank == c))
                    def _():
                        act(
                            pltpu.make_async_copy(
                                updates.at[0, pl.ds(q * block, block)],
                                outs[(k - 1) * plan.capacity + c],
                                slot_sems.at[q],
                            )
                        )

                rank = rank + jnp.where(named, 1, 0)

    buckets(lambda c: c.start())
    copies = []
    if tail:
        touched = touched_ref[0]
        chosen = first_rows(plan, touched, [plan.early[o] for o in tail], order)
        for i, o in enumerate(tail):
            target = jnp.bitwise_xor(column, o)
            for k in range(plan.early[o]):
                for cc in range(plan.col_groups):
                    copies.append(
                        pltpu.make_async_copy(
                            panel.at[0, at(order[k], block), at(cc * GRID_COLS + target, block)],
                            packed[i].at[pl.ds(k * block, block), pl.ds(cc * block, block)],
                            sems.at[i, k, cc],
                        )
                    )
                    copies[-1].start()
            put_tag(plan, chosen[i], o, packed[i])
    for copy in copies:
        copy.wait()
    buckets(lambda c: c.wait())


def assemble_kernel(plan, *refs):
    groups, block = plan.groups, plan.block
    head_refs, refs = refs[:groups], refs[groups:]
    code_refs, refs = refs[:groups], refs[groups:]
    panel, updates, refs = refs[0], refs[1], refs[2:]
    count = (groups - 1) * plan.capacity
    got, refs = refs[:count], refs[count:]
    outs, refs = refs[: len(plan.late)], refs[len(plan.late) :]
    total, raw, moved, place_ref, row_sems, slot_sems = refs
    me = lax.axis_index("front")
    column = lax.axis_index("wide") // plan.grid_rows

    slot_copies = [
        pltpu.make_async_copy(
            updates.at[0, pl.ds(q * block, block)], moved.at[q], slot_sems.at[q]
        )
        for q in range(plan.slots)
    ]
    for k in range(1, groups):
        for c in range(plan.capacity):
            part = (k - 1) * plan.capacity + c
            index = plan.slots + part
            slot_copies.append(
                pltpu.make_async_copy(got[part], moved.at[index], slot_sems.at[index])
            )
    row_copies = [
        pltpu.make_async_copy(panel.at[0, pl.ds(t * block, block)], raw.at[t], row_sems.at[t])
        for t in range(plan.rows)
    ]
    for copy in row_copies + slot_copies:
        copy.start()

    touched = touched_rows(plan, head_refs)
    limits = list(plan.early.values())
    for o, chosen in zip(plan.early, first_rows(plan, touched, limits)):
        for t, (bit, place) in enumerate(positions(plan, chosen)):
            place_ref[o, t] = jnp.where(bit == 1, -1, place)

    for t in range(plan.rows):
        row_copies[t].wait()
    for copy in slot_copies:
        copy.wait()

    def widen(t, carry):
        total[t] = raw[t].astype(jnp.float32)
        return carry

    lax.fori_loop(0, plan.rows, widen, 0)

    for s, (heads, codes) in enumerate(zip(head_refs, code_refs)):

        def add_slot(q, rank):
            named, t = own_row(plan, heads, q, me)
            index = q if s == 0 else plan.slots + (s - 1) * plan.capacity + rank

            @pl.when(named)
            def _():
                for j in range(plan.columns):
                    code = codes[q, j]
                    col = code % plan.window

                    @pl.when(code >= plan.window)
                    def _():
                        where = at(col, block)
                        total[t, :, where] += moved[
                            index, :, pl.ds(j * block, block)
                        ].astype(jnp.float32)

            return rank + jnp.where(named, 1, 0)

        lax.fori_loop(0, plan.slots, add_slot, jnp.int32(0))

    def pack(t, carry):
        for ref, (o, lo, hi) in zip(outs, plan.late):
            target = jnp.bitwise_xor(column, o)

            def put(row):
                for cc in range(plan.col_groups):
                    ref[at(row, block), pl.ds(cc * block, block)] = total[
                        t, :, at(cc * GRID_COLS + target, block)
                    ].astype(jnp.bfloat16)

            if hi - lo == plan.rows:
                put(t)
            else:
                place = place_ref[o, t] if plan.early.get(o) else t
                pl.when(jnp.logical_and(place >= lo, place < hi))(lambda: put(place - lo))

        return carry

    lax.fori_loop(0, plan.rows, pack, 0)


def place_early_kernel(plan, offsets, *refs):
    count = len(offsets)
    pieces, out, sets, refs = refs[:count], refs[count], refs[count + 1], refs[count + 2 :]
    tags, where, tag_sems, sems = refs
    column = lax.axis_index("wide") // plan.grid_rows
    block = plan.block
    run_all(
        [
            pltpu.make_async_copy(
                pieces[i].at[pl.ds(plan.early[o] * block, TAG)], tags.at[i], tag_sems.at[i]
            )
            for i, o in enumerate(offsets)
        ]
    )
    copies = []
    for i, o in enumerate(offsets):
        source = jnp.bitwise_xor(column, o)
        chosen = jnp.max(tags[i].astype(jnp.float32)).astype(jnp.int32)
        sets[i] = chosen
        list_rows(plan, chosen, 1, where.at[i])
        for k in range(plan.early[o]):
            copies.append(
                pltpu.make_async_copy(
                    pieces[i].at[pl.ds(k * block, block)],
                    out.at[where[i, k], source],
                    sems.at[i, k],
                )
            )
            copies[-1].start()
    for copy in copies:
        copy.wait()


def place_late_kernel(plan, messages, early, sets, pieces, out, held, where, set_sem, sems):
    column = lax.axis_index("wide") // plan.grid_rows
    block = plan.block
    copies = []

    def place(i, rows):
        o, lo, hi = messages[i]
        source = jnp.bitwise_xor(column, o)
        if rows is None:
            moves = [(pieces[i], out.at[pl.ds(lo, hi - lo), source])]
        else:
            moves = [(pieces[i].at[k - lo], out.at[rows[k], source]) for k in range(lo, hi)]
        for k, (src, dst) in enumerate(moves):
            copies.append(pltpu.make_async_copy(src, dst, sems.at[i, k]))
            copies[-1].start()

    split = [i for i, m in enumerate(messages) if m[0] in early]
    if split:
        fetch = pltpu.make_async_copy(sets, held, set_sem)
        fetch.start()
    for i in range(len(messages)):
        if i not in split:
            place(i, None)
    if split:
        fetch.wait()
    for i in split:
        list_rows(plan, held[early.index(messages[i][0])], 0, where.at[i])
        place(i, where.at[i])
    for copy in copies:
        copy.wait()


def after(value, *others):
    return lax.optimization_barrier((value, *others))[0]


def across(value, plan, offset):
    pairs = [
        (c * plan.grid_rows + r, (c ^ offset) * plan.grid_rows + r)
        for c in range(GRID_COLS)
        for r in range(plan.grid_rows)
    ]
    return lax.ppermute(value, "wide", pairs)


def along(value, plan, steps):
    return lax.ppermute(
        value, "front", [(f, (f + steps) % plan.groups) for f in range(plan.groups)]
    )


def local(updates, parent_panels, slot_parent, slot_row, slot_cols, slot_mask):
    plan = Plan(updates, parent_panels, slot_cols)
    block, width = plan.block, plan.width
    bf16 = jnp.bfloat16
    heads = slot_parent[0, :, 0] * plan.rows + slot_row[0]
    all_heads = [heads] + [along(heads, plan, k) for k in range(1, plan.groups)]
    codes = slot_mask[0] * plan.window + slot_cols[0]
    panels = pltpu.with_memory_space_constraint(parent_panels, pltpu.HBM)
    moving = pltpu.with_memory_space_constraint(updates, pltpu.HBM)


    early = [o for o in plan.early if plan.early[o]]
    lead, tail = early[:2], early[2:]
    packed, touched = {}, []

    def early_shape(o):
        return jax.ShapeDtypeStruct((plan.early[o] * block + TAG, width), bf16)

    if lead:
        staged = pl.pallas_call(
            functools.partial(stage_kernel, plan, lead),
            out_shape=[jax.ShapeDtypeStruct((plan.rows * block, width), bf16) for _ in lead],
            in_specs=[HBM],
            out_specs=[VMEM] * len(lead),
            scratch_shapes=[pltpu.SemaphoreType.DMA((len(lead), plan.col_groups))],
            compiler_params=params(),
            cost_estimate=COST,
            name="stage",
        )(panels)
        *outs, touched_set = pl.pallas_call(
            functools.partial(pack_kernel, plan, lead),
            out_shape=[early_shape(o) for o in lead] + [jax.ShapeDtypeStruct((1,), jnp.int32)],
            in_specs=[SMEM] * plan.groups + [VMEM] * len(lead),
            out_specs=[VMEM] * len(lead) + [SMEM],
            scratch_shapes=[pltpu.SMEM((plan.rows,), jnp.int32)],
            compiler_params=params(),
            cost_estimate=COST,
            name="pack_early",
        )(*all_heads, *staged)
        packed = dict(zip(lead, outs))
        touched = [touched_set]

    count = (plan.groups - 1) * plan.capacity
    outs = pl.pallas_call(
        functools.partial(bucket_kernel, plan, tail),
        out_shape=[jax.ShapeDtypeStruct((block, updates.shape[2]), bf16)] * count
        + [early_shape(o) for o in tail],
        in_specs=[SMEM] * (1 + len(touched)) + [HBM, HBM],
        out_specs=[VMEM] * (count + len(tail)),
        scratch_shapes=[
            pltpu.SMEM((plan.rows,), jnp.int32),
            pltpu.SemaphoreType.DMA((plan.slots,)),
            pltpu.SemaphoreType.DMA((max(1, len(tail)), max(1, plan.first), plan.col_groups)),
        ],
        compiler_params=params(),
        cost_estimate=COST,
        name="bucket",
    )(heads, *touched, moving, panels)
    packed.update(zip(tail, outs[count:]))

    all_codes = [after(codes, *touched)]
    all_codes += [along(all_codes[0], plan, k) for k in range(1, plan.groups)]
    got = [
        along(outs[(k - 1) * plan.capacity + c], plan, k)
        for k in range(1, plan.groups)
        for c in range(plan.capacity)
    ]

    moved = plan.slots + (plan.groups - 1) * plan.capacity
    assembled = pl.pallas_call(
        functools.partial(assemble_kernel, plan),
        out_shape=[
            jax.ShapeDtypeStruct(((hi - lo) * block, width), bf16) for o, lo, hi in plan.late
        ],
        in_specs=[SMEM] * (2 * plan.groups) + [HBM, HBM] + [ANY] * len(got),
        out_specs=[VMEM] * len(plan.late),
        scratch_shapes=[
            pltpu.VMEM((plan.rows, block, parent_panels.shape[2]), jnp.float32),
            pltpu.VMEM((plan.rows, block, parent_panels.shape[2]), bf16),
            pltpu.VMEM((moved, block, updates.shape[2]), bf16),
            pltpu.SMEM((GRID_COLS, plan.rows), jnp.int32),
            pltpu.SemaphoreType.DMA((plan.rows,)),
            pltpu.SemaphoreType.DMA((moved,)),
        ],
        compiler_params=params(),
        cost_estimate=COST,
        name="assemble",
    )(*all_heads, *all_codes, panels, moving, *got)

    ready = dict(zip(plan.late, assembled))

    def late(o, part=0):
        return [m for m in plan.late if m[0] == o][part]

    arrived = {late(0): ready[late(0)]}

    def send(message, *others):
        arrived[message] = across(after(ready[message], *others), plan, message[0])
        return arrived[message]

    first = {}

    def send_early(o, *others):
        if o in packed:
            first[o] = across(after(packed[o], *others), plan, o)

    def came(*offsets):
        return [first[o] for o in offsets if o in first]

    send_early(4)
    send_early(5)
    send_early(7, *came(4), *all_codes[1:])
    b5 = send(late(5), *came(5))
    b7 = send(late(7), *came(7))
    send(late(6), b5)
    send(late(4), b7)
    n2 = send(late(2), *came(5))
    send(late(3), *came(7))
    send(late(1, 0), n2)
    send(late(1, 1), b7)

    out_shape = jax.ShapeDtypeStruct((plan.rows, GRID_COLS, block, width), bf16)
    held, sets = [], []
    if early:
        out, sets = pl.pallas_call(
            functools.partial(place_early_kernel, plan, early),
            out_shape=[out_shape, jax.ShapeDtypeStruct((len(early),), jnp.int32)],
            in_specs=[ANY] * len(early),
            out_specs=[HBM, SMEM],
            scratch_shapes=[
                pltpu.VMEM((len(early), TAG, width), bf16),
                pltpu.SMEM((len(early), plan.rows), jnp.int32),
                pltpu.SemaphoreType.DMA((len(early),)),
                pltpu.SemaphoreType.DMA((len(early), plan.first)),
            ],
            compiler_params=params(),
            cost_estimate=COST,
            name="place_early",
        )(*[first[o] for o in early])
        held, sets = [out], [sets]

    def place(held, messages, name):
        known = sets if any(m[0] in early for m in messages) else []

        def body(*refs):
            refs = list(refs)[len(held) :]
            sets_ref = refs.pop(0) if known else None
            count = len(messages)
            place_late_kernel(plan, messages, early, sets_ref, refs[:count], *refs[count:])

        return [
            pl.pallas_call(
                body,
                out_shape=out_shape,
                in_specs=[HBM] * len(held) + [ANY] * (len(known) + len(messages)),
                out_specs=HBM,
                input_output_aliases={0: 0} if held else {},
                scratch_shapes=[
                    pltpu.SMEM((max(1, len(early)),), jnp.int32),
                    pltpu.SMEM((len(messages), plan.rows), jnp.int32),
                    pltpu.SemaphoreType.DMA,
                    pltpu.SemaphoreType.DMA((len(messages), plan.rows)),
                ],
                compiler_params=params(),
                cost_estimate=MID if name == "place_mid" else COST,
                name=name,
            )(*held, *known, *[arrived[m].reshape(-1, block, width) for m in messages])
        ]

    last = [late(4), late(6)]
    held = place(held, [m for m in plan.late if m not in last], "place_mid")
    held = place(held, last, "place_last")
    return held[0].reshape(1, plan.rows * GRID_COLS * block, width)


def solution(mesh):
    return jax.shard_map(
        local,
        mesh=mesh,
        in_specs=(
            P("front", "wide", None),
            P("front", "wide", None),
            P("front", "wide", None),
            P("front", "wide"),
            P("front", "wide", None),
            P("front", "wide", None),
        ),
        out_specs=P("front", "wide", None),
        check_vma=False,
    )
```

```python
import functools

import jax
import jax.numpy as jnp
from jax import lax
from jax.experimental import pallas as pl
from jax.experimental.pallas import tpu as pltpu
from jax.sharding import PartitionSpec as P

GRID_COLS = 8
NEAR = GRID_COLS // 2
TAG = 8

ANY = pl.BlockSpec(memory_space=pl.ANY)
HBM = pl.BlockSpec(memory_space=pltpu.HBM)
SMEM = pl.BlockSpec(memory_space=pltpu.SMEM)
VMEM = pl.BlockSpec(memory_space=pltpu.VMEM)


class Plan:
    def __init__(self, updates, panels, slot_cols):
        self.groups = lax.axis_size("front")
        self.lanes = lax.axis_size("wide")
        self.grid_rows = self.lanes // GRID_COLS
        self.slots = slot_cols.shape[1]
        self.columns = slot_cols.shape[2]
        self.block = updates.shape[1] // self.slots
        self.rows = panels.shape[1] // self.block
        self.window = panels.shape[2] // self.block
        self.col_groups = self.window // GRID_COLS
        self.width = self.col_groups * self.block
        self.capacity = max(self.slots // 4, self.slots // self.groups)
        self.first = max(0, self.rows - self.capacity * self.groups)
        self.early = {4: 3 * self.first // 4, 5: self.first, 7: self.first}
        self.late = []
        for o in range(GRID_COLS):
            count = self.rows - self.early.get(o, 0)
            cuts = [0, count // 2, count] if o == 1 else [0, count]
            self.late += [(o, lo, hi) for lo, hi in zip(cuts, cuts[1:]) if lo < hi]


MID = pl.CostEstimate(flops=0, transcendentals=0, bytes_accessed=0)
COST = pl.CostEstimate(flops=0, transcendentals=0, bytes_accessed=0)


def params():
    return pltpu.CompilerParams(vmem_limit_bytes=48 << 20)


def at(start, size):
    return pl.ds(pl.multiple_of(start * size, size), size)


def own_row(plan, heads, q, front):
    row = heads[q] - front * plan.rows
    return jnp.logical_and(row >= 0, row < plan.rows), row


def touched_rows(plan, head_refs):
    me = lax.axis_index("front")
    touched = jnp.int32(0)
    for heads in head_refs:
        for q in range(plan.slots):
            named, row = own_row(plan, heads, q, me)
            bit = jnp.left_shift(jnp.int32(1), jnp.where(named, row, 0))
            touched = touched | jnp.where(named, bit, 0)
    return touched


def first_rows(plan, touched, limits, order=None):
    chosen, count = [jnp.int32(0) for _ in limits], jnp.int32(0)
    for t in range(plan.rows):
        free = 1 - (jnp.right_shift(touched, t) & 1)
        chosen = [c | jnp.where(count < n, free << t, 0) for c, n in zip(chosen, limits)]
        if order is not None:
            order[count] = t
        count = count + free
    return chosen


def positions(plan, chosen):
    out, count = [], jnp.int32(0)
    for t in range(plan.rows):
        bit = jnp.right_shift(chosen, t) & 1
        out.append((bit, jnp.where(bit == 1, count, t - count)))
        count = count + bit
    return out


def list_rows(plan, chosen, bit_wanted, where):
    for t, (bit, place) in enumerate(positions(plan, chosen)):

        @pl.when(bit == bit_wanted)
        def _():
            where[place] = t


def run_all(copies):
    for copy in copies:
        copy.start()
    for copy in copies:
        copy.wait()


def stage_kernel(plan, lead, panel, *refs):
    staged, sems = refs[: len(lead)], refs[len(lead)]
    column = lax.axis_index("wide") // plan.grid_rows
    block = plan.block
    run_all(
        [
            pltpu.make_async_copy(
                panel.at[0, :, at(cc * GRID_COLS + jnp.bitwise_xor(column, o), block)],
                staged[i].at[:, pl.ds(cc * block, block)],
                sems.at[i, cc],
            )
            for i, o in enumerate(lead)
            for cc in range(plan.col_groups)
        ]
    )


def put_tag(plan, chosen, o, out):
    chosen = chosen.astype(jnp.float32)
    tag = jnp.full((TAG, plan.width), chosen, jnp.float32).astype(jnp.bfloat16)
    out[plan.early[o] * plan.block :, :] = tag


def pack_kernel(plan, lead, *refs):
    groups, count = plan.groups, len(lead)
    head_refs, staged, refs = refs[:groups], refs[groups : groups + count], refs[groups + count :]
    outs, (touched_out, order) = refs[:count], refs[count:]
    block = plan.block
    touched = touched_rows(plan, head_refs)
    touched_out[0] = touched
    chosen = first_rows(plan, touched, [plan.early[o] for o in lead], order)
    for i, o in enumerate(lead):
        for k in range(plan.early[o]):
            outs[i][pl.ds(k * block, block), :] = staged[i][at(order[k], block), :]
        put_tag(plan, chosen[i], o, outs[i])


def bucket_kernel(plan, tail, heads, *refs):
    touched_ref, refs = (refs[0], refs[1:]) if tail else (None, refs)
    updates, panel, refs = refs[0], refs[1], refs[2:]
    count = (plan.groups - 1) * plan.capacity
    outs, packed, refs = refs[:count], refs[count : count + len(tail)], refs[count + len(tail) :]
    order, slot_sems, sems = refs
    me = lax.axis_index("front")
    column = lax.axis_index("wide") // plan.grid_rows
    block = plan.block

    def buckets(act):
        for k in range(1, plan.groups):
            target = lax.rem(me + k, plan.groups)
            rank = jnp.int32(0)
            for q in range(plan.slots):
                named, _ = own_row(plan, heads, q, target)
                for c in range(plan.capacity):

                    @pl.when(jnp.logical_and(named, rank == c))
                    def _():
                        act(
                            pltpu.make_async_copy(
                                updates.at[0, pl.ds(q * block, block)],
                                outs[(k - 1) * plan.capacity + c],
                                slot_sems.at[q],
                            )
                        )

                rank = rank + jnp.where(named, 1, 0)

    buckets(lambda c: c.start())
    copies = []
    if tail:
        touched = touched_ref[0]
        chosen = first_rows(plan, touched, [plan.early[o] for o in tail], order)
        for i, o in enumerate(tail):
            target = jnp.bitwise_xor(column, o)
            for k in range(plan.early[o]):
                for cc in range(plan.col_groups):
                    copies.append(
                        pltpu.make_async_copy(
                            panel.at[0, at(order[k], block), at(cc * GRID_COLS + target, block)],
                            packed[i].at[pl.ds(k * block, block), pl.ds(cc * block, block)],
                            sems.at[i, k, cc],
                        )
                    )
                    copies[-1].start()
            put_tag(plan, chosen[i], o, packed[i])
    for copy in copies:
        copy.wait()
    buckets(lambda c: c.wait())


def assemble_kernel(plan, *refs):
    groups, block = plan.groups, plan.block
    head_refs, refs = refs[:groups], refs[groups:]
    code_refs, refs = refs[:groups], refs[groups:]
    panel, updates, refs = refs[0], refs[1], refs[2:]
    count = (groups - 1) * plan.capacity
    got, refs = refs[:count], refs[count:]
    outs, refs = refs[: len(plan.late)], refs[len(plan.late) :]
    total, raw, moved, place_ref, row_sems, slot_sems = refs
    me = lax.axis_index("front")
    column = lax.axis_index("wide") // plan.grid_rows

    slot_copies = [
        pltpu.make_async_copy(
            updates.at[0, pl.ds(q * block, block)], moved.at[q], slot_sems.at[q]
        )
        for q in range(plan.slots)
    ]
    for k in range(1, groups):
        for c in range(plan.capacity):
            part = (k - 1) * plan.capacity + c
            index = plan.slots + part
            slot_copies.append(
                pltpu.make_async_copy(got[part], moved.at[index], slot_sems.at[index])
            )
    row_copies = [
        pltpu.make_async_copy(panel.at[0, pl.ds(t * block, block)], raw.at[t], row_sems.at[t])
        for t in range(plan.rows)
    ]
    for copy in row_copies + slot_copies:
        copy.start()

    touched = touched_rows(plan, head_refs)
    limits = list(plan.early.values())
    for o, chosen in zip(plan.early, first_rows(plan, touched, limits)):
        for t, (bit, place) in enumerate(positions(plan, chosen)):
            place_ref[o, t] = jnp.where(bit == 1, -1, place)

    for t in range(plan.rows):
        row_copies[t].wait()
    for copy in slot_copies:
        copy.wait()

    def widen(t, carry):
        total[t] = raw[t].astype(jnp.float32)
        return carry

    lax.fori_loop(0, plan.rows, widen, 0)

    for s, (heads, codes) in enumerate(zip(head_refs, code_refs)):

        def add_slot(q, rank):
            named, t = own_row(plan, heads, q, me)
            index = q if s == 0 else plan.slots + (s - 1) * plan.capacity + rank

            @pl.when(named)
            def _():
                for j in range(plan.columns):
                    code = codes[q, j]
                    col = code % plan.window

                    @pl.when(code >= plan.window)
                    def _():
                        where = at(col, block)
                        total[t, :, where] += moved[
                            index, :, pl.ds(j * block, block)
                        ].astype(jnp.float32)

            return rank + jnp.where(named, 1, 0)

        lax.fori_loop(0, plan.slots, add_slot, jnp.int32(0))

    def pack(t, carry):
        for ref, (o, lo, hi) in zip(outs, plan.late):
            target = jnp.bitwise_xor(column, o)

            def put(row):
                for cc in range(plan.col_groups):
                    ref[at(row, block), pl.ds(cc * block, block)] = total[
                        t, :, at(cc * GRID_COLS + target, block)
                    ].astype(jnp.bfloat16)

            if hi - lo == plan.rows:
                put(t)
            else:
                place = place_ref[o, t] if plan.early.get(o) else t
                pl.when(jnp.logical_and(place >= lo, place < hi))(lambda: put(place - lo))

        return carry

    lax.fori_loop(0, plan.rows, pack, 0)


def place_early_kernel(plan, offsets, *refs):
    count = len(offsets)
    pieces, out, sets, refs = refs[:count], refs[count], refs[count + 1], refs[count + 2 :]
    tags, where, tag_sems, sems = refs
    column = lax.axis_index("wide") // plan.grid_rows
    block = plan.block
    run_all(
        [
            pltpu.make_async_copy(
                pieces[i].at[pl.ds(plan.early[o] * block, TAG)], tags.at[i], tag_sems.at[i]
            )
            for i, o in enumerate(offsets)
        ]
    )
    copies = []
    for i, o in enumerate(offsets):
        source = jnp.bitwise_xor(column, o)
        chosen = jnp.max(tags[i].astype(jnp.float32)).astype(jnp.int32)
        sets[i] = chosen
        list_rows(plan, chosen, 1, where.at[i])
        for k in range(plan.early[o]):
            copies.append(
                pltpu.make_async_copy(
                    pieces[i].at[pl.ds(k * block, block)],
                    out.at[where[i, k], source],
                    sems.at[i, k],
                )
            )
            copies[-1].start()
    for copy in copies:
        copy.wait()


def place_late_kernel(plan, messages, early, sets, pieces, out, held, where, set_sem, sems):
    column = lax.axis_index("wide") // plan.grid_rows
    block = plan.block
    copies = []

    def place(i, rows):
        o, lo, hi = messages[i]
        source = jnp.bitwise_xor(column, o)
        if rows is None:
            moves = [(pieces[i], out.at[pl.ds(lo, hi - lo), source])]
        else:
            moves = [(pieces[i].at[k - lo], out.at[rows[k], source]) for k in range(lo, hi)]
        for k, (src, dst) in enumerate(moves):
            copies.append(pltpu.make_async_copy(src, dst, sems.at[i, k]))
            copies[-1].start()

    split = [i for i, m in enumerate(messages) if m[0] in early]
    if split:
        fetch = pltpu.make_async_copy(sets, held, set_sem)
        fetch.start()
    for i in range(len(messages)):
        if i not in split:
            place(i, None)
    if split:
        fetch.wait()
    for i in split:
        list_rows(plan, held[early.index(messages[i][0])], 0, where.at[i])
        place(i, where.at[i])
    for copy in copies:
        copy.wait()


def after(value, *others):
    return lax.optimization_barrier((value, *others))[0]


def across(value, plan, offset):
    pairs = [
        (c * plan.grid_rows + r, (c ^ offset) * plan.grid_rows + r)
        for c in range(GRID_COLS)
        for r in range(plan.grid_rows)
    ]
    return lax.ppermute(value, "wide", pairs)


def along(value, plan, steps):
    return lax.ppermute(
        value, "front", [(f, (f + steps) % plan.groups) for f in range(plan.groups)]
    )


def local(updates, parent_panels, slot_parent, slot_row, slot_cols, slot_mask):
    plan = Plan(updates, parent_panels, slot_cols)
    block, width = plan.block, plan.width
    bf16 = jnp.bfloat16
    heads = slot_parent[0, :, 0] * plan.rows + slot_row[0]
    all_heads = [heads] + [along(heads, plan, k) for k in range(1, plan.groups)]
    codes = slot_mask[0] * plan.window + slot_cols[0]
    panels = pltpu.with_memory_space_constraint(parent_panels, pltpu.HBM)
    moving = pltpu.with_memory_space_constraint(updates, pltpu.HBM)


    early = [o for o in plan.early if plan.early[o]]
    lead, tail = early[:2], early[2:]
    packed, touched = {}, []

    def early_shape(o):
        return jax.ShapeDtypeStruct((plan.early[o] * block + TAG, width), bf16)

    if lead:
        staged = pl.pallas_call(
            functools.partial(stage_kernel, plan, lead),
            out_shape=[jax.ShapeDtypeStruct((plan.rows * block, width), bf16) for _ in lead],
            in_specs=[HBM],
            out_specs=[VMEM] * len(lead),
            scratch_shapes=[pltpu.SemaphoreType.DMA((len(lead), plan.col_groups))],
            compiler_params=params(),
            cost_estimate=COST,
            name="stage",
        )(panels)
        *outs, touched_set = pl.pallas_call(
            functools.partial(pack_kernel, plan, lead),
            out_shape=[early_shape(o) for o in lead] + [jax.ShapeDtypeStruct((1,), jnp.int32)],
            in_specs=[SMEM] * plan.groups + [VMEM] * len(lead),
            out_specs=[VMEM] * len(lead) + [SMEM],
            scratch_shapes=[pltpu.SMEM((plan.rows,), jnp.int32)],
            compiler_params=params(),
            cost_estimate=COST,
            name="pack_early",
        )(*all_heads, *staged)
        packed = dict(zip(lead, outs))
        touched = [touched_set]

    count = (plan.groups - 1) * plan.capacity
    outs = pl.pallas_call(
        functools.partial(bucket_kernel, plan, tail),
        out_shape=[jax.ShapeDtypeStruct((block, updates.shape[2]), bf16)] * count
        + [early_shape(o) for o in tail],
        in_specs=[SMEM] * (1 + len(touched)) + [HBM, HBM],
        out_specs=[VMEM] * (count + len(tail)),
        scratch_shapes=[
            pltpu.SMEM((plan.rows,), jnp.int32),
            pltpu.SemaphoreType.DMA((plan.slots,)),
            pltpu.SemaphoreType.DMA((max(1, len(tail)), max(1, plan.first), plan.col_groups)),
        ],
        compiler_params=params(),
        cost_estimate=COST,
        name="bucket",
    )(heads, *touched, moving, panels)
    packed.update(zip(tail, outs[count:]))

    all_codes = [after(codes, *touched)]
    all_codes += [along(all_codes[0], plan, k) for k in range(1, plan.groups)]
    got = [
        along(outs[(k - 1) * plan.capacity + c], plan, k)
        for k in range(1, plan.groups)
        for c in range(plan.capacity)
    ]

    moved = plan.slots + (plan.groups - 1) * plan.capacity
    assembled = pl.pallas_call(
        functools.partial(assemble_kernel, plan),
        out_shape=[
            jax.ShapeDtypeStruct(((hi - lo) * block, width), bf16) for o, lo, hi in plan.late
        ],
        in_specs=[SMEM] * (2 * plan.groups) + [HBM, HBM] + [ANY] * len(got),
        out_specs=[VMEM] * len(plan.late),
        scratch_shapes=[
            pltpu.VMEM((plan.rows, block, parent_panels.shape[2]), jnp.float32),
            pltpu.VMEM((plan.rows, block, parent_panels.shape[2]), bf16),
            pltpu.VMEM((moved, block, updates.shape[2]), bf16),
            pltpu.SMEM((GRID_COLS, plan.rows), jnp.int32),
            pltpu.SemaphoreType.DMA((plan.rows,)),
            pltpu.SemaphoreType.DMA((moved,)),
        ],
        compiler_params=params(),
        cost_estimate=COST,
        name="assemble",
    )(*all_heads, *all_codes, panels, moving, *got)

    ready = dict(zip(plan.late, assembled))

    def late(o, part=0):
        return [m for m in plan.late if m[0] == o][part]

    arrived = {late(0): ready[late(0)]}

    def send(message, *others):
        arrived[message] = across(after(ready[message], *others), plan, message[0])
        return arrived[message]

    first = {}

    def send_early(o, *others):
        if o in packed:
            first[o] = across(after(packed[o], *others), plan, o)

    def came(*offsets):
        return [first[o] for o in offsets if o in first]

    send_early(4)
    send_early(5)
    send_early(7, *came(4), *all_codes[1:])
    b5 = send(late(5), *came(5))
    b7 = send(late(7), *came(7))
    send(late(6), b5)
    send(late(4), b7)
    n2 = send(late(2), *came(5))
    send(late(3), *came(7))
    send(late(1, 0), n2)
    send(late(1, 1), b7)

    out_shape = jax.ShapeDtypeStruct((plan.rows, GRID_COLS, block, width), bf16)
    held, sets = [], []
    if early:
        out, sets = pl.pallas_call(
            functools.partial(place_early_kernel, plan, early),
            out_shape=[out_shape, jax.ShapeDtypeStruct((len(early),), jnp.int32)],
            in_specs=[ANY] * len(early),
            out_specs=[HBM, SMEM],
            scratch_shapes=[
                pltpu.VMEM((len(early), TAG, width), bf16),
                pltpu.SMEM((len(early), plan.rows), jnp.int32),
                pltpu.SemaphoreType.DMA((len(early),)),
                pltpu.SemaphoreType.DMA((len(early), plan.first)),
            ],
            compiler_params=params(),
            cost_estimate=COST,
            name="place_early",
        )(*[first[o] for o in early])
        held, sets = [out], [sets]

    def place(held, messages, name):
        known = sets if any(m[0] in early for m in messages) else []

        def body(*refs):
            refs = list(refs)[len(held) :]
            sets_ref = refs.pop(0) if known else None
            count = len(messages)
            place_late_kernel(plan, messages, early, sets_ref, refs[:count], *refs[count:])

        return [
            pl.pallas_call(
                body,
                out_shape=out_shape,
                in_specs=[HBM] * len(held) + [ANY] * (len(known) + len(messages)),
                out_specs=HBM,
                input_output_aliases={0: 0} if held else {},
                scratch_shapes=[
                    pltpu.SMEM((max(1, len(early)),), jnp.int32),
                    pltpu.SMEM((len(messages), plan.rows), jnp.int32),
                    pltpu.SemaphoreType.DMA,
                    pltpu.SemaphoreType.DMA((len(messages), plan.rows)),
                ],
                compiler_params=params(),
                cost_estimate=MID if name == "place_mid" else COST,
                name=name,
            )(*held, *known, *[arrived[m].reshape(-1, block, width) for m in messages])
        ]

    last = [late(4), late(6)]
    held = place(held, [m for m in plan.late if m not in last], "place_mid")
    held = place(held, last, "place_last")
    return held[0].reshape(1, plan.rows * GRID_COLS * block, width)


def solution(mesh):
    return jax.shard_map(
        local,
        mesh=mesh,
        in_specs=(
            P("front", "wide", None),
            P("front", "wide", None),
            P("front", "wide", None),
            P("front", "wide"),
            P("front", "wide", None),
            P("front", "wide", None),
        ),
        out_specs=P("front", "wide", None),
        check_vma=False,
    )
```

```python
import functools

import jax
import jax.numpy as jnp
from jax import lax
from jax.experimental import pallas as pl
from jax.experimental.pallas import tpu as pltpu
from jax.sharding import PartitionSpec as P

GRID_COLS = 8
NEAR = GRID_COLS // 2
TAG = 8

ANY = pl.BlockSpec(memory_space=pl.ANY)
HBM = pl.BlockSpec(memory_space=pltpu.HBM)
SMEM = pl.BlockSpec(memory_space=pltpu.SMEM)
VMEM = pl.BlockSpec(memory_space=pltpu.VMEM)


class Plan:
    def __init__(self, updates, panels, slot_cols):
        self.groups = lax.axis_size("front")
        self.lanes = lax.axis_size("wide")
        self.grid_rows = self.lanes // GRID_COLS
        self.slots = slot_cols.shape[1]
        self.columns = slot_cols.shape[2]
        self.block = updates.shape[1] // self.slots
        self.rows = panels.shape[1] // self.block
        self.window = panels.shape[2] // self.block
        self.col_groups = self.window // GRID_COLS
        self.width = self.col_groups * self.block
        self.capacity = max(self.slots // 4, self.slots // self.groups)
        self.first = max(0, self.rows - self.capacity * self.groups)
        self.early = {6: self.first // 2, 5: self.first, 7: self.first}
        self.late = []
        for o in range(GRID_COLS):
            count = self.rows - self.early.get(o, 0)
            cuts = [0, max(1, 5 * count // 8), count] if o == 1 else [0, count]
            self.late += [(o, lo, hi) for lo, hi in zip(cuts, cuts[1:]) if lo < hi]


MID = pl.CostEstimate(flops=0, transcendentals=0, bytes_accessed=0)
COST = pl.CostEstimate(flops=0, transcendentals=0, bytes_accessed=0)


def params():
    return pltpu.CompilerParams(vmem_limit_bytes=48 << 20)


def at(start, size):
    return pl.ds(pl.multiple_of(start * size, size), size)


def own_row(plan, heads, q, front):
    row = heads[q] - front * plan.rows
    return jnp.logical_and(row >= 0, row < plan.rows), row


def touched_rows(plan, head_refs):
    me = lax.axis_index("front")
    touched = jnp.int32(0)
    for heads in head_refs:
        for q in range(plan.slots):
            named, row = own_row(plan, heads, q, me)
            bit = jnp.left_shift(jnp.int32(1), jnp.where(named, row, 0))
            touched = touched | jnp.where(named, bit, 0)
    return touched


def first_rows(plan, touched, limits, order=None):
    chosen, count = [jnp.int32(0) for _ in limits], jnp.int32(0)
    for t in range(plan.rows):
        free = 1 - (jnp.right_shift(touched, t) & 1)
        chosen = [c | jnp.where(count < n, free << t, 0) for c, n in zip(chosen, limits)]
        if order is not None:
            order[count] = t
        count = count + free
    return chosen


def positions(plan, chosen):
    out, count = [], jnp.int32(0)
    for t in range(plan.rows):
        bit = jnp.right_shift(chosen, t) & 1
        out.append((bit, jnp.where(bit == 1, count, t - count)))
        count = count + bit
    return out


def list_rows(plan, chosen, bit_wanted, where):
    for t, (bit, place) in enumerate(positions(plan, chosen)):

        @pl.when(bit == bit_wanted)
        def _():
            where[place] = t


def run_all(copies):
    for copy in copies:
        copy.start()
    for copy in copies:
        copy.wait()


def stage_kernel(plan, lead, panel, *refs):
    staged, sems = refs[: len(lead)], refs[len(lead)]
    column = lax.axis_index("wide") // plan.grid_rows
    block = plan.block
    run_all(
        [
            pltpu.make_async_copy(
                panel.at[0, :, at(cc * GRID_COLS + jnp.bitwise_xor(column, o), block)],
                staged[i].at[:, pl.ds(cc * block, block)],
                sems.at[i, cc],
            )
            for i, o in enumerate(lead)
            for cc in range(plan.col_groups)
        ]
    )


def put_tag(plan, chosen, o, out):
    chosen = chosen.astype(jnp.float32)
    tag = jnp.full((TAG, plan.width), chosen, jnp.float32).astype(jnp.bfloat16)
    out[plan.early[o] * plan.block :, :] = tag


def pack_kernel(plan, lead, *refs):
    groups, count = plan.groups, len(lead)
    head_refs, staged, refs = refs[:groups], refs[groups : groups + count], refs[groups + count :]
    outs, (touched_out, order) = refs[:count], refs[count:]
    block = plan.block
    touched = touched_rows(plan, head_refs)
    touched_out[0] = touched
    chosen = first_rows(plan, touched, [plan.early[o] for o in lead], order)
    for i, o in enumerate(lead):
        for k in range(plan.early[o]):
            outs[i][pl.ds(k * block, block), :] = staged[i][at(order[k], block), :]
        put_tag(plan, chosen[i], o, outs[i])


def bucket_kernel(plan, tail, heads, *refs):
    touched_ref, refs = (refs[0], refs[1:]) if tail else (None, refs)
    updates, panel, refs = refs[0], refs[1], refs[2:]
    count = (plan.groups - 1) * plan.capacity
    outs, packed, refs = refs[:count], refs[count : count + len(tail)], refs[count + len(tail) :]
    order, slot_sems, sems = refs
    me = lax.axis_index("front")
    column = lax.axis_index("wide") // plan.grid_rows
    block = plan.block

    def buckets(act):
        for k in range(1, plan.groups):
            target = lax.rem(me + k, plan.groups)
            rank = jnp.int32(0)
            for q in range(plan.slots):
                named, _ = own_row(plan, heads, q, target)
                for c in range(plan.capacity):

                    @pl.when(jnp.logical_and(named, rank == c))
                    def _():
                        act(
                            pltpu.make_async_copy(
                                updates.at[0, pl.ds(q * block, block)],
                                outs[(k - 1) * plan.capacity + c],
                                slot_sems.at[q],
                            )
                        )

                rank = rank + jnp.where(named, 1, 0)

    buckets(lambda c: c.start())
    copies = []
    if tail:
        touched = touched_ref[0]
        chosen = first_rows(plan, touched, [plan.early[o] for o in tail], order)
        for i, o in enumerate(tail):
            target = jnp.bitwise_xor(column, o)
            for k in range(plan.early[o]):
                for cc in range(plan.col_groups):
                    copies.append(
                        pltpu.make_async_copy(
                            panel.at[0, at(order[k], block), at(cc * GRID_COLS + target, block)],
                            packed[i].at[pl.ds(k * block, block), pl.ds(cc * block, block)],
                            sems.at[i, k, cc],
                        )
                    )
                    copies[-1].start()
            put_tag(plan, chosen[i], o, packed[i])
    for copy in copies:
        copy.wait()
    buckets(lambda c: c.wait())


def assemble_kernel(plan, *refs):
    groups, block = plan.groups, plan.block
    head_refs, refs = refs[:groups], refs[groups:]
    code_refs, refs = refs[:groups], refs[groups:]
    panel, updates, refs = refs[0], refs[1], refs[2:]
    count = (groups - 1) * plan.capacity
    got, refs = refs[:count], refs[count:]
    outs, refs = refs[: len(plan.late)], refs[len(plan.late) :]
    total, raw, moved, place_ref, row_sems, slot_sems = refs
    me = lax.axis_index("front")
    column = lax.axis_index("wide") // plan.grid_rows

    slot_copies = [
        pltpu.make_async_copy(
            updates.at[0, pl.ds(q * block, block)], moved.at[q], slot_sems.at[q]
        )
        for q in range(plan.slots)
    ]
    for k in range(1, groups):
        for c in range(plan.capacity):
            part = (k - 1) * plan.capacity + c
            index = plan.slots + part
            slot_copies.append(
                pltpu.make_async_copy(got[part], moved.at[index], slot_sems.at[index])
            )
    row_copies = [
        pltpu.make_async_copy(panel.at[0, pl.ds(t * block, block)], raw.at[t], row_sems.at[t])
        for t in range(plan.rows)
    ]
    for copy in row_copies + slot_copies:
        copy.start()

    touched = touched_rows(plan, head_refs)
    limits = list(plan.early.values())
    for o, chosen in zip(plan.early, first_rows(plan, touched, limits)):
        for t, (bit, place) in enumerate(positions(plan, chosen)):
            place_ref[o, t] = jnp.where(bit == 1, -1, place)

    for t in range(plan.rows):
        row_copies[t].wait()
    for copy in slot_copies:
        copy.wait()

    def widen(t, carry):
        total[t] = raw[t].astype(jnp.float32)
        return carry

    lax.fori_loop(0, plan.rows, widen, 0)

    for s, (heads, codes) in enumerate(zip(head_refs, code_refs)):

        def add_slot(q, rank):
            named, t = own_row(plan, heads, q, me)
            index = q if s == 0 else plan.slots + (s - 1) * plan.capacity + rank

            @pl.when(named)
            def _():
                for j in range(plan.columns):
                    code = codes[q, j]
                    col = code % plan.window

                    @pl.when(code >= plan.window)
                    def _():
                        where = at(col, block)
                        total[t, :, where] += moved[
                            index, :, pl.ds(j * block, block)
                        ].astype(jnp.float32)

            return rank + jnp.where(named, 1, 0)

        lax.fori_loop(0, plan.slots, add_slot, jnp.int32(0))

    def pack(t, carry):
        for ref, (o, lo, hi) in zip(outs, plan.late):
            target = jnp.bitwise_xor(column, o)

            def put(row):
                for cc in range(plan.col_groups):
                    ref[at(row, block), pl.ds(cc * block, block)] = total[
                        t, :, at(cc * GRID_COLS + target, block)
                    ].astype(jnp.bfloat16)

            if hi - lo == plan.rows:
                put(t)
            else:
                place = place_ref[o, t] if plan.early.get(o) else t
                pl.when(jnp.logical_and(place >= lo, place < hi))(lambda: put(place - lo))

        return carry

    lax.fori_loop(0, plan.rows, pack, 0)


def place_early_kernel(plan, offsets, *refs):
    count = len(offsets)
    pieces, out, sets, refs = refs[:count], refs[count], refs[count + 1], refs[count + 2 :]
    tags, where, tag_sems, sems = refs
    column = lax.axis_index("wide") // plan.grid_rows
    block = plan.block
    run_all(
        [
            pltpu.make_async_copy(
                pieces[i].at[pl.ds(plan.early[o] * block, TAG)], tags.at[i], tag_sems.at[i]
            )
            for i, o in enumerate(offsets)
        ]
    )
    copies = []
    for i, o in enumerate(offsets):
        source = jnp.bitwise_xor(column, o)
        chosen = jnp.max(tags[i].astype(jnp.float32)).astype(jnp.int32)
        sets[i] = chosen
        list_rows(plan, chosen, 1, where.at[i])
        for k in range(plan.early[o]):
            copies.append(
                pltpu.make_async_copy(
                    pieces[i].at[pl.ds(k * block, block)],
                    out.at[where[i, k], source],
                    sems.at[i, k],
                )
            )
            copies[-1].start()
    for copy in copies:
        copy.wait()


def place_late_kernel(plan, messages, early, sets, pieces, out, held, where, set_sem, sems):
    column = lax.axis_index("wide") // plan.grid_rows
    block = plan.block
    copies = []

    def place(i, rows):
        o, lo, hi = messages[i]
        source = jnp.bitwise_xor(column, o)
        if rows is None:
            moves = [(pieces[i], out.at[pl.ds(lo, hi - lo), source])]
        else:
            moves = [(pieces[i].at[k - lo], out.at[rows[k], source]) for k in range(lo, hi)]
        for k, (src, dst) in enumerate(moves):
            copies.append(pltpu.make_async_copy(src, dst, sems.at[i, k]))
            copies[-1].start()

    split = [i for i, m in enumerate(messages) if m[0] in early]
    if split:
        fetch = pltpu.make_async_copy(sets, held, set_sem)
        fetch.start()
    for i in range(len(messages)):
        if i not in split:
            place(i, None)
    if split:
        fetch.wait()
    for i in split:
        list_rows(plan, held[early.index(messages[i][0])], 0, where.at[i])
        place(i, where.at[i])
    for copy in copies:
        copy.wait()


def after(value, *others):
    return lax.optimization_barrier((value, *others))[0]


def across(value, plan, offset):
    pairs = [
        (c * plan.grid_rows + r, (c ^ offset) * plan.grid_rows + r)
        for c in range(GRID_COLS)
        for r in range(plan.grid_rows)
    ]
    return lax.ppermute(value, "wide", pairs)


def along(value, plan, steps):
    return lax.ppermute(
        value, "front", [(f, (f + steps) % plan.groups) for f in range(plan.groups)]
    )


def local(updates, parent_panels, slot_parent, slot_row, slot_cols, slot_mask):
    plan = Plan(updates, parent_panels, slot_cols)
    block, width = plan.block, plan.width
    bf16 = jnp.bfloat16
    heads = slot_parent[0, :, 0] * plan.rows + slot_row[0]
    all_heads = [heads] + [along(heads, plan, k) for k in range(1, plan.groups)]
    codes = slot_mask[0] * plan.window + slot_cols[0]
    panels = pltpu.with_memory_space_constraint(parent_panels, pltpu.HBM)
    moving = pltpu.with_memory_space_constraint(updates, pltpu.HBM)


    early = [o for o in plan.early if plan.early[o]]
    lead, tail = early[:2], early[2:]
    packed, touched = {}, []

    def early_shape(o):
        return jax.ShapeDtypeStruct((plan.early[o] * block + TAG, width), bf16)

    if lead:
        staged = pl.pallas_call(
            functools.partial(stage_kernel, plan, lead),
            out_shape=[jax.ShapeDtypeStruct((plan.rows * block, width), bf16) for _ in lead],
            in_specs=[HBM],
            out_specs=[VMEM] * len(lead),
            scratch_shapes=[pltpu.SemaphoreType.DMA((len(lead), plan.col_groups))],
            compiler_params=params(),
            cost_estimate=COST,
            name="stage",
        )(panels)
        *outs, touched_set = pl.pallas_call(
            functools.partial(pack_kernel, plan, lead),
            out_shape=[early_shape(o) for o in lead] + [jax.ShapeDtypeStruct((1,), jnp.int32)],
            in_specs=[SMEM] * plan.groups + [VMEM] * len(lead),
            out_specs=[VMEM] * len(lead) + [SMEM],
            scratch_shapes=[pltpu.SMEM((plan.rows,), jnp.int32)],
            compiler_params=params(),
            cost_estimate=COST,
            name="pack_early",
        )(*all_heads, *staged)
        packed = dict(zip(lead, outs))
        touched = [touched_set]

    count = (plan.groups - 1) * plan.capacity
    outs = pl.pallas_call(
        functools.partial(bucket_kernel, plan, tail),
        out_shape=[jax.ShapeDtypeStruct((block, updates.shape[2]), bf16)] * count
        + [early_shape(o) for o in tail],
        in_specs=[SMEM] * (1 + len(touched)) + [HBM, HBM],
        out_specs=[VMEM] * (count + len(tail)),
        scratch_shapes=[
            pltpu.SMEM((plan.rows,), jnp.int32),
            pltpu.SemaphoreType.DMA((plan.slots,)),
            pltpu.SemaphoreType.DMA((max(1, len(tail)), max(1, plan.first), plan.col_groups)),
        ],
        compiler_params=params(),
        cost_estimate=COST,
        name="bucket",
    )(heads, *touched, moving, panels)
    packed.update(zip(tail, outs[count:]))

    all_codes = [after(codes, *touched)]
    all_codes += [along(all_codes[0], plan, k) for k in range(1, plan.groups)]
    got = [
        along(outs[(k - 1) * plan.capacity + c], plan, k)
        for k in range(1, plan.groups)
        for c in range(plan.capacity)
    ]

    moved = plan.slots + (plan.groups - 1) * plan.capacity
    assembled = pl.pallas_call(
        functools.partial(assemble_kernel, plan),
        out_shape=[
            jax.ShapeDtypeStruct(((hi - lo) * block, width), bf16) for o, lo, hi in plan.late
        ],
        in_specs=[SMEM] * (2 * plan.groups) + [HBM, HBM] + [ANY] * len(got),
        out_specs=[VMEM] * len(plan.late),
        scratch_shapes=[
            pltpu.VMEM((plan.rows, block, parent_panels.shape[2]), jnp.float32),
            pltpu.VMEM((plan.rows, block, parent_panels.shape[2]), bf16),
            pltpu.VMEM((moved, block, updates.shape[2]), bf16),
            pltpu.SMEM((GRID_COLS, plan.rows), jnp.int32),
            pltpu.SemaphoreType.DMA((plan.rows,)),
            pltpu.SemaphoreType.DMA((moved,)),
        ],
        compiler_params=params(),
        cost_estimate=COST,
        name="assemble",
    )(*all_heads, *all_codes, panels, moving, *got)

    ready = dict(zip(plan.late, assembled))

    def late(o, part=0):
        return [m for m in plan.late if m[0] == o][part]

    arrived = {late(0): ready[late(0)]}

    def send(message, *others):
        arrived[message] = across(after(ready[message], *others), plan, message[0])
        return arrived[message]

    first = {}

    def send_early(o, *others):
        if o in packed:
            first[o] = across(after(packed[o], *others), plan, o)

    def came(*offsets):
        return [first[o] for o in offsets if o in first]

    send_early(6)
    send_early(5)
    send_early(7, *came(6), *all_codes[1:])
    b5 = send(late(5), *came(5))
    b7 = send(late(7), *came(7))
    send(late(6), b5)
    send(late(4), b7)
    n2 = send(late(2), *came(5))
    send(late(3), *came(7))
    send(late(1, 0), n2)
    send(late(1, 1), b7)

    out_shape = jax.ShapeDtypeStruct((plan.rows, GRID_COLS, block, width), bf16)
    held, sets = [], []
    if early:
        out, sets = pl.pallas_call(
            functools.partial(place_early_kernel, plan, early),
            out_shape=[out_shape, jax.ShapeDtypeStruct((len(early),), jnp.int32)],
            in_specs=[ANY] * len(early),
            out_specs=[HBM, SMEM],
            scratch_shapes=[
                pltpu.VMEM((len(early), TAG, width), bf16),
                pltpu.SMEM((len(early), plan.rows), jnp.int32),
                pltpu.SemaphoreType.DMA((len(early),)),
                pltpu.SemaphoreType.DMA((len(early), plan.first)),
            ],
            compiler_params=params(),
            cost_estimate=COST,
            name="place_early",
        )(*[first[o] for o in early])
        held, sets = [out], [sets]

    def place(held, messages, name):
        known = sets if any(m[0] in early for m in messages) else []

        def body(*refs):
            refs = list(refs)[len(held) :]
            sets_ref = refs.pop(0) if known else None
            count = len(messages)
            place_late_kernel(plan, messages, early, sets_ref, refs[:count], *refs[count:])

        return [
            pl.pallas_call(
                body,
                out_shape=out_shape,
                in_specs=[HBM] * len(held) + [ANY] * (len(known) + len(messages)),
                out_specs=HBM,
                input_output_aliases={0: 0} if held else {},
                scratch_shapes=[
                    pltpu.SMEM((max(1, len(early)),), jnp.int32),
                    pltpu.SMEM((len(messages), plan.rows), jnp.int32),
                    pltpu.SemaphoreType.DMA,
                    pltpu.SemaphoreType.DMA((len(messages), plan.rows)),
                ],
                compiler_params=params(),
                cost_estimate=MID if name == "place_mid" else COST,
                name=name,
            )(*held, *known, *[arrived[m].reshape(-1, block, width) for m in messages])
        ]

    last = [late(4)]
    held = place(held, [m for m in plan.late if m not in last], "place_mid")
    held = place(held, last, "place_last")
    return held[0].reshape(1, plan.rows * GRID_COLS * block, width)


def solution(mesh):
    return jax.shard_map(
        local,
        mesh=mesh,
        in_specs=(
            P("front", "wide", None),
            P("front", "wide", None),
            P("front", "wide", None),
            P("front", "wide"),
            P("front", "wide", None),
            P("front", "wide", None),
        ),
        out_specs=P("front", "wide", None),
        check_vma=False,
    )
```

```python
import functools

import jax
import jax.numpy as jnp
from jax import lax
from jax.experimental import pallas as pl
from jax.experimental.pallas import tpu as pltpu
from jax.sharding import PartitionSpec as P

GRID_COLS = 8
NEAR = GRID_COLS // 2
TAG = 8

ANY = pl.BlockSpec(memory_space=pl.ANY)
HBM = pl.BlockSpec(memory_space=pltpu.HBM)
SMEM = pl.BlockSpec(memory_space=pltpu.SMEM)
VMEM = pl.BlockSpec(memory_space=pltpu.VMEM)


class Plan:
    def __init__(self, updates, panels, slot_cols):
        self.groups = lax.axis_size("front")
        self.lanes = lax.axis_size("wide")
        self.grid_rows = self.lanes // GRID_COLS
        self.slots = slot_cols.shape[1]
        self.columns = slot_cols.shape[2]
        self.block = updates.shape[1] // self.slots
        self.rows = panels.shape[1] // self.block
        self.window = panels.shape[2] // self.block
        self.col_groups = self.window // GRID_COLS
        self.width = self.col_groups * self.block
        self.capacity = max(self.slots // 4, self.slots // self.groups)
        self.first = max(0, self.rows - self.capacity * self.groups)
        self.early = {6: 3 * self.first // 4, 5: self.first, 7: self.first}
        self.late = []
        for o in range(GRID_COLS):
            count = self.rows - self.early.get(o, 0)
            cuts = [0, max(1, 5 * count // 8), count] if o == 1 else [0, count]
            self.late += [(o, lo, hi) for lo, hi in zip(cuts, cuts[1:]) if lo < hi]


MID = pl.CostEstimate(flops=0, transcendentals=0, bytes_accessed=0)
COST = pl.CostEstimate(flops=0, transcendentals=0, bytes_accessed=0)


def params():
    return pltpu.CompilerParams(vmem_limit_bytes=48 << 20)


def at(start, size):
    return pl.ds(pl.multiple_of(start * size, size), size)


def own_row(plan, heads, q, front):
    row = heads[q] - front * plan.rows
    return jnp.logical_and(row >= 0, row < plan.rows), row


def touched_rows(plan, head_refs):
    me = lax.axis_index("front")
    touched = jnp.int32(0)
    for heads in head_refs:
        for q in range(plan.slots):
            named, row = own_row(plan, heads, q, me)
            bit = jnp.left_shift(jnp.int32(1), jnp.where(named, row, 0))
            touched = touched | jnp.where(named, bit, 0)
    return touched


def first_rows(plan, touched, limits, order=None):
    chosen, count = [jnp.int32(0) for _ in limits], jnp.int32(0)
    for t in range(plan.rows):
        free = 1 - (jnp.right_shift(touched, t) & 1)
        chosen = [c | jnp.where(count < n, free << t, 0) for c, n in zip(chosen, limits)]
        if order is not None:
            order[count] = t
        count = count + free
    return chosen


def positions(plan, chosen):
    out, count = [], jnp.int32(0)
    for t in range(plan.rows):
        bit = jnp.right_shift(chosen, t) & 1
        out.append((bit, jnp.where(bit == 1, count, t - count)))
        count = count + bit
    return out


def list_rows(plan, chosen, bit_wanted, where):
    for t, (bit, place) in enumerate(positions(plan, chosen)):

        @pl.when(bit == bit_wanted)
        def _():
            where[place] = t


def run_all(copies):
    for copy in copies:
        copy.start()
    for copy in copies:
        copy.wait()


def stage_kernel(plan, lead, panel, *refs):
    staged, sems = refs[: len(lead)], refs[len(lead)]
    column = lax.axis_index("wide") // plan.grid_rows
    block = plan.block
    run_all(
        [
            pltpu.make_async_copy(
                panel.at[0, :, at(cc * GRID_COLS + jnp.bitwise_xor(column, o), block)],
                staged[i].at[:, pl.ds(cc * block, block)],
                sems.at[i, cc],
            )
            for i, o in enumerate(lead)
            for cc in range(plan.col_groups)
        ]
    )


def put_tag(plan, chosen, o, out):
    chosen = chosen.astype(jnp.float32)
    tag = jnp.full((TAG, plan.width), chosen, jnp.float32).astype(jnp.bfloat16)
    out[plan.early[o] * plan.block :, :] = tag


def pack_kernel(plan, lead, *refs):
    groups, count = plan.groups, len(lead)
    head_refs, staged, refs = refs[:groups], refs[groups : groups + count], refs[groups + count :]
    outs, (touched_out, order) = refs[:count], refs[count:]
    block = plan.block
    touched = touched_rows(plan, head_refs)
    touched_out[0] = touched
    chosen = first_rows(plan, touched, [plan.early[o] for o in lead], order)
    for i, o in enumerate(lead):
        for k in range(plan.early[o]):
            outs[i][pl.ds(k * block, block), :] = staged[i][at(order[k], block), :]
        put_tag(plan, chosen[i], o, outs[i])


def bucket_kernel(plan, tail, heads, *refs):
    touched_ref, refs = (refs[0], refs[1:]) if tail else (None, refs)
    updates, panel, refs = refs[0], refs[1], refs[2:]
    count = (plan.groups - 1) * plan.capacity
    outs, packed, refs = refs[:count], refs[count : count + len(tail)], refs[count + len(tail) :]
    order, slot_sems, sems = refs
    me = lax.axis_index("front")
    column = lax.axis_index("wide") // plan.grid_rows
    block = plan.block

    def buckets(act):
        for k in range(1, plan.groups):
            target = lax.rem(me + k, plan.groups)
            rank = jnp.int32(0)
            for q in range(plan.slots):
                named, _ = own_row(plan, heads, q, target)
                for c in range(plan.capacity):

                    @pl.when(jnp.logical_and(named, rank == c))
                    def _():
                        act(
                            pltpu.make_async_copy(
                                updates.at[0, pl.ds(q * block, block)],
                                outs[(k - 1) * plan.capacity + c],
                                slot_sems.at[q],
                            )
                        )

                rank = rank + jnp.where(named, 1, 0)

    buckets(lambda c: c.start())
    copies = []
    if tail:
        touched = touched_ref[0]
        chosen = first_rows(plan, touched, [plan.early[o] for o in tail], order)
        for i, o in enumerate(tail):
            target = jnp.bitwise_xor(column, o)
            for k in range(plan.early[o]):
                for cc in range(plan.col_groups):
                    copies.append(
                        pltpu.make_async_copy(
                            panel.at[0, at(order[k], block), at(cc * GRID_COLS + target, block)],
                            packed[i].at[pl.ds(k * block, block), pl.ds(cc * block, block)],
                            sems.at[i, k, cc],
                        )
                    )
                    copies[-1].start()
            put_tag(plan, chosen[i], o, packed[i])
    for copy in copies:
        copy.wait()
    buckets(lambda c: c.wait())


def assemble_kernel(plan, *refs):
    groups, block = plan.groups, plan.block
    head_refs, refs = refs[:groups], refs[groups:]
    code_refs, refs = refs[:groups], refs[groups:]
    panel, updates, refs = refs[0], refs[1], refs[2:]
    count = (groups - 1) * plan.capacity
    got, refs = refs[:count], refs[count:]
    outs, refs = refs[: len(plan.late)], refs[len(plan.late) :]
    total, raw, moved, place_ref, row_sems, slot_sems = refs
    me = lax.axis_index("front")
    column = lax.axis_index("wide") // plan.grid_rows

    slot_copies = [
        pltpu.make_async_copy(
            updates.at[0, pl.ds(q * block, block)], moved.at[q], slot_sems.at[q]
        )
        for q in range(plan.slots)
    ]
    for k in range(1, groups):
        for c in range(plan.capacity):
            part = (k - 1) * plan.capacity + c
            index = plan.slots + part
            slot_copies.append(
                pltpu.make_async_copy(got[part], moved.at[index], slot_sems.at[index])
            )
    row_copies = [
        pltpu.make_async_copy(panel.at[0, pl.ds(t * block, block)], raw.at[t], row_sems.at[t])
        for t in range(plan.rows)
    ]
    for copy in row_copies + slot_copies:
        copy.start()

    touched = touched_rows(plan, head_refs)
    limits = list(plan.early.values())
    for o, chosen in zip(plan.early, first_rows(plan, touched, limits)):
        for t, (bit, place) in enumerate(positions(plan, chosen)):
            place_ref[o, t] = jnp.where(bit == 1, -1, place)

    for t in range(plan.rows):
        row_copies[t].wait()
    for copy in slot_copies:
        copy.wait()

    def widen(t, carry):
        total[t] = raw[t].astype(jnp.float32)
        return carry

    lax.fori_loop(0, plan.rows, widen, 0)

    for s, (heads, codes) in enumerate(zip(head_refs, code_refs)):

        def add_slot(q, rank):
            named, t = own_row(plan, heads, q, me)
            index = q if s == 0 else plan.slots + (s - 1) * plan.capacity + rank

            @pl.when(named)
            def _():
                for j in range(plan.columns):
                    code = codes[q, j]
                    col = code % plan.window

                    @pl.when(code >= plan.window)
                    def _():
                        where = at(col, block)
                        total[t, :, where] += moved[
                            index, :, pl.ds(j * block, block)
                        ].astype(jnp.float32)

            return rank + jnp.where(named, 1, 0)

        lax.fori_loop(0, plan.slots, add_slot, jnp.int32(0))

    def pack(t, carry):
        for ref, (o, lo, hi) in zip(outs, plan.late):
            target = jnp.bitwise_xor(column, o)

            def put(row):
                for cc in range(plan.col_groups):
                    ref[at(row, block), pl.ds(cc * block, block)] = total[
                        t, :, at(cc * GRID_COLS + target, block)
                    ].astype(jnp.bfloat16)

            if hi - lo == plan.rows:
                put(t)
            else:
                place = place_ref[o, t] if plan.early.get(o) else t
                pl.when(jnp.logical_and(place >= lo, place < hi))(lambda: put(place - lo))

        return carry

    lax.fori_loop(0, plan.rows, pack, 0)


def place_early_kernel(plan, offsets, *refs):
    count = len(offsets)
    pieces, out, sets, refs = refs[:count], refs[count], refs[count + 1], refs[count + 2 :]
    tags, where, tag_sems, sems = refs
    column = lax.axis_index("wide") // plan.grid_rows
    block = plan.block
    run_all(
        [
            pltpu.make_async_copy(
                pieces[i].at[pl.ds(plan.early[o] * block, TAG)], tags.at[i], tag_sems.at[i]
            )
            for i, o in enumerate(offsets)
        ]
    )
    copies = []
    for i, o in enumerate(offsets):
        source = jnp.bitwise_xor(column, o)
        chosen = jnp.max(tags[i].astype(jnp.float32)).astype(jnp.int32)
        sets[i] = chosen
        list_rows(plan, chosen, 1, where.at[i])
        for k in range(plan.early[o]):
            copies.append(
                pltpu.make_async_copy(
                    pieces[i].at[pl.ds(k * block, block)],
                    out.at[where[i, k], source],
                    sems.at[i, k],
                )
            )
            copies[-1].start()
    for copy in copies:
        copy.wait()


def place_late_kernel(plan, messages, early, sets, pieces, out, held, where, set_sem, sems):
    column = lax.axis_index("wide") // plan.grid_rows
    block = plan.block
    copies = []

    def place(i, rows):
        o, lo, hi = messages[i]
        source = jnp.bitwise_xor(column, o)
        if rows is None:
            moves = [(pieces[i], out.at[pl.ds(lo, hi - lo), source])]
        else:
            moves = [(pieces[i].at[k - lo], out.at[rows[k], source]) for k in range(lo, hi)]
        for k, (src, dst) in enumerate(moves):
            copies.append(pltpu.make_async_copy(src, dst, sems.at[i, k]))
            copies[-1].start()

    split = [i for i, m in enumerate(messages) if m[0] in early]
    if split:
        fetch = pltpu.make_async_copy(sets, held, set_sem)
        fetch.start()
    for i in range(len(messages)):
        if i not in split:
            place(i, None)
    if split:
        fetch.wait()
    for i in split:
        list_rows(plan, held[early.index(messages[i][0])], 0, where.at[i])
        place(i, where.at[i])
    for copy in copies:
        copy.wait()


def after(value, *others):
    return lax.optimization_barrier((value, *others))[0]


def across(value, plan, offset):
    pairs = [
        (c * plan.grid_rows + r, (c ^ offset) * plan.grid_rows + r)
        for c in range(GRID_COLS)
        for r in range(plan.grid_rows)
    ]
    return lax.ppermute(value, "wide", pairs)


def along(value, plan, steps):
    return lax.ppermute(
        value, "front", [(f, (f + steps) % plan.groups) for f in range(plan.groups)]
    )


def local(updates, parent_panels, slot_parent, slot_row, slot_cols, slot_mask):
    plan = Plan(updates, parent_panels, slot_cols)
    block, width = plan.block, plan.width
    bf16 = jnp.bfloat16
    heads = slot_parent[0, :, 0] * plan.rows + slot_row[0]
    all_heads = [heads] + [along(heads, plan, k) for k in range(1, plan.groups)]
    codes = slot_mask[0] * plan.window + slot_cols[0]
    panels = pltpu.with_memory_space_constraint(parent_panels, pltpu.HBM)
    moving = pltpu.with_memory_space_constraint(updates, pltpu.HBM)


    early = [o for o in plan.early if plan.early[o]]
    lead, tail = early[:2], early[2:]
    packed, touched = {}, []

    def early_shape(o):
        return jax.ShapeDtypeStruct((plan.early[o] * block + TAG, width), bf16)

    if lead:
        staged = pl.pallas_call(
            functools.partial(stage_kernel, plan, lead),
            out_shape=[jax.ShapeDtypeStruct((plan.rows * block, width), bf16) for _ in lead],
            in_specs=[HBM],
            out_specs=[VMEM] * len(lead),
            scratch_shapes=[pltpu.SemaphoreType.DMA((len(lead), plan.col_groups))],
            compiler_params=params(),
            cost_estimate=COST,
            name="stage",
        )(panels)
        *outs, touched_set = pl.pallas_call(
            functools.partial(pack_kernel, plan, lead),
            out_shape=[early_shape(o) for o in lead] + [jax.ShapeDtypeStruct((1,), jnp.int32)],
            in_specs=[SMEM] * plan.groups + [VMEM] * len(lead),
            out_specs=[VMEM] * len(lead) + [SMEM],
            scratch_shapes=[pltpu.SMEM((plan.rows,), jnp.int32)],
            compiler_params=params(),
            cost_estimate=COST,
            name="pack_early",
        )(*all_heads, *staged)
        packed = dict(zip(lead, outs))
        touched = [touched_set]

    count = (plan.groups - 1) * plan.capacity
    outs = pl.pallas_call(
        functools.partial(bucket_kernel, plan, tail),
        out_shape=[jax.ShapeDtypeStruct((block, updates.shape[2]), bf16)] * count
        + [early_shape(o) for o in tail],
        in_specs=[SMEM] * (1 + len(touched)) + [HBM, HBM],
        out_specs=[VMEM] * (count + len(tail)),
        scratch_shapes=[
            pltpu.SMEM((plan.rows,), jnp.int32),
            pltpu.SemaphoreType.DMA((plan.slots,)),
            pltpu.SemaphoreType.DMA((max(1, len(tail)), max(1, plan.first), plan.col_groups)),
        ],
        compiler_params=params(),
        cost_estimate=COST,
        name="bucket",
    )(heads, *touched, moving, panels)
    packed.update(zip(tail, outs[count:]))

    all_codes = [after(codes, *touched)]
    all_codes += [along(all_codes[0], plan, k) for k in range(1, plan.groups)]
    got = [
        along(outs[(k - 1) * plan.capacity + c], plan, k)
        for k in range(1, plan.groups)
        for c in range(plan.capacity)
    ]

    moved = plan.slots + (plan.groups - 1) * plan.capacity
    assembled = pl.pallas_call(
        functools.partial(assemble_kernel, plan),
        out_shape=[
            jax.ShapeDtypeStruct(((hi - lo) * block, width), bf16) for o, lo, hi in plan.late
        ],
        in_specs=[SMEM] * (2 * plan.groups) + [HBM, HBM] + [ANY] * len(got),
        out_specs=[VMEM] * len(plan.late),
        scratch_shapes=[
            pltpu.VMEM((plan.rows, block, parent_panels.shape[2]), jnp.float32),
            pltpu.VMEM((plan.rows, block, parent_panels.shape[2]), bf16),
            pltpu.VMEM((moved, block, updates.shape[2]), bf16),
            pltpu.SMEM((GRID_COLS, plan.rows), jnp.int32),
            pltpu.SemaphoreType.DMA((plan.rows,)),
            pltpu.SemaphoreType.DMA((moved,)),
        ],
        compiler_params=params(),
        cost_estimate=COST,
        name="assemble",
    )(*all_heads, *all_codes, panels, moving, *got)

    ready = dict(zip(plan.late, assembled))

    def late(o, part=0):
        return [m for m in plan.late if m[0] == o][part]

    arrived = {late(0): ready[late(0)]}

    def send(message, *others):
        arrived[message] = across(after(ready[message], *others), plan, message[0])
        return arrived[message]

    first = {}

    def send_early(o, *others):
        if o in packed:
            first[o] = across(after(packed[o], *others), plan, o)

    def came(*offsets):
        return [first[o] for o in offsets if o in first]

    send_early(6)
    send_early(5)
    send_early(7, *came(6), *all_codes[1:])
    b5 = send(late(5), *came(5))
    b7 = send(late(7), *came(7))
    send(late(6), b5)
    send(late(4), b7)
    n2 = send(late(2), *came(5))
    send(late(3), *came(7))
    send(late(1, 0), n2)
    send(late(1, 1), b7)

    out_shape = jax.ShapeDtypeStruct((plan.rows, GRID_COLS, block, width), bf16)
    held, sets = [], []
    if early:
        out, sets = pl.pallas_call(
            functools.partial(place_early_kernel, plan, early),
            out_shape=[out_shape, jax.ShapeDtypeStruct((len(early),), jnp.int32)],
            in_specs=[ANY] * len(early),
            out_specs=[HBM, SMEM],
            scratch_shapes=[
                pltpu.VMEM((len(early), TAG, width), bf16),
                pltpu.SMEM((len(early), plan.rows), jnp.int32),
                pltpu.SemaphoreType.DMA((len(early),)),
                pltpu.SemaphoreType.DMA((len(early), plan.first)),
            ],
            compiler_params=params(),
            cost_estimate=COST,
            name="place_early",
        )(*[first[o] for o in early])
        held, sets = [out], [sets]

    def place(held, messages, name):
        known = sets if any(m[0] in early for m in messages) else []

        def body(*refs):
            refs = list(refs)[len(held) :]
            sets_ref = refs.pop(0) if known else None
            count = len(messages)
            place_late_kernel(plan, messages, early, sets_ref, refs[:count], *refs[count:])

        return [
            pl.pallas_call(
                body,
                out_shape=out_shape,
                in_specs=[HBM] * len(held) + [ANY] * (len(known) + len(messages)),
                out_specs=HBM,
                input_output_aliases={0: 0} if held else {},
                scratch_shapes=[
                    pltpu.SMEM((max(1, len(early)),), jnp.int32),
                    pltpu.SMEM((len(messages), plan.rows), jnp.int32),
                    pltpu.SemaphoreType.DMA,
                    pltpu.SemaphoreType.DMA((len(messages), plan.rows)),
                ],
                compiler_params=params(),
                cost_estimate=MID if name == "place_mid" else COST,
                name=name,
            )(*held, *known, *[arrived[m].reshape(-1, block, width) for m in messages])
        ]

    last = [late(4)]
    held = place(held, [m for m in plan.late if m not in last], "place_mid")
    held = place(held, last, "place_last")
    return held[0].reshape(1, plan.rows * GRID_COLS * block, width)


def solution(mesh):
    return jax.shard_map(
        local,
        mesh=mesh,
        in_specs=(
            P("front", "wide", None),
            P("front", "wide", None),
            P("front", "wide", None),
            P("front", "wide"),
            P("front", "wide", None),
            P("front", "wide", None),
        ),
        out_specs=P("front", "wide", None),
        check_vma=False,
    )
```

```python
import functools

import jax
import jax.numpy as jnp
from jax import lax
from jax.experimental import pallas as pl
from jax.experimental.pallas import tpu as pltpu
from jax.sharding import PartitionSpec as P

GRID_COLS = 8
NEAR = GRID_COLS // 2
TAG = 8

ANY = pl.BlockSpec(memory_space=pl.ANY)
HBM = pl.BlockSpec(memory_space=pltpu.HBM)
SMEM = pl.BlockSpec(memory_space=pltpu.SMEM)
VMEM = pl.BlockSpec(memory_space=pltpu.VMEM)


class Plan:
    def __init__(self, updates, panels, slot_cols):
        self.groups = lax.axis_size("front")
        self.lanes = lax.axis_size("wide")
        self.grid_rows = self.lanes // GRID_COLS
        self.slots = slot_cols.shape[1]
        self.columns = slot_cols.shape[2]
        self.block = updates.shape[1] // self.slots
        self.rows = panels.shape[1] // self.block
        self.window = panels.shape[2] // self.block
        self.col_groups = self.window // GRID_COLS
        self.width = self.col_groups * self.block
        self.capacity = max(self.slots // 4, self.slots // self.groups)
        self.first = max(0, self.rows - self.capacity * self.groups)
        self.early = {4: self.first // 2, 5: self.first, 7: self.first}
        self.late = []
        for o in range(GRID_COLS):
            count = self.rows - self.early.get(o, 0)
            cuts = [0, count // 2, count] if o == 3 else [0, count]
            self.late += [(o, lo, hi) for lo, hi in zip(cuts, cuts[1:]) if lo < hi]


MID = pl.CostEstimate(flops=0, transcendentals=0, bytes_accessed=0)
COST = pl.CostEstimate(flops=0, transcendentals=0, bytes_accessed=0)


def params():
    return pltpu.CompilerParams(vmem_limit_bytes=48 << 20)


def at(start, size):
    return pl.ds(pl.multiple_of(start * size, size), size)


def own_row(plan, heads, q, front):
    row = heads[q] - front * plan.rows
    return jnp.logical_and(row >= 0, row < plan.rows), row


def touched_rows(plan, head_refs):
    me = lax.axis_index("front")
    touched = jnp.int32(0)
    for heads in head_refs:
        for q in range(plan.slots):
            named, row = own_row(plan, heads, q, me)
            bit = jnp.left_shift(jnp.int32(1), jnp.where(named, row, 0))
            touched = touched | jnp.where(named, bit, 0)
    return touched


def first_rows(plan, touched, limits, order=None):
    chosen, count = [jnp.int32(0) for _ in limits], jnp.int32(0)
    for t in range(plan.rows):
        free = 1 - (jnp.right_shift(touched, t) & 1)
        chosen = [c | jnp.where(count < n, free << t, 0) for c, n in zip(chosen, limits)]
        if order is not None:
            order[count] = t
        count = count + free
    return chosen


def positions(plan, chosen):
    out, count = [], jnp.int32(0)
    for t in range(plan.rows):
        bit = jnp.right_shift(chosen, t) & 1
        out.append((bit, jnp.where(bit == 1, count, t - count)))
        count = count + bit
    return out


def list_rows(plan, chosen, bit_wanted, where):
    for t, (bit, place) in enumerate(positions(plan, chosen)):

        @pl.when(bit == bit_wanted)
        def _():
            where[place] = t


def run_all(copies):
    for copy in copies:
        copy.start()
    for copy in copies:
        copy.wait()


def stage_kernel(plan, lead, panel, *refs):
    staged, sems = refs[: len(lead)], refs[len(lead)]
    column = lax.axis_index("wide") // plan.grid_rows
    block = plan.block
    run_all(
        [
            pltpu.make_async_copy(
                panel.at[0, :, at(cc * GRID_COLS + jnp.bitwise_xor(column, o), block)],
                staged[i].at[:, pl.ds(cc * block, block)],
                sems.at[i, cc],
            )
            for i, o in enumerate(lead)
            for cc in range(plan.col_groups)
        ]
    )


def put_tag(plan, chosen, o, out):
    chosen = chosen.astype(jnp.float32)
    tag = jnp.full((TAG, plan.width), chosen, jnp.float32).astype(jnp.bfloat16)
    out[plan.early[o] * plan.block :, :] = tag


def pack_kernel(plan, lead, *refs):
    groups, count = plan.groups, len(lead)
    head_refs, staged, refs = refs[:groups], refs[groups : groups + count], refs[groups + count :]
    outs, (touched_out, order) = refs[:count], refs[count:]
    block = plan.block
    touched = touched_rows(plan, head_refs)
    touched_out[0] = touched
    chosen = first_rows(plan, touched, [plan.early[o] for o in lead], order)
    for i, o in enumerate(lead):
        for k in range(plan.early[o]):
            outs[i][pl.ds(k * block, block), :] = staged[i][at(order[k], block), :]
        put_tag(plan, chosen[i], o, outs[i])


def bucket_kernel(plan, tail, heads, *refs):
    touched_ref, refs = (refs[0], refs[1:]) if tail else (None, refs)
    updates, panel, refs = refs[0], refs[1], refs[2:]
    count = (plan.groups - 1) * plan.capacity
    outs, packed, refs = refs[:count], refs[count : count + len(tail)], refs[count + len(tail) :]
    order, slot_sems, sems = refs
    me = lax.axis_index("front")
    column = lax.axis_index("wide") // plan.grid_rows
    block = plan.block

    def buckets(act):
        for k in range(1, plan.groups):
            target = lax.rem(me + k, plan.groups)
            rank = jnp.int32(0)
            for q in range(plan.slots):
                named, _ = own_row(plan, heads, q, target)
                for c in range(plan.capacity):

                    @pl.when(jnp.logical_and(named, rank == c))
                    def _():
                        act(
                            pltpu.make_async_copy(
                                updates.at[0, pl.ds(q * block, block)],
                                outs[(k - 1) * plan.capacity + c],
                                slot_sems.at[q],
                            )
                        )

                rank = rank + jnp.where(named, 1, 0)

    buckets(lambda c: c.start())
    copies = []
    if tail:
        touched = touched_ref[0]
        chosen = first_rows(plan, touched, [plan.early[o] for o in tail], order)
        for i, o in enumerate(tail):
            target = jnp.bitwise_xor(column, o)
            for k in range(plan.early[o]):
                for cc in range(plan.col_groups):
                    copies.append(
                        pltpu.make_async_copy(
                            panel.at[0, at(order[k], block), at(cc * GRID_COLS + target, block)],
                            packed[i].at[pl.ds(k * block, block), pl.ds(cc * block, block)],
                            sems.at[i, k, cc],
                        )
                    )
                    copies[-1].start()
            put_tag(plan, chosen[i], o, packed[i])
    for copy in copies:
        copy.wait()
    buckets(lambda c: c.wait())


def assemble_kernel(plan, *refs):
    groups, block = plan.groups, plan.block
    head_refs, refs = refs[:groups], refs[groups:]
    code_refs, refs = refs[:groups], refs[groups:]
    panel, updates, refs = refs[0], refs[1], refs[2:]
    count = (groups - 1) * plan.capacity
    got, refs = refs[:count], refs[count:]
    outs, refs = refs[: len(plan.late)], refs[len(plan.late) :]
    total, raw, moved, place_ref, row_sems, slot_sems = refs
    me = lax.axis_index("front")
    column = lax.axis_index("wide") // plan.grid_rows

    slot_copies = [
        pltpu.make_async_copy(
            updates.at[0, pl.ds(q * block, block)], moved.at[q], slot_sems.at[q]
        )
        for q in range(plan.slots)
    ]
    for k in range(1, groups):
        for c in range(plan.capacity):
            part = (k - 1) * plan.capacity + c
            index = plan.slots + part
            slot_copies.append(
                pltpu.make_async_copy(got[part], moved.at[index], slot_sems.at[index])
            )
    row_copies = [
        pltpu.make_async_copy(panel.at[0, pl.ds(t * block, block)], raw.at[t], row_sems.at[t])
        for t in range(plan.rows)
    ]
    for copy in row_copies + slot_copies:
        copy.start()

    touched = touched_rows(plan, head_refs)
    limits = list(plan.early.values())
    for o, chosen in zip(plan.early, first_rows(plan, touched, limits)):
        for t, (bit, place) in enumerate(positions(plan, chosen)):
            place_ref[o, t] = jnp.where(bit == 1, -1, place)

    for t in range(plan.rows):
        row_copies[t].wait()
    for copy in slot_copies:
        copy.wait()

    def widen(t, carry):
        total[t] = raw[t].astype(jnp.float32)
        return carry

    lax.fori_loop(0, plan.rows, widen, 0)

    for s, (heads, codes) in enumerate(zip(head_refs, code_refs)):

        def add_slot(q, rank):
            named, t = own_row(plan, heads, q, me)
            index = q if s == 0 else plan.slots + (s - 1) * plan.capacity + rank

            @pl.when(named)
            def _():
                for j in range(plan.columns):
                    code = codes[q, j]
                    col = code % plan.window

                    @pl.when(code >= plan.window)
                    def _():
                        where = at(col, block)
                        total[t, :, where] += moved[
                            index, :, pl.ds(j * block, block)
                        ].astype(jnp.float32)

            return rank + jnp.where(named, 1, 0)

        lax.fori_loop(0, plan.slots, add_slot, jnp.int32(0))

    def pack(t, carry):
        for ref, (o, lo, hi) in zip(outs, plan.late):
            target = jnp.bitwise_xor(column, o)

            def put(row):
                for cc in range(plan.col_groups):
                    ref[at(row, block), pl.ds(cc * block, block)] = total[
                        t, :, at(cc * GRID_COLS + target, block)
                    ].astype(jnp.bfloat16)

            if hi - lo == plan.rows:
                put(t)
            else:
                place = place_ref[o, t] if plan.early.get(o) else t
                pl.when(jnp.logical_and(place >= lo, place < hi))(lambda: put(place - lo))

        return carry

    lax.fori_loop(0, plan.rows, pack, 0)


def place_early_kernel(plan, offsets, *refs):
    count = len(offsets)
    pieces, out, sets, refs = refs[:count], refs[count], refs[count + 1], refs[count + 2 :]
    tags, where, tag_sems, sems = refs
    column = lax.axis_index("wide") // plan.grid_rows
    block = plan.block
    run_all(
        [
            pltpu.make_async_copy(
                pieces[i].at[pl.ds(plan.early[o] * block, TAG)], tags.at[i], tag_sems.at[i]
            )
            for i, o in enumerate(offsets)
        ]
    )
    copies = []
    for i, o in enumerate(offsets):
        source = jnp.bitwise_xor(column, o)
        chosen = jnp.max(tags[i].astype(jnp.float32)).astype(jnp.int32)
        sets[i] = chosen
        list_rows(plan, chosen, 1, where.at[i])
        for k in range(plan.early[o]):
            copies.append(
                pltpu.make_async_copy(
                    pieces[i].at[pl.ds(k * block, block)],
                    out.at[where[i, k], source],
                    sems.at[i, k],
                )
            )
            copies[-1].start()
    for copy in copies:
        copy.wait()


def place_late_kernel(plan, messages, early, sets, pieces, out, held, where, set_sem, sems):
    column = lax.axis_index("wide") // plan.grid_rows
    block = plan.block
    copies = []

    def place(i, rows):
        o, lo, hi = messages[i]
        source = jnp.bitwise_xor(column, o)
        if rows is None:
            moves = [(pieces[i], out.at[pl.ds(lo, hi - lo), source])]
        else:
            moves = [(pieces[i].at[k - lo], out.at[rows[k], source]) for k in range(lo, hi)]
        for k, (src, dst) in enumerate(moves):
            copies.append(pltpu.make_async_copy(src, dst, sems.at[i, k]))
            copies[-1].start()

    split = [i for i, m in enumerate(messages) if m[0] in early]
    if split:
        fetch = pltpu.make_async_copy(sets, held, set_sem)
        fetch.start()
    for i in range(len(messages)):
        if i not in split:
            place(i, None)
    if split:
        fetch.wait()
    for i in split:
        list_rows(plan, held[early.index(messages[i][0])], 0, where.at[i])
        place(i, where.at[i])
    for copy in copies:
        copy.wait()


def after(value, *others):
    return lax.optimization_barrier((value, *others))[0]


def across(value, plan, offset):
    pairs = [
        (c * plan.grid_rows + r, (c ^ offset) * plan.grid_rows + r)
        for c in range(GRID_COLS)
        for r in range(plan.grid_rows)
    ]
    return lax.ppermute(value, "wide", pairs)


def along(value, plan, steps):
    return lax.ppermute(
        value, "front", [(f, (f + steps) % plan.groups) for f in range(plan.groups)]
    )


def local(updates, parent_panels, slot_parent, slot_row, slot_cols, slot_mask):
    plan = Plan(updates, parent_panels, slot_cols)
    block, width = plan.block, plan.width
    bf16 = jnp.bfloat16
    heads = slot_parent[0, :, 0] * plan.rows + slot_row[0]
    all_heads = [heads] + [along(heads, plan, k) for k in range(1, plan.groups)]
    codes = slot_mask[0] * plan.window + slot_cols[0]
    panels = pltpu.with_memory_space_constraint(parent_panels, pltpu.HBM)
    moving = pltpu.with_memory_space_constraint(updates, pltpu.HBM)


    early = [o for o in plan.early if plan.early[o]]
    lead, tail = early[:2], early[2:]
    packed, touched = {}, []

    def early_shape(o):
        return jax.ShapeDtypeStruct((plan.early[o] * block + TAG, width), bf16)

    if lead:
        staged = pl.pallas_call(
            functools.partial(stage_kernel, plan, lead),
            out_shape=[jax.ShapeDtypeStruct((plan.rows * block, width), bf16) for _ in lead],
            in_specs=[HBM],
            out_specs=[VMEM] * len(lead),
            scratch_shapes=[pltpu.SemaphoreType.DMA((len(lead), plan.col_groups))],
            compiler_params=params(),
            cost_estimate=COST,
            name="stage",
        )(panels)
        *outs, touched_set = pl.pallas_call(
            functools.partial(pack_kernel, plan, lead),
            out_shape=[early_shape(o) for o in lead] + [jax.ShapeDtypeStruct((1,), jnp.int32)],
            in_specs=[SMEM] * plan.groups + [VMEM] * len(lead),
            out_specs=[VMEM] * len(lead) + [SMEM],
            scratch_shapes=[pltpu.SMEM((plan.rows,), jnp.int32)],
            compiler_params=params(),
            cost_estimate=COST,
            name="pack_early",
        )(*all_heads, *staged)
        packed = dict(zip(lead, outs))
        touched = [touched_set]

    count = (plan.groups - 1) * plan.capacity
    outs = pl.pallas_call(
        functools.partial(bucket_kernel, plan, tail),
        out_shape=[jax.ShapeDtypeStruct((block, updates.shape[2]), bf16)] * count
        + [early_shape(o) for o in tail],
        in_specs=[SMEM] * (1 + len(touched)) + [HBM, HBM],
        out_specs=[VMEM] * (count + len(tail)),
        scratch_shapes=[
            pltpu.SMEM((plan.rows,), jnp.int32),
            pltpu.SemaphoreType.DMA((plan.slots,)),
            pltpu.SemaphoreType.DMA((max(1, len(tail)), max(1, plan.first), plan.col_groups)),
        ],
        compiler_params=params(),
        cost_estimate=COST,
        name="bucket",
    )(heads, *touched, moving, panels)
    packed.update(zip(tail, outs[count:]))

    all_codes = [after(codes, *touched)]
    all_codes += [along(all_codes[0], plan, k) for k in range(1, plan.groups)]
    got = [
        along(outs[(k - 1) * plan.capacity + c], plan, k)
        for k in range(1, plan.groups)
        for c in range(plan.capacity)
    ]

    moved = plan.slots + (plan.groups - 1) * plan.capacity
    assembled = pl.pallas_call(
        functools.partial(assemble_kernel, plan),
        out_shape=[
            jax.ShapeDtypeStruct(((hi - lo) * block, width), bf16) for o, lo, hi in plan.late
        ],
        in_specs=[SMEM] * (2 * plan.groups) + [HBM, HBM] + [ANY] * len(got),
        out_specs=[VMEM] * len(plan.late),
        scratch_shapes=[
            pltpu.VMEM((plan.rows, block, parent_panels.shape[2]), jnp.float32),
            pltpu.VMEM((plan.rows, block, parent_panels.shape[2]), bf16),
            pltpu.VMEM((moved, block, updates.shape[2]), bf16),
            pltpu.SMEM((GRID_COLS, plan.rows), jnp.int32),
            pltpu.SemaphoreType.DMA((plan.rows,)),
            pltpu.SemaphoreType.DMA((moved,)),
        ],
        compiler_params=params(),
        cost_estimate=COST,
        name="assemble",
    )(*all_heads, *all_codes, panels, moving, *got)

    ready = dict(zip(plan.late, assembled))

    def late(o, part=0):
        return [m for m in plan.late if m[0] == o][part]

    arrived = {late(0): ready[late(0)]}

    def send(message, *others):
        arrived[message] = across(after(ready[message], *others), plan, message[0])
        return arrived[message]

    first = {}

    def send_early(o, *others):
        if o in packed:
            first[o] = across(after(packed[o], *others), plan, o)

    def came(*offsets):
        return [first[o] for o in offsets if o in first]

    send_early(4)
    send_early(5)
    send_early(7, *came(4), *all_codes[1:])
    b5 = send(late(5), *came(5))
    b7 = send(late(7), *came(7))
    send(late(6), b5)
    send(late(4), b7)
    n1 = send(late(1), *came(5))
    send(late(2), *came(7))
    send(late(3, 0), n1)
    send(late(3, 1), b7)

    out_shape = jax.ShapeDtypeStruct((plan.rows, GRID_COLS, block, width), bf16)
    held, sets = [], []
    if early:
        out, sets = pl.pallas_call(
            functools.partial(place_early_kernel, plan, early),
            out_shape=[out_shape, jax.ShapeDtypeStruct((len(early),), jnp.int32)],
            in_specs=[ANY] * len(early),
            out_specs=[HBM, SMEM],
            scratch_shapes=[
                pltpu.VMEM((len(early), TAG, width), bf16),
                pltpu.SMEM((len(early), plan.rows), jnp.int32),
                pltpu.SemaphoreType.DMA((len(early),)),
                pltpu.SemaphoreType.DMA((len(early), plan.first)),
            ],
            compiler_params=params(),
            cost_estimate=COST,
            name="place_early",
        )(*[first[o] for o in early])
        held, sets = [out], [sets]

    def place(held, messages, name):
        known = sets if any(m[0] in early for m in messages) else []

        def body(*refs):
            refs = list(refs)[len(held) :]
            sets_ref = refs.pop(0) if known else None
            count = len(messages)
            place_late_kernel(plan, messages, early, sets_ref, refs[:count], *refs[count:])

        return [
            pl.pallas_call(
                body,
                out_shape=out_shape,
                in_specs=[HBM] * len(held) + [ANY] * (len(known) + len(messages)),
                out_specs=HBM,
                input_output_aliases={0: 0} if held else {},
                scratch_shapes=[
                    pltpu.SMEM((max(1, len(early)),), jnp.int32),
                    pltpu.SMEM((len(messages), plan.rows), jnp.int32),
                    pltpu.SemaphoreType.DMA,
                    pltpu.SemaphoreType.DMA((len(messages), plan.rows)),
                ],
                compiler_params=params(),
                cost_estimate=MID if name == "place_mid" else COST,
                name=name,
            )(*held, *known, *[arrived[m].reshape(-1, block, width) for m in messages])
        ]

    last = [late(4), late(6)]
    held = place(held, [m for m in plan.late if m not in last], "place_mid")
    held = place(held, last, "place_last")
    return held[0].reshape(1, plan.rows * GRID_COLS * block, width)


def solution(mesh):
    return jax.shard_map(
        local,
        mesh=mesh,
        in_specs=(
            P("front", "wide", None),
            P("front", "wide", None),
            P("front", "wide", None),
            P("front", "wide"),
            P("front", "wide", None),
            P("front", "wide", None),
        ),
        out_specs=P("front", "wide", None),
        check_vma=False,
    )
```
